32 devices in a mesh: groups: 2 (over y), wide: 4 (over x, core), narrow: 4 (over z).
Axes of the slice: x: 2, y: 2, z: 4, core: 2. Of those that a mesh axis runs over, the one named last changes fastest.
Arguments:
- spectra: bfloat16 [2, 32, 640, 2, 1281], P(None, ('groups', 'wide'), 'narrow'), parts along dimension 1, may hold values from -6 to 6
- legendre: bfloat16 [320, 1281, 128], P('narrow'), may hold values from -0.15625 to 0.15625
- pair_of_slot: int32 [640], replicated, may hold values from 0 to 639, each once
- lat_owner: int32 [128], replicated, may hold values from 0 to 3, as said below
- region_of_lon: int32 [2048], replicated, may hold values from 0 to 63, never falling along the last dimension, each value on 1 to 48 neighbouring positions
Outputs:
- peak: float32 [4, 128, 64], P('groups', 'narrow', 'wide'), parts along dimension 0
- peak_slope: float32 [4, 128, 64], P('groups', 'narrow', 'wide'), parts along dimension 0
The draws below stay inside these ranges and needn't reach their ends.
There are 2 independent parts, one for each index of `groups`. The reference program is written for one: setup_inputs(seed, part) draws one part's arguments, and reference() takes and returns one part's arrays. A program takes and returns all parts, laid end to end along the dimension named above; an argument that names none is the same for every part. Nothing has to cross between parts.
Inputs may be any that keep to these rules, and one draw needn't show every extreme that they name: `lat_owner`: each index of narrow owns exactly 32 latitudes. `region_of_lon`: regions never fall along the longitudes and every region has at least one longitude. `pair_of_slot`: a permutation.
All inputs are finite; a program needn't handle non-finite values.
Results may differ from the reference program's by a relative error of at most 0.0003.
Values sent between devices are 32-bit elements; how exact they have to be, the bound alone decides.
A program may use at most 192 MiB of HBM per device.

```python
import math
import jax
import jax.numpy as jnp
import numpy as np
from jax import lax

M = 1280
LAT = 128
LON = 2048
MEMBERS = 2
PAIRS = 640
PAIR_LEN = 1281
LATH = 64
LAT_DEV = 32
LON_FULL = 5120
TIMES = 16
REGIONS = 64


def draw_lat_owner(key, part):
    shuffled = jax.random.permutation(key, LAT)
    return (shuffled // LAT_DEV).astype(jnp.int32)


def shard_levels(rng, dims, split, least, largest):
    factor_of = 1.0
    for axis_at, parts in split:
        steps = jax.random.uniform(jax.random.fold_in(jax.random.fold_in(rng, 6), axis_at), (parts,), jnp.float32, least / len(split), largest / len(split))
        factor_of = factor_of * jnp.repeat(jnp.exp(steps), dims[axis_at] // parts).reshape((-1,) + (1,) * (len(dims) - 1 - axis_at))
    return factor_of


def split_up(number_of, total, bound, skew):
    loads = [(1 << 20) // math.isqrt(rank ** skew) + 1 for rank in range(2, number_of + 1)]
    surplus, given = total - bound - (number_of - 1), [1] * (number_of - 1)
    while surplus > 0:
        movable = [i for i in range(number_of - 1) if given[i] < bound]
        whole, budget = sum([loads[i] for i in movable]), surplus
        for i in movable:
            extra = min(bound - given[i], max(1, budget * loads[i] // whole), surplus)
            given[i] = given[i] + extra
            surplus = surplus - extra
    return np.array([bound] + given)


def ragged(own_key, number_of, total, most, skew):
    if number_of == 2:
        one = jax.random.randint(own_key, (), max(1, total - most), min(most, total - 1) + 1)
        return jnp.stack([one, total - one])
    tallies = jnp.asarray(split_up(number_of, total, most, skew), jnp.int32)
    twos = (number_of - 1) // 2
    source_of, taker = tallies[1:1 + 2 * twos:2], tallies[2:2 + 2 * twos:2]
    room = jnp.minimum(source_of - 1, most - taker)
    shifted = jax.random.randint(jax.random.fold_in(own_key, 1), (twos,), 0, 1 << 20) % (room + 1)
    tallies = tallies.at[1:1 + 2 * twos:2].set(source_of - shifted).at[2:2 + 2 * twos:2].set(taker + shifted)
    return tallies[jax.random.permutation(jax.random.fold_in(own_key, 2), number_of)]


def scatter_about(key, extent, spread, bound, cuts=(), held_as=jnp.bfloat16):
    drawn = spread * jax.random.normal(key, extent, jnp.float32)
    if cuts:
        drawn = drawn * shard_levels(key, extent, cuts, -0.22, 0.18)
    return jnp.clip(drawn, -bound, bound).astype(held_as)


def setup_inputs(seed: int = 0, part: int = 0) -> dict:
    streams_of = jax.random.split(jax.random.key(seed), 6)
    part_keys = jax.random.split(jax.random.fold_in(streams_of[5], part), 6)
    return {
        "spectra": scatter_about(part_keys[0], (MEMBERS, TIMES, PAIRS, 2, PAIR_LEN), 1.0, 6.0, ((1, 4), (2, 4))),
        "legendre": scatter_about(streams_of[1], (PAIRS // 2, PAIR_LEN, 2 * LATH), M ** -0.5, 0.15625, ((0, 4),)),
        "pair_of_slot": jax.random.permutation(streams_of[2], PAIRS).astype(jnp.int32),
        "lat_owner": draw_lat_owner(jax.random.fold_in(streams_of[5], 71), part),
        "region_of_lon": jnp.searchsorted(jnp.cumsum(ragged(streams_of[4], REGIONS, LON, 48, 0)), jnp.arange(LON), side="right").astype(jnp.int32),
    }


def legendre_slot(coef, table, paired):
    position = jnp.arange(PAIR_LEN, dtype=jnp.int32)
    first_len = M - paired
    leading = position < first_len
    offset = jnp.where(leading, position, position - first_len)
    even_term = offset % 2 == 0
    masks = jnp.stack([leading & even_term, leading & ~even_term, ~leading & even_term, ~leading & ~even_term], axis=0).astype(jnp.float32)
    masked = masks[:, None, None, None, :] * coef.astype(jnp.float32)[None]
    sums = jnp.einsum("getcl,lj->getcj", masked, table.astype(jnp.float32), precision=lax.Precision.HIGHEST)
    north_lead = sums[0] + sums[1]
    south_lead = sums[0] - sums[1]
    north_tail = sums[2] + sums[3]
    south_tail = sums[2] - sums[3]
    lead = jnp.concatenate([north_lead, jnp.flip(south_lead, axis=-1)], axis=-1)
    tail = jnp.concatenate([north_tail, jnp.flip(south_tail, axis=-1)], axis=-1)
    return jnp.stack([lead, tail], axis=0)


def synthesize(operand, waves, start, width):
    columns = start + jnp.arange(width, dtype=jnp.int32)
    phase = (waves[:, None] * columns[None, :]) % LON_FULL
    angle = phase.astype(jnp.float32) * (2.0 * math.pi / LON_FULL)
    cosine = jnp.cos(angle)
    sine = jnp.sin(angle)
    rate = (waves.astype(jnp.float32) / M)[:, None]
    upper = jnp.concatenate([cosine, -rate * sine], axis=1)
    lower = jnp.concatenate([-sine, -rate * cosine], axis=1)
    table = jnp.concatenate([upper, lower], axis=0) * (M ** -0.5)
    return jnp.dot(operand, table, precision=lax.Precision.HIGHEST)


def synthesize_all(operand, waves):
    width = min(512, LON)
    starts = jnp.arange(LON // width, dtype=jnp.int32) * width

    def one_block(begin):
        return synthesize(operand, waves, begin, width)

    blocks = lax.map(one_block, starts)
    blocks = blocks.reshape(blocks.shape[0], blocks.shape[1], 2, width)
    value = jnp.transpose(blocks[:, :, 0], (1, 0, 2)).reshape(operand.shape[0], LON)
    slope = jnp.transpose(blocks[:, :, 1], (1, 0, 2)).reshape(operand.shape[0], LON)
    return value, slope


def region_peak(values, region_of_lon, wanted):
    hits = region_of_lon[:, None] == wanted[None, :]
    masked = jnp.where(hits[None, None], values[..., None], -1e30)
    return masked.max(axis=2)


def reference(spectra, legendre, pair_of_slot, lat_owner, region_of_lon):
    table_all = legendre.reshape(PAIRS // 2, PAIR_LEN, 2, LATH)
    table_all = jnp.transpose(table_all, (0, 2, 1, 3)).reshape(PAIRS, PAIR_LEN, LATH)

    def per_slot(items):
        return legendre_slot(items[0], items[1], items[2])

    slotted = lax.map(per_slot, (jnp.moveaxis(spectra, 2, 0), table_all, pair_of_slot))
    grid = jnp.zeros((M, MEMBERS, TIMES, 2, LAT), jnp.float32)
    grid = grid.at[pair_of_slot].set(slotted[:, 0])
    grid = grid.at[M - 1 - pair_of_slot].set(slotted[:, 1])
    order = jnp.argsort(lat_owner, stable=True).astype(jnp.int32)
    grid = jnp.take(grid, order, axis=4)
    operand = jnp.transpose(grid, (1, 2, 4, 3, 0)).reshape(MEMBERS * TIMES * LAT, 2 * M)
    waves = jnp.arange(M, dtype=jnp.int32)
    value, slope = synthesize_all(operand, waves)
    value = value.reshape(MEMBERS, TIMES, LAT, LON).max(axis=1)
    slope = jnp.abs(slope).reshape(MEMBERS, TIMES, LAT, LON).max(axis=1)
    wanted = jnp.arange(REGIONS, dtype=jnp.int32)
    peak = region_peak(value, region_of_lon, wanted)
    peak_slope = region_peak(slope, region_of_lon, wanted)
    return peak, peak_slope
```

```python
import functools
import math

import jax
import jax.numpy as jnp
from jax import lax
from jax.experimental import pallas as pl
from jax.experimental.pallas import tpu as pltpu
from jax.sharding import PartitionSpec as P

M = 1280
LON = 2048
REG_DEV = 16
LON_FULL = 5120


def synthesize(operand, waves, start, width):
    columns = start + jnp.arange(width, dtype=jnp.int32)
    phase = waves[:, None] * columns[None, :] % LON_FULL
    angle = phase.astype(jnp.float32) * (2.0 * math.pi / LON_FULL)
    cosine = jnp.cos(angle)
    sine = jnp.sin(angle)
    rate = (waves.astype(jnp.float32) / M)[:, None]
    upper = jnp.concatenate([cosine, -rate * sine], axis=1)
    lower = jnp.concatenate([-sine, -rate * cosine], axis=1)
    table = jnp.concatenate([upper, lower], axis=0) * M ** (-0.5)
    return jnp.dot(operand, table, precision=lax.Precision.HIGHEST)


def synthesize_all(operand, waves):
    width = min(512, LON)
    starts = jnp.arange(LON // width, dtype=jnp.int32) * width

    def one_block(begin):
        return synthesize(operand, waves, begin, width)

    blocks = lax.map(one_block, starts)
    blocks = blocks.reshape(blocks.shape[0], blocks.shape[1], 2, width)
    value = jnp.transpose(blocks[:, :, 0], (1, 0, 2)).reshape(operand.shape[0], LON)
    slope = jnp.transpose(blocks[:, :, 1], (1, 0, 2)).reshape(operand.shape[0], LON)
    return (value, slope)


def region_peak(values, region_of_lon, wanted):
    hits = region_of_lon[:, None] == wanted[None, :]
    masked = jnp.where(hits[None, None], values[..., None], -1e30)
    return masked.max(axis=2)


def per_device_plain(spectra, legendre, pair_of_slot, lat_owner, region_of_lon):
    members = spectra.shape[0]
    steps_here = spectra.shape[1]
    slot_count = spectra.shape[2]
    length = spectra.shape[4]
    half_count = legendre.shape[0]
    lat_half = legendre.shape[2] // 2
    here = lax.axis_index("narrow")
    paired = lax.dynamic_slice_in_dim(pair_of_slot, here * slot_count, slot_count)
    position = jnp.arange(length, dtype=jnp.int32)[None, :]
    first_len = (M - paired)[:, None]
    leading = position < first_len
    offset = jnp.where(leading, position, position - first_len)
    even_term = offset % 2 == 0
    masks = jnp.stack(
        [leading & even_term, leading & ~even_term, ~leading & even_term, ~leading & ~even_term],
        axis=1,
    ).astype(jnp.bfloat16)
    ordered = jnp.transpose(spectra, (2, 0, 1, 3, 4))
    masked = masks[:, :, None, None, None, :] * ordered[:, None]
    masked = masked.reshape(half_count, 2, -1, length)
    table = legendre.reshape(half_count, length, 2, lat_half)
    sums = jnp.einsum("abrl,albj->abrj", masked, table, preferred_element_type=jnp.float32)
    sums = sums.reshape(slot_count, 4, members, steps_here, 2, lat_half)
    north_lead = sums[:, 0] + sums[:, 1]
    south_lead = sums[:, 0] - sums[:, 1]
    north_tail = sums[:, 2] + sums[:, 3]
    south_tail = sums[:, 2] - sums[:, 3]
    lead = jnp.concatenate([north_lead, jnp.flip(south_lead, axis=-1)], axis=-1)
    tail = jnp.concatenate([north_tail, jnp.flip(south_tail, axis=-1)], axis=-1)
    waved = jnp.stack([lead, tail], axis=1).reshape(2 * slot_count, members, steps_here, 2, -1)
    order = jnp.argsort(lat_owner, stable=True)
    waved = jnp.take(waved, order, axis=4)
    arrived = lax.all_to_all(waved, "narrow", split_axis=4, concat_axis=0, tiled=True)
    waves = jnp.stack([pair_of_slot, M - 1 - pair_of_slot], axis=1).reshape(-1)
    lat_here = arrived.shape[4]
    operand = jnp.transpose(arrived, (1, 2, 4, 3, 0)).reshape(members * steps_here * lat_here, -1)
    value, slope = synthesize_all(operand, waves)
    value = value.reshape(members, steps_here, lat_here, LON).max(axis=1)
    slope = jnp.abs(slope).reshape(members, steps_here, lat_here, LON).max(axis=1)
    wide_count = lax.axis_size("wide")
    mine_start = lax.axis_index("wide") * REG_DEV
    wanted = jnp.arange(REG_DEV * wide_count, dtype=jnp.int32)
    peaks = region_peak(value, region_of_lon, wanted)
    slopes = region_peak(slope, region_of_lon, wanted)
    peaks, slopes = lax.pmax((peaks, slopes), "wide")
    peak = lax.dynamic_slice_in_dim(peaks, mine_start, REG_DEV, 2)
    peak_slope = lax.dynamic_slice_in_dim(slopes, mine_start, REG_DEV, 2)
    return (peak, peak_slope)


CHUNK = 16
HALF = 8
FINE = 32
GROUP = 256
MESH = pl.DeviceIdType.MESH


def split(values):
    high = values.astype(jnp.bfloat16)
    low = (values - high.astype(jnp.float32)).astype(jnp.bfloat16)
    return high, low


def dot(left, right):
    return jnp.dot(left, right, preferred_element_type=jnp.float32)


def turn(count):
    quarter = LON_FULL // 2
    whole = jnp.floor(count * (1.0 / quarter) + 0.5)
    angle = (count - whole * quarter) * (math.pi / LON_FULL)
    square = angle * angle
    sine = angle * (1.0 + square * (-1 / 6 + square * (1 / 120 + square * (-1 / 5040 + square * (1 / 362880)))))
    cosine = 1.0 + square * (
        -1 / 2 + square * (1 / 24 + square * (-1 / 720 + square * (1 / 40320 + square * (-1 / 3628800))))
    )
    turns = whole.astype(jnp.int32)
    swap = (turns & 1) == 1
    cos_sign = jnp.where(((turns + 1) & 2) == 2, -1.0, 1.0)
    sin_sign = jnp.where((turns & 2) == 2, -1.0, 1.0)
    return cos_sign * jnp.where(swap, sine, cosine), sin_sign * jnp.where(swap, cosine, sine)


def iota(shape, dim):
    return lax.broadcasted_iota(jnp.int32, shape, dim)


def fields_kernel(
    dims, pair_ref, owner_ref, region_ref, x_hbm, table_hbm, out_ref,
    table_buf, x_buf, lined, spread, sums, place, sent, held, coef, coarse, fine, part_cos, part_sin, field,
    apart, apart_blocks, pick, pick_blocks, absent, peaks, peaks_in,
    fetch_sem, send_sem, recv_sem, wide_send, wide_recv,
):
    narrow, wide, chunks, rows, members, steps_here, lat_here, lon = dims
    me = lax.axis_index("narrow")
    me_wide = lax.axis_index("wide")
    slot_count = chunks * CHUNK
    pairs = CHUNK // 2
    half_lon = lon // 2
    lat = narrow * lat_here

    def fetches(c, slot):
        return (
            pltpu.make_async_copy(
                table_hbm.at[:, pl.ds(pl.multiple_of(c * pairs, pairs), pairs), :], table_buf.at[slot],
                fetch_sem.at[0, slot],
            ),
            pltpu.make_async_copy(
                x_hbm.at[:, :, pl.ds(c * CHUNK, CHUNK), :, :], x_buf.at[slot], fetch_sem.at[1, slot]
            ),
        )

    def start_fetch(c, slot):
        for copy in fetches(c, slot):
            copy.start()

    def partner(ahead):
        return lax.rem(me + ahead, narrow)

    order = (2, 1, 3) if narrow == 4 else tuple(range(1, narrow))

    def send(c, ahead, h):
        target = partner(ahead)
        span = pl.ds(0, 2 * CHUNK) if h is None else pl.ds(h * CHUNK, CHUNK)
        at = 0 if h is None else h
        return pltpu.make_async_remote_copy(
            src_ref=sent.at[c, target, span], dst_ref=held.at[c, me, span],
            send_sem=send_sem.at[at, c, target], recv_sem=recv_sem.at[at, c, me],
            device_id={"narrow": target}, device_id_type=MESH,
        )

    def receive(c, ahead, h):
        origin = partner(ahead)
        span = pl.ds(0, 2 * CHUNK) if h is None else pl.ds(h * CHUNK, CHUNK)
        at = 0 if h is None else h
        return pltpu.make_async_remote_copy(
            src_ref=sent.at[c, origin, span], dst_ref=held.at[c, origin, span],
            send_sem=send_sem.at[at, c, origin], recv_sem=recv_sem.at[at, c, origin],
            device_id={"narrow": origin}, device_id_type=MESH,
        )

    start_fetch(0, 0)
    barrier = pltpu.get_barrier_semaphore()
    for ahead in range(1, narrow):
        pl.semaphore_signal(barrier, inc=1, device_id={"narrow": partner(ahead)}, device_id_type=MESH)
    for ahead in range(1, wide):
        pl.semaphore_signal(
            barrier, inc=1, device_id={"wide": lax.rem(me_wide + ahead, wide)}, device_id_type=MESH
        )

    lane = iota((lat, lat), 1)
    below = iota((lat, lat), 0)
    below = jnp.where(below < lat // 2, below, 3 * lat // 2 - 1 - below)
    owners = jnp.broadcast_to(owner_ref[...], (lat, lat)).astype(jnp.float32)
    owner = jnp.sum(jnp.where(lane == below, owners, 0.0), axis=1, keepdims=True)
    ahead_of = (owners < owner) | ((owners == owner) & (lane < below))
    rank = jnp.sum(jnp.where(ahead_of, 1.0, 0.0), axis=1, keepdims=True).astype(jnp.int32)
    column = iota((lat, narrow * 128), 1)
    goal = (column // 128) * lat_here + column % lat_here
    for n in range(2 * members):
        wanted = (goal == rank) & ((column // lat_here) % (2 * members) == n)
        place[n * lat:(n + 1) * lat, :] = jnp.where(wanted, 1.0, 0.0).astype(jnp.bfloat16)

    position = iota((1, M), 1)
    half_lane = iota((rows, 128), 1)
    block = M // 8

    def one_pair(c, slot, at, u):
        parts = []
        extras = []
        for half in range(2):
            inside = 2 * at + half
            lines = 2 * u + half
            first_len = M - pair_ref[me * slot_count + c * CHUNK + inside]
            leading = (position < first_len).astype(jnp.float32)
            trailing = 1.0 - leading
            sign_lead = (1 - 2 * (position & 1)).astype(jnp.float32)
            flip = (1 - 2 * (first_len & 1)).astype(jnp.float32)
            for e in range(members):
                for t in range(steps_here):
                    row = 2 * (e * steps_here + t)
                    lined[lines, row:row + 2, :] = x_buf[slot, e, t, inside].astype(jnp.float32)
            body = lined[lines, :, :M].astype(jnp.bfloat16)
            for mask in (leading, leading * sign_lead, trailing, trailing * (sign_lead * flip)):
                parts.append(body * mask.astype(jnp.bfloat16))
            last = lined[lines, :, M:]
            extras.append((last, flip))
        table = spread[pl.ds(at, M, stride=pairs), :].astype(jnp.bfloat16)
        out = dot(jnp.concatenate(parts, axis=0), table)
        edge = spread[pl.ds(M * pairs + at, 1), :]
        for half in range(2):
            base = half * 4 * rows
            piece = [out[base + v * rows:base + (v + 1) * rows] for v in range(4)]
            last, flip = extras[half]
            term = last * edge
            piece[2] = piece[2] + term
            piece[3] = piece[3] + term * flip
            for tail_at in range(2):
                north, south = piece[2 * tail_at], piece[2 * tail_at + 1]
                if half == 0:
                    both = jnp.where(half_lane < 64, north, pltpu.roll(south, 64, 1))
                else:
                    both = jnp.where(half_lane < 64, pltpu.roll(north, 64, 1), south)
                at_row = (tail_at * HALF + 2 * u + half) * rows
                sums[at_row:at_row + rows, :] = both

    def one_half(c, slot, h):
        for u in range(HALF // 2):
            one_pair(c, slot, h * (HALF // 2) + u, u)
        highs, lows = [], []
        for t in range(steps_here):
            wide_rows = jnp.concatenate(
                [
                    sums[pl.ds((e * steps_here + t) * 2 + part, CHUNK, stride=rows), :]
                    for part in range(2) for e in range(members)
                ],
                axis=1,
            )
            high, low = split(wide_rows)
            highs.append(high)
            lows.append(low)
        both = dot(jnp.concatenate(highs + lows, axis=0), place[...])
        moved = both[:steps_here * CHUNK] + both[steps_here * CHUNK:]
        where_to = pl.ds(pl.multiple_of(h * CHUNK, CHUNK), CHUNK)
        for t in range(steps_here):
            for d in range(narrow):
                sent[c, d, where_to, t * 128:(t + 1) * 128] = (
                    moved[t * CHUNK:(t + 1) * CHUNK, d * 128:(d + 1) * 128]
                )
        held[c, me, where_to, :] = sent[c, me, where_to, :]

        @pl.when((c == 0) & (h == 0))
        def _():
            pl.semaphore_wait(barrier, narrow - 1 + wide - 1)
            for ahead in order:
                send(0, ahead, 0).start()

        @pl.when((c == 0) & (h == 1))
        def _():
            for ahead in order:
                send(0, ahead, 1).start()

        @pl.when((c == chunks - 1) & (h == 0))
        def _():
            for ahead in order:
                send(chunks - 1, ahead, 0).start()

        @pl.when((c == chunks - 1) & (h == 1))
        def _():
            for ahead in order:
                send(chunks - 1, ahead, 1).start()

        @pl.when((c > 0) & (c < chunks - 1) & (h == 1))
        def _():
            for ahead in order:
                send(c, ahead, None).start()

    def tables(c):
        lanes = iota((8, 128), 1)
        base = lanes & ~HALF
        lead = jnp.zeros((8, 128), jnp.int32)
        for h in range(2):
            for d in range(narrow):
                for s in range(HALF):
                    at = (h * narrow + d) * CHUNK + s
                    lead = jnp.where(base == at, pair_ref[d * slot_count + c * CHUNK + h * HALF + s], lead)
        wave = jnp.where((lanes & HALF) == HALF, M - 1 - lead, lead).astype(jnp.float32)
        here = pl.ds(pl.multiple_of(c * 128, 128), 128)
        rows_of = jnp.broadcast_to(wave[:1], (FINE, 128))
        index = iota((FINE, 128), 0).astype(jnp.float32)
        cosine, sine = turn(rows_of * (index * (2.0 * FINE)))
        coarse[0, :, here] = cosine
        coarse[1, :, here] = sine
        cosine, sine = turn(rows_of * (index * 2.0 + 1.0))
        fine[0, :, here] = cosine
        fine[1, :, here] = sine
        down = jnp.transpose(jnp.broadcast_to(wave[:1], (128, 128)))
        cosine, sine = turn(down * (lon - 1.0))
        low = iota((128, 128), 1) < 64
        cosine = cosine * (M ** -0.5)
        sine = sine * (M ** -0.5)
        rate = down * (1.0 / M)
        coef[0, here, :] = cosine * jnp.where(low, 1.0, -rate)
        coef[1, here, :] = sine * jnp.where(low, -1.0, -rate)
        coef[2, here, :] = sine * jnp.where(low, 1.0, -rate)
        coef[3, here, :] = cosine * jnp.where(low, 1.0, rate)

    def one_chunk(c, carry):
        slot = lax.rem(c, 2)
        for copy in fetches(c, slot):
            copy.wait()

        @pl.when(c + 1 < chunks)
        def _():
            start_fetch(c + 1, 1 - slot)

        def widen(n, carry):
            part = table_buf[slot, pl.ds(n * block, block)].astype(jnp.float32)
            where_to = pl.ds(pl.multiple_of(n * block * pairs, 8), block * pairs)
            spread[where_to, :] = part.reshape(block * pairs, 128)
            return carry

        lax.fori_loop(0, 8, widen, 0)
        spread[M * pairs:, :] = table_buf[slot, M].astype(jnp.float32)

        def halves(h, carry):
            one_half(c, slot, h)
            return carry

        lax.fori_loop(0, 2, halves, 0)
        tables(c)
        return carry

    lax.fori_loop(0, chunks, one_chunk, 0)

    def turned(pieces, here):
        evens, odds = [], []
        c1, s1, c2, s2 = (coef[n, here, :] for n in range(4))
        for t in range(steps_here):
            data = jnp.concatenate([held[c, d, span, t * 128:(t + 1) * 128] for c, d, span in pieces], axis=0)
            other = pltpu.roll(data, 64, 1)
            evens.append(data * c1 + other * s1)
            odds.append(data * c2 + other * s2)
        return split(jnp.concatenate(evens, axis=1)), split(jnp.concatenate(odds, axis=1))

    def waves_at(g, coarse_of, fine_of):
        cosines, sines = [], []
        many = GROUP // FINE
        span = pl.ds(pl.multiple_of(g * many, many), many)
        cu, su = coarse_of(0, span), coarse_of(1, span)
        c2, s2 = fine_of
        for u in range(many):
            c1, s1 = cu[u:u + 1], su[u:u + 1]
            cosines.append(c1 * c2 - s1 * s2)
            sines.append(s1 * c2 + c1 * s2)
        return split(jnp.concatenate(cosines, axis=0)), split(jnp.concatenate(sines, axis=0))

    def span_of(h):
        return pl.ds(h * CHUNK, CHUNK)

    regions = wide * REG_DEV
    blocks = half_lon // 8

    def region_tables():
        number = iota((regions, 128), 0)
        begin = jnp.zeros((regions, 128), jnp.int32)
        end = begin
        for n in range(lon // 128):
            ids = region_ref[n:n + 1, :]
            begin = begin + jnp.where(ids < number, 1, 0)
            end = end + jnp.where(ids <= number, 1, 0)
        reach = 64
        while reach:
            begin = begin + pltpu.roll(begin, reach, 1)
            end = end + pltpu.roll(end, reach, 1)
            reach //= 2
        lanes = iota((regions, 128), 1)
        for side in range(2):
            if side == 0:
                first, last = half_lon - jnp.minimum(end, half_lon), half_lon - jnp.minimum(begin, half_lon)
            else:
                first, last = jnp.maximum(begin, half_lon) - half_lon, jnp.maximum(end, half_lon) - half_lon
            here = first < last
            for n in range(half_lon // 128):
                hit = (lanes + n * 128 == first) & here
                pick[side, :, n * 128:(n + 1) * 128] = jnp.where(hit, 1.0, 0.0).astype(jnp.bfloat16)
            start = (first + 7) >> 3
            whole = start * 8 < last
            pick_blocks[side] = jnp.where((lanes == start) & whole, 1.0, 0.0).astype(jnp.bfloat16)
            absent[2 * side] = jnp.where(here, 0.0, -1e30)
            absent[2 * side + 1] = jnp.where(whole, 0.0, -1e30)
        across, down = iota((128, 128), 1), iota((128, 128), 0)
        mirror = jnp.where(across + down == 127, 1.0, 0.0).astype(jnp.bfloat16)
        ids = region_ref[...].astype(jnp.float32)
        flipped = dot(ids.astype(jnp.bfloat16), mirror)
        tiles = half_lon // 128
        sub = iota((16, 8, 128), 1)
        for side in range(2):
            for n in range(tiles):
                source = flipped[tiles - 1 - n:tiles - n] if side == 0 else ids[tiles + n:tiles + n + 1]
                column = jnp.transpose(jnp.broadcast_to(source, (128, 128)))
                span = pl.ds(side * half_lon + n * 128, 128)
                field[span, :] = column
                column = column.reshape(16, 8, 128)
                for i, step in enumerate((1, 2, 4)):
                    same = (pltpu.roll(column, 8 - step, 1) == column) & (sub + step < 8)
                    apart[i, span, :] = jnp.where(same, 0.0, -1e30).reshape(128, 128)
            starts = field[pl.ds(side * half_lon, blocks, stride=8), :]
            for i, step in enumerate((1, 2, 4)):
                same = (pltpu.roll(starts, blocks - step, 0) == starts) & (iota((blocks, 128), 0) + step < blocks)
                apart_blocks[side, i] = jnp.where(same, 0.0, -1e30)

    region_tables()

    def arrive(c, h):
        for ahead in range(1, narrow):
            receive(c, ahead, h).wait_recv()

    def two_chunks(k, carry):
        first = 2 * k

        @pl.when(k == 0)
        def _():
            arrive(0, 0)
            arrive(0, 1)

        @pl.when(k > 0)
        def _():
            arrive(first, None)

        arrive(first + 1, None)
        here = pl.ds(pl.multiple_of(first * 128, 256), 256)
        pieces = [(first + n, d, span_of(h)) for n in range(2) for h in range(2) for d in range(narrow)]
        (even_hi, even_lo), (odd_hi, odd_lo) = turned(pieces, here)
        fine_of = fine[0, :, here], fine[1, :, here]

        def one_group(g, carry):
            (cos_hi, cos_lo), (sin_hi, sin_lo) = waves_at(g, lambda n, span: coarse[n, span, here], fine_of)
            where_to = pl.ds(pl.multiple_of(g * GROUP, GROUP), GROUP)
            new_cos = dot(cos_hi, even_hi) + dot(cos_lo, even_hi) + dot(cos_hi, even_lo)
            new_sin = dot(sin_hi, odd_hi) + dot(sin_lo, odd_hi) + dot(sin_hi, odd_lo)

            @pl.when(k == 0)
            def _():
                part_cos[where_to, :] = new_cos
                part_sin[where_to, :] = new_sin

            @pl.when(k > 0)
            def _():
                part_cos[where_to, :] += new_cos
                part_sin[where_to, :] += new_sin

            return carry

        lax.fori_loop(0, half_lon // GROUP, one_group, 0)
        return carry

    lax.fori_loop(0, chunks // 2 - 1, two_chunks, 0)

    def half_chunk(c, h, last):
        here = pl.ds((c * 2 + h) * 64, 64)
        (even_hi, even_lo), (odd_hi, odd_lo) = turned([(c, d, span_of(h)) for d in range(narrow)], here)
        even = jnp.concatenate([even_hi, even_hi, even_lo, jnp.zeros_like(even_lo)], axis=0)
        odd = jnp.concatenate([odd_hi, odd_hi, odd_lo, jnp.zeros_like(odd_lo)], axis=0)
        chunk_here = pl.ds(c * 128, 128)

        def doubled(values):
            kept = iota(values.shape, 1) < 64
            moved = pltpu.roll(values, 64, 1)
            return jnp.where(kept, values, moved) if h == 0 else jnp.where(kept, moved, values)

        fine_of = tuple(doubled(fine[n, :, chunk_here]) for n in range(2))
        low = iota((GROUP, 128), 1) < 64
        slopes = iota((GROUP, 128), 1) >= 64

        def one_group(g, carry):
            (cos_hi, cos_lo), (sin_hi, sin_lo) = waves_at(
                g, lambda n, span: doubled(coarse[n, span, chunk_here]), fine_of
            )
            where_to = pl.ds(pl.multiple_of(g * GROUP, GROUP), GROUP)
            new_cos = dot(jnp.concatenate([jnp.where(low, cos_hi, cos_lo), cos_hi], axis=1), even)
            new_sin = dot(jnp.concatenate([jnp.where(low, sin_hi, sin_lo), sin_hi], axis=1), odd)
            if not last:
                part_cos[where_to, :] += new_cos
                part_sin[where_to, :] += new_sin
                return carry
            most = [None, None]
            least = [None, None]
            for t in range(steps_here):
                lanes = slice(t * 128, (t + 1) * 128)
                even_part = part_cos[where_to, lanes] + new_cos[:, lanes]
                odd_part = part_sin[where_to, lanes] + new_sin[:, lanes]
                for side, full in enumerate((even_part + odd_part, even_part - odd_part)):
                    most[side] = full if t == 0 else jnp.maximum(most[side], full)
                    least[side] = full if t == 0 else jnp.minimum(least[side], full)
            for side in range(2):
                span = pl.ds(pl.multiple_of(side * half_lon + g * GROUP, GROUP), GROUP)
                best = jnp.maximum(most[side], jnp.where(slopes, -least[side], most[side]))
                best = best.reshape(GROUP // 8, 8, 128)
                for i, step in enumerate((1, 2, 4)):
                    best = jnp.maximum(
                        best, pltpu.roll(best, 8 - step, 1) + apart[i, span, :].reshape(GROUP // 8, 8, 128)
                    )
                field[span, :] = best.reshape(GROUP, 128)
            return carry

        lax.fori_loop(0, half_lon // GROUP, one_group, 0)

    arrive(chunks - 2, None)
    half_chunk(chunks - 2, 0, False)
    half_chunk(chunks - 2, 1, False)
    arrive(chunks - 1, 0)
    half_chunk(chunks - 1, 0, False)
    arrive(chunks - 1, 1)
    half_chunk(chunks - 1, 1, True)

    def chosen(picks, values, missing):
        high, low = split(values)
        both = dot(picks, jnp.concatenate([high, low], axis=1))
        return both[:, :128] + both[:, 128:] + missing

    parts = []
    for side in range(2):
        starts = field[pl.ds(side * half_lon, blocks, stride=8), :]
        for i, step in enumerate((1, 2, 4)):
            starts = jnp.maximum(starts, pltpu.roll(starts, blocks - step, 0) + apart_blocks[side, i])
        parts.append(chosen(pick_blocks[side], starts, absent[2 * side + 1]))
        parts.append(chosen(pick[side], field[pl.ds(side * half_lon, half_lon), :], absent[2 * side]))
    peaks[...] = jnp.maximum(jnp.maximum(parts[0], parts[1]), jnp.maximum(parts[2], parts[3]))

    def exchange(ahead, arriving):
        other = lax.rem(me_wide + ahead, wide)
        return pltpu.make_async_remote_copy(
            src_ref=peaks.at[pl.ds(pl.multiple_of(other * REG_DEV, REG_DEV), REG_DEV)],
            dst_ref=peaks_in.at[other if arriving else me_wide],
            send_sem=wide_send.at[other], recv_sem=wide_recv.at[other if arriving else me_wide],
            device_id={"wide": other}, device_id_type=MESH,
        )

    for ahead in range(wide - 1, 0, -1):
        exchange(ahead, False).start()
    best = peaks[pl.ds(pl.multiple_of(me_wide * REG_DEV, REG_DEV), REG_DEV), :]
    for ahead in range(1, wide):
        exchange(ahead, True).wait_recv()
        best = jnp.maximum(best, peaks_in[lax.rem(me_wide + ahead, wide)])
    for n in range(2 * members):
        out_ref[n] = best[:, n * lat_here:(n + 1) * lat_here]

    for ahead in range(1, wide):
        exchange(ahead, False).wait_send()
    for c in (0, chunks - 1):
        for h in range(2):
            for ahead in range(1, narrow):
                send(c, ahead, h).wait_send()

    def drain(c, carry):
        for ahead in range(1, narrow):
            send(c, ahead, None).wait_send()
        return carry

    lax.fori_loop(1, chunks - 1, drain, 0)


def per_device(spectra, legendre, pair_of_slot, lat_owner, region_of_lon):
    members, steps_here, slot_count, _, length = spectra.shape
    lat = legendre.shape[2]
    narrow, wide = lax.axis_size("narrow"), lax.axis_size("wide")
    lat_here = lat // narrow
    lon = region_of_lon.shape[0]
    rows = members * steps_here * 2
    chunks = slot_count // CHUNK
    regions = REG_DEV * wide
    lanes = steps_here * 128
    dims = (narrow, wide, chunks, rows, members, steps_here, lat_here, lon)
    vmem = pl.BlockSpec(memory_space=pltpu.VMEM)
    hbm = pl.BlockSpec(memory_space=pl.ANY)
    best = pl.pallas_call(
        functools.partial(fields_kernel, dims),
        in_specs=[pl.BlockSpec(memory_space=pltpu.SMEM), vmem, vmem, hbm, hbm],
        out_specs=vmem,
        out_shape=jax.ShapeDtypeStruct((2 * members, REG_DEV, lat_here), jnp.float32),
        scratch_shapes=[
            pltpu.VMEM((2, length, CHUNK // 2, lat), jnp.bfloat16),
            pltpu.VMEM((2, members, steps_here, CHUNK, 2, length), jnp.bfloat16),
            pltpu.VMEM((HALF, rows, length), jnp.float32),
            pltpu.VMEM((length * CHUNK // 2, 128), jnp.float32),
            pltpu.VMEM((CHUNK * rows, 128), jnp.float32),
            pltpu.VMEM((2 * members * lat, narrow * 128), jnp.bfloat16),
            pltpu.VMEM((chunks, narrow, 2 * CHUNK, lanes), jnp.float32),
            pltpu.VMEM((chunks, narrow, 2 * CHUNK, lanes), jnp.float32),
            pltpu.VMEM((4, chunks * 128, 128), jnp.float32),
            pltpu.VMEM((2, FINE, chunks * 128), jnp.float32),
            pltpu.VMEM((2, FINE, chunks * 128), jnp.float32),
            pltpu.VMEM((lon // 2, lanes), jnp.float32),
            pltpu.VMEM((lon // 2, lanes), jnp.float32),
            pltpu.VMEM((lon, 128), jnp.float32),
            pltpu.VMEM((3, lon, 128), jnp.float32),
            pltpu.VMEM((2, 3, lon // 16, 128), jnp.float32),
            pltpu.VMEM((2, regions, lon // 2), jnp.bfloat16),
            pltpu.VMEM((2, regions, lon // 16), jnp.bfloat16),
            pltpu.VMEM((4, regions, 128), jnp.float32),
            pltpu.VMEM((regions, 128), jnp.float32),
            pltpu.VMEM((wide, REG_DEV, 128), jnp.float32),
            pltpu.SemaphoreType.DMA((2, 2)),
            pltpu.SemaphoreType.DMA((2, chunks, narrow)),
            pltpu.SemaphoreType.DMA((2, chunks, narrow)),
            pltpu.SemaphoreType.DMA((wide,)),
            pltpu.SemaphoreType.DMA((wide,)),
        ],
        compiler_params=pltpu.CompilerParams(
            collective_id=0, has_side_effects=True, vmem_limit_bytes=60 * 1024 * 1024
        ),
    )(
        pair_of_slot, lat_owner.reshape(1, lat), region_of_lon.reshape(-1, 128), spectra,
        jnp.transpose(legendre, (1, 0, 2)),
    )
    best = jnp.transpose(best, (0, 2, 1))
    return (best[:members], best[members:])


def solution(mesh):
    in_specs = (
        P(None, ("groups", "wide"), "narrow", None, None),
        P("narrow", None, None),
        P(),
        P(),
        P(),
    )
    out_specs = (P("groups", "narrow", "wide"), P("groups", "narrow", "wide"))

    def body(spectra, legendre, *rest):
        members, steps_here, slot_count = spectra.shape[:3]
        lat_here = legendre.shape[2] // mesh.shape["narrow"]
        packs = steps_here * lat_here == 128 and 2 * members * lat_here == 128
        packs = packs and slot_count % (2 * CHUNK) == 0 and slot_count >= 4 * CHUNK
        packs = packs and legendre.shape[2] == 128 and mesh.shape["narrow"] * CHUNK == 64
        packs = packs and rest[2].shape[0] == 2 * FINE * FINE
        chosen = per_device if packs else per_device_plain
        return chosen(spectra, legendre, *rest)

    return jax.shard_map(
        body, mesh=mesh, in_specs=in_specs, out_specs=out_specs, check_vma=False
    )
```

```python
import functools
import math

import jax
import jax.numpy as jnp
from jax import lax
from jax.experimental import pallas as pl
from jax.experimental.pallas import tpu as pltpu
from jax.sharding import PartitionSpec as P

M = 1280
LON = 2048
REG_DEV = 16
LON_FULL = 5120


def synthesize(operand, waves, start, width):
    columns = start + jnp.arange(width, dtype=jnp.int32)
    phase = waves[:, None] * columns[None, :] % LON_FULL
    angle = phase.astype(jnp.float32) * (2.0 * math.pi / LON_FULL)
    cosine = jnp.cos(angle)
    sine = jnp.sin(angle)
    rate = (waves.astype(jnp.float32) / M)[:, None]
    upper = jnp.concatenate([cosine, -rate * sine], axis=1)
    lower = jnp.concatenate([-sine, -rate * cosine], axis=1)
    table = jnp.concatenate([upper, lower], axis=0) * M ** (-0.5)
    return jnp.dot(operand, table, precision=lax.Precision.HIGHEST)


def synthesize_all(operand, waves):
    width = min(512, LON)
    starts = jnp.arange(LON // width, dtype=jnp.int32) * width

    def one_block(begin):
        return synthesize(operand, waves, begin, width)

    blocks = lax.map(one_block, starts)
    blocks = blocks.reshape(blocks.shape[0], blocks.shape[1], 2, width)
    value = jnp.transpose(blocks[:, :, 0], (1, 0, 2)).reshape(operand.shape[0], LON)
    slope = jnp.transpose(blocks[:, :, 1], (1, 0, 2)).reshape(operand.shape[0], LON)
    return (value, slope)


def region_peak(values, region_of_lon, wanted):
    hits = region_of_lon[:, None] == wanted[None, :]
    masked = jnp.where(hits[None, None], values[..., None], -1e30)
    return masked.max(axis=2)


def per_device_plain(spectra, legendre, pair_of_slot, lat_owner, region_of_lon):
    members = spectra.shape[0]
    steps_here = spectra.shape[1]
    slot_count = spectra.shape[2]
    length = spectra.shape[4]
    half_count = legendre.shape[0]
    lat_half = legendre.shape[2] // 2
    here = lax.axis_index("narrow")
    paired = lax.dynamic_slice_in_dim(pair_of_slot, here * slot_count, slot_count)
    position = jnp.arange(length, dtype=jnp.int32)[None, :]
    first_len = (M - paired)[:, None]
    leading = position < first_len
    offset = jnp.where(leading, position, position - first_len)
    even_term = offset % 2 == 0
    masks = jnp.stack(
        [leading & even_term, leading & ~even_term, ~leading & even_term, ~leading & ~even_term],
        axis=1,
    ).astype(jnp.bfloat16)
    ordered = jnp.transpose(spectra, (2, 0, 1, 3, 4))
    masked = masks[:, :, None, None, None, :] * ordered[:, None]
    masked = masked.reshape(half_count, 2, -1, length)
    table = legendre.reshape(half_count, length, 2, lat_half)
    sums = jnp.einsum("abrl,albj->abrj", masked, table, preferred_element_type=jnp.float32)
    sums = sums.reshape(slot_count, 4, members, steps_here, 2, lat_half)
    north_lead = sums[:, 0] + sums[:, 1]
    south_lead = sums[:, 0] - sums[:, 1]
    north_tail = sums[:, 2] + sums[:, 3]
    south_tail = sums[:, 2] - sums[:, 3]
    lead = jnp.concatenate([north_lead, jnp.flip(south_lead, axis=-1)], axis=-1)
    tail = jnp.concatenate([north_tail, jnp.flip(south_tail, axis=-1)], axis=-1)
    waved = jnp.stack([lead, tail], axis=1).reshape(2 * slot_count, members, steps_here, 2, -1)
    order = jnp.argsort(lat_owner, stable=True)
    waved = jnp.take(waved, order, axis=4)
    arrived = lax.all_to_all(waved, "narrow", split_axis=4, concat_axis=0, tiled=True)
    waves = jnp.stack([pair_of_slot, M - 1 - pair_of_slot], axis=1).reshape(-1)
    lat_here = arrived.shape[4]
    operand = jnp.transpose(arrived, (1, 2, 4, 3, 0)).reshape(members * steps_here * lat_here, -1)
    value, slope = synthesize_all(operand, waves)
    value = value.reshape(members, steps_here, lat_here, LON).max(axis=1)
    slope = jnp.abs(slope).reshape(members, steps_here, lat_here, LON).max(axis=1)
    wide_count = lax.axis_size("wide")
    mine_start = lax.axis_index("wide") * REG_DEV
    wanted = jnp.arange(REG_DEV * wide_count, dtype=jnp.int32)
    peaks = region_peak(value, region_of_lon, wanted)
    slopes = region_peak(slope, region_of_lon, wanted)
    peaks, slopes = lax.pmax((peaks, slopes), "wide")
    peak = lax.dynamic_slice_in_dim(peaks, mine_start, REG_DEV, 2)
    peak_slope = lax.dynamic_slice_in_dim(slopes, mine_start, REG_DEV, 2)
    return (peak, peak_slope)


CHUNK = 16
HALF = 8
FINE = 32
GROUP = 256
FETCHES = 4
LAST = 512
WIDEN = 32
MESH = pl.DeviceIdType.MESH


def split(values):
    high = values.astype(jnp.bfloat16)
    low = (values - high.astype(jnp.float32)).astype(jnp.bfloat16)
    return high, low


def dot(left, right):
    return jnp.dot(left, right, preferred_element_type=jnp.float32)


def turn(count):
    quarter = LON_FULL // 2
    whole = jnp.floor(count * (1.0 / quarter) + 0.5)
    angle = (count - whole * quarter) * (math.pi / LON_FULL)
    square = angle * angle
    sine = angle * (1.0 + square * (-1 / 6 + square * (1 / 120 + square * (-1 / 5040 + square * (1 / 362880)))))
    cosine = 1.0 + square * (
        -1 / 2 + square * (1 / 24 + square * (-1 / 720 + square * (1 / 40320 + square * (-1 / 3628800))))
    )
    turns = whole.astype(jnp.int32)
    swap = (turns & 1) == 1
    cos_sign = jnp.where(((turns + 1) & 2) == 2, -1.0, 1.0)
    sin_sign = jnp.where((turns & 2) == 2, -1.0, 1.0)
    return cos_sign * jnp.where(swap, sine, cosine), sin_sign * jnp.where(swap, cosine, sine)


def iota(shape, dim):
    return lax.broadcasted_iota(jnp.int32, shape, dim)


def fields_kernel(
    dims, pair_ref, owner_ref, region_ref, x_hbm, table_hbm, out_ref,
    table_buf, x_buf, lined, spread, last_row, sums, place, sent, held, ready, coef, coarse, fine, part_cos, part_sin, field,
    apart, apart_blocks, pick, pick_blocks, absent, peaks, peaks_in,
    fetch_sem, send_sem, recv_sem, wide_send, wide_recv,
):
    narrow, wide, chunks, rows, members, steps_here, lat_here, lon = dims
    me = lax.axis_index("narrow")
    me_wide = lax.axis_index("wide")
    slot_count = chunks * CHUNK
    pairs = CHUNK // 2
    half_lon = lon // 2
    lat = narrow * lat_here

    part = M // FETCHES
    parts_of = [pl.ds(n * part, part + (n == FETCHES - 1)) for n in range(FETCHES)]

    def fetches(c, slot):
        return (
            *(
                pltpu.make_async_copy(
                    table_hbm.at[span, pl.ds(pl.multiple_of(c * pairs, pairs), pairs), :], table_buf.at[slot, span],
                    fetch_sem.at[1 + n, slot],
                )
                for n, span in enumerate(parts_of)
            ),
            pltpu.make_async_copy(
                x_hbm.at[:, :, pl.ds(c * CHUNK, CHUNK), :, :], x_buf.at[slot], fetch_sem.at[0, slot]
            ),
        )

    def start_fetch(c, slot):
        for copy in fetches(c, slot):
            copy.start()

    def partner(ahead):
        return lax.rem(me + ahead, narrow)

    order = (2, 1, 3) if narrow == 4 else tuple(range(1, narrow))

    def rows_of(c, kind):
        if kind < 2:
            return pl.ds(pl.multiple_of(c * 2 * CHUNK + kind * CHUNK, CHUNK), CHUNK), kind
        return pl.ds(pl.multiple_of(c * 2 * CHUNK, 2 * CHUNK), (kind - 1) * 2 * CHUNK), 0

    def send(c, ahead, kind):
        target = partner(ahead)
        span, at = rows_of(c, kind)
        return pltpu.make_async_remote_copy(
            src_ref=sent.at[target, span], dst_ref=held.at[me, span],
            send_sem=send_sem.at[at, c, target], recv_sem=recv_sem.at[at, c, me],
            device_id={"narrow": target}, device_id_type=MESH,
        )

    def arrive(c, kind):
        for ahead in range(1, narrow):
            origin = partner(ahead)
            span, at = rows_of(c, kind)
            pltpu.make_async_remote_copy(
                src_ref=sent.at[origin, span], dst_ref=held.at[origin, span],
                send_sem=send_sem.at[at, c, origin], recv_sem=recv_sem.at[at, c, origin],
                device_id={"narrow": origin}, device_id_type=MESH,
            ).wait_recv()

    start_fetch(0, 0)
    barrier = pltpu.get_barrier_semaphore()
    for ahead in range(1, narrow):
        pl.semaphore_signal(barrier, inc=1, device_id={"narrow": partner(ahead)}, device_id_type=MESH)
    for ahead in range(1, wide):
        pl.semaphore_signal(
            barrier, inc=1, device_id={"wide": lax.rem(me_wide + ahead, wide)}, device_id_type=MESH
        )

    lane = iota((lat, lat), 1)
    below = iota((lat, lat), 0)
    below = jnp.where(below < lat // 2, below, 3 * lat // 2 - 1 - below)
    owners = jnp.broadcast_to(owner_ref[...], (lat, lat)).astype(jnp.float32)
    owner = jnp.sum(jnp.where(lane == below, owners, 0.0), axis=1, keepdims=True)
    ahead_of = (owners < owner) | ((owners == owner) & (lane < below))
    rank = jnp.sum(jnp.where(ahead_of, 1.0, 0.0), axis=1, keepdims=True).astype(jnp.int32)
    column = iota((lat, narrow * 128), 1)
    goal = (column // 128) * lat_here + column % lat_here
    for n in range(2 * members):
        wanted = (goal == rank) & ((column // lat_here) % (2 * members) == n)
        place[n * lat:(n + 1) * lat, :] = jnp.where(wanted, 1.0, 0.0).astype(jnp.bfloat16)

    position = iota((1, M), 1)
    sign = (1 - 2 * (position & 1)).astype(jnp.float32).astype(jnp.bfloat16)
    half_lane = iota((rows, 128), 1)
    block = M // 8

    def one_pair(c, slot, h, u):
        at = h * (HALF // 2) + u
        parts = []
        extras = []
        for half in range(2):
            inside = 2 * at + half
            lines = 2 * u + half
            first_len = M - pair_ref[me * slot_count + c * CHUNK + inside]
            leading = (position < first_len).astype(jnp.float32).astype(jnp.bfloat16)
            flip = (1 - 2 * (first_len & 1)).astype(jnp.float32)
            for e in range(members):
                for t in range(steps_here):
                    row = 2 * (e * steps_here + t)
                    lined[lines, row:row + 2, :] = x_buf[slot, e, t, inside]
            body = lined[lines, :, :M]
            first_part = body * leading
            parts.extend((first_part, first_part * sign, body, body * sign))
            last = lined[lines, :, M:].astype(jnp.float32)
            extras.append((last, flip))
        table = spread[h, pl.ds(u, M, stride=4), :].astype(jnp.bfloat16)
        out = dot(jnp.concatenate(parts, axis=0), table)
        edge = last_row[pl.ds(at, 1), :]
        for half in range(2):
            base = half * 4 * rows
            piece = [out[base + v * rows:base + (v + 1) * rows] for v in range(4)]
            last, flip = extras[half]
            term = last * edge
            piece[2] = piece[2] - piece[0] + term
            piece[3] = (piece[3] - piece[1] + term) * flip
            for tail_at in range(2):
                north, south = piece[2 * tail_at], piece[2 * tail_at + 1]
                if half == 0:
                    both = jnp.where(half_lane < 64, north, pltpu.roll(south, 64, 1))
                else:
                    both = jnp.where(half_lane < 64, pltpu.roll(north, 64, 1), south)
                at_row = (tail_at * HALF + 2 * u + half) * rows
                sums[at_row:at_row + rows, :] = both

    def one_half(c, slot, h):
        for u in range(HALF // 2):
            one_pair(c, slot, h, u)
        highs, lows = [], []
        for t in range(steps_here):
            wide_rows = jnp.concatenate(
                [
                    sums[pl.ds((e * steps_here + t) * 2 + part, CHUNK, stride=rows), :]
                    for part in range(2) for e in range(members)
                ],
                axis=1,
            )
            high, low = split(wide_rows)
            highs.append(high)
            lows.append(low)
        both = dot(jnp.concatenate(highs + lows, axis=0), place[...])
        moved = both[:steps_here * CHUNK] + both[steps_here * CHUNK:]
        where_to = pl.ds(pl.multiple_of((2 * c + h) * CHUNK, CHUNK), CHUNK)
        for t in range(steps_here):
            for d in range(narrow):
                sent[d, where_to, t * 128:(t + 1) * 128] = (
                    moved[t * CHUNK:(t + 1) * CHUNK, d * 128:(d + 1) * 128]
                )
        held[me, where_to, :] = sent[me, where_to, :]

        def send_when(when, first, kind):
            @pl.when(when)
            def _():
                for ahead in order:
                    send(first, ahead, kind).start()

        @pl.when((c == 0) & (h == 0))
        def _():
            pl.semaphore_wait(barrier, narrow - 1 + wide - 1)

        send_when((c == 0) & (h == 0), 0, 0)
        send_when((c == 0) & (h == 1), 0, 1)
        send_when(((c == 1) | (c == chunks - 2)) & (h == 1), c, 2)
        send_when((c > 1) & (c < chunks - 2) & (lax.rem(c, 2) == 1) & (h == 1), c - 1, 3)
        send_when((c == chunks - 1) & (h == 0), chunks - 1, 0)
        send_when((c == chunks - 1) & (h == 1), chunks - 1, 1)

    def tables(c):
        lanes = iota((8, 128), 1)
        base = lanes & ~HALF
        lead = jnp.zeros((8, 128), jnp.int32)
        for h in range(2):
            for d in range(narrow):
                for s in range(HALF):
                    at = (h * narrow + d) * CHUNK + s
                    lead = jnp.where(base == at, pair_ref[d * slot_count + c * CHUNK + h * HALF + s], lead)
        wave = jnp.where((lanes & HALF) == HALF, M - 1 - lead, lead).astype(jnp.float32)
        here = pl.ds(pl.multiple_of(c * 128, 128), 128)
        rows_of = jnp.broadcast_to(wave[:1], (FINE, 128))
        index = iota((FINE, 128), 0).astype(jnp.float32)
        cosine, sine = turn(rows_of * (index * (2.0 * FINE)))
        coarse[0, :, here] = cosine
        coarse[1, :, here] = sine
        cosine, sine = turn(rows_of * (index * 2.0 + 1.0))
        fine[0, :, here] = cosine
        fine[1, :, here] = sine
        down = jnp.transpose(jnp.broadcast_to(wave[:1], (128, 128)))
        cosine, sine = turn(down * (lon - 1.0))
        low = iota((128, 128), 1) < 64
        cosine = cosine * (M ** -0.5)
        sine = sine * (M ** -0.5)
        rate = down * (1.0 / M)
        coef[0, here, :] = cosine * jnp.where(low, 1.0, -rate)
        coef[1, here, :] = sine * jnp.where(low, -1.0, -rate)
        coef[2, here, :] = sine * jnp.where(low, 1.0, -rate)
        coef[3, here, :] = cosine * jnp.where(low, 1.0, rate)

    def one_chunk(c, carry):
        slot = lax.rem(c, 2)
        for copy in fetches(c, slot):
            copy.wait()

        @pl.when(c + 1 < chunks)
        def _():
            start_fetch(c + 1, 1 - slot)

        def widen(groups):
            def some(n, carry):
                for v in range(block // WIDEN):
                    at = n * block + v * WIDEN
                    part = table_buf[slot, pl.ds(at, WIDEN)].astype(jnp.float32).reshape(WIDEN // 2, 2, pairs, 128)
                    first, second = part[:, 0], part[:, 1]
                    upper = iota(first.shape, 1) < 4
                    where_to = pl.ds(pl.multiple_of(at * 4, 8), WIDEN * 4)
                    if 0 in groups:
                        merged = jnp.where(upper, first, pltpu.roll(second, 4, 1))
                        spread[0, where_to, :] = merged.reshape(WIDEN * 4, 128)
                    if 1 in groups:
                        merged = jnp.where(upper, pltpu.roll(first, 4, 1), second)
                        spread[1, where_to, :] = merged.reshape(WIDEN * 4, 128)
                return carry

            lax.fori_loop(0, 8, some, 0)

        @pl.when(c > 0)
        def _():
            widen((0, 1))

        last_row[...] = table_buf[slot, M].astype(jnp.float32)

        def halves(h, carry):
            @pl.when((c == 0) & (h == 0))
            def _():
                widen((0,))

            @pl.when((c == 0) & (h == 1))
            def _():
                widen((1,))

            one_half(c, slot, h)
            return carry

        lax.fori_loop(0, 2, halves, 0)
        tables(c)
        return carry

    lax.fori_loop(0, chunks, one_chunk, 0)

    def turned(pieces, here):
        evens, odds = [], []
        c1, s1, c2, s2 = (coef[n, here, :] for n in range(4))
        for t in range(steps_here):
            data = jnp.concatenate([held[d, span, t * 128:(t + 1) * 128] for d, span in pieces], axis=0)
            other = pltpu.roll(data, 64, 1)
            evens.append(data * c1 + other * s1)
            odds.append(data * c2 + other * s2)
        return split(jnp.concatenate(evens, axis=1)), split(jnp.concatenate(odds, axis=1))

    def waves_at(g, coarse_of, fine_of):
        cosines, sines = [], []
        many = GROUP // FINE
        span = pl.ds(pl.multiple_of(g * many, many), many)
        cu, su = coarse_of(0, span), coarse_of(1, span)
        c2, s2 = fine_of
        for u in range(many):
            c1, s1 = cu[u:u + 1], su[u:u + 1]
            cosines.append(c1 * c2 - s1 * s2)
            sines.append(s1 * c2 + c1 * s2)
        return split(jnp.concatenate(cosines, axis=0)), split(jnp.concatenate(sines, axis=0))

    def span_of(c, h):
        return pl.ds(pl.multiple_of((2 * c + h) * CHUNK, CHUNK), CHUNK)

    regions = wide * REG_DEV
    blocks = half_lon // 8

    def region_tables():
        number = iota((regions, 128), 0)
        begin = jnp.zeros((regions, 128), jnp.int32)
        end = begin
        for n in range(lon // 128):
            ids = region_ref[n:n + 1, :]
            begin = begin + jnp.where(ids < number, 1, 0)
            end = end + jnp.where(ids <= number, 1, 0)
        reach = 64
        while reach:
            begin = begin + pltpu.roll(begin, reach, 1)
            end = end + pltpu.roll(end, reach, 1)
            reach //= 2
        lanes = iota((regions, 128), 1)
        for side in range(2):
            if side == 0:
                first, last = half_lon - jnp.minimum(end, half_lon), half_lon - jnp.minimum(begin, half_lon)
            else:
                first, last = jnp.maximum(begin, half_lon) - half_lon, jnp.maximum(end, half_lon) - half_lon
            here = first < last
            for n in range(half_lon // 128):
                hit = (lanes + n * 128 == first) & here
                pick[side, :, n * 128:(n + 1) * 128] = jnp.where(hit, 1.0, 0.0).astype(jnp.bfloat16)
            start = (first + 7) >> 3
            whole = start * 8 < last
            pick_blocks[side] = jnp.where((lanes == start) & whole, 1.0, 0.0).astype(jnp.bfloat16)
            absent[2 * side] = jnp.where(here, 0.0, -1e30)
            absent[2 * side + 1] = jnp.where(whole, 0.0, -1e30)
        across, down = iota((128, 128), 1), iota((128, 128), 0)
        mirror = jnp.where(across + down == 127, 1.0, 0.0).astype(jnp.bfloat16)
        ids = region_ref[...].astype(jnp.float32)
        flipped = dot(ids.astype(jnp.bfloat16), mirror)
        tiles = half_lon // 128
        sub = iota((16, 8, 128), 1)
        for side in range(2):
            for n in range(tiles):
                source = flipped[tiles - 1 - n:tiles - n] if side == 0 else ids[tiles + n:tiles + n + 1]
                column = jnp.transpose(jnp.broadcast_to(source, (128, 128)))
                span = pl.ds(side * half_lon + n * 128, 128)
                field[span, :] = column
                column = column.reshape(16, 8, 128)
                for i, step in enumerate((1, 2, 4)):
                    same = (pltpu.roll(column, 8 - step, 1) == column) & (sub + step < 8)
                    apart[i, span, :] = jnp.where(same, 0.0, -1e30).reshape(128, 128)
            starts = field[pl.ds(side * half_lon, blocks, stride=8), :]
            for i, step in enumerate((1, 2, 4)):
                same = (pltpu.roll(starts, blocks - step, 0) == starts) & (iota((blocks, 128), 0) + step < blocks)
                apart_blocks[side, i] = jnp.where(same, 0.0, -1e30)

    region_tables()

    def two_chunks(k, carry):
        first = 2 * k

        @pl.when(k == 0)
        def _():
            arrive(0, 0)
            arrive(0, 1)
            arrive(1, 2)

        @pl.when(k > 0)
        def _():
            arrive(first, 3)

        here = pl.ds(pl.multiple_of(first * 128, 256), 256)
        pieces = [(d, span_of(first + n, h)) for n in range(2) for h in range(2) for d in range(narrow)]
        (even_hi, even_lo), (odd_hi, odd_lo) = turned(pieces, here)
        fine_of = fine[0, :, here], fine[1, :, here]

        def one_group(g, carry):
            (cos_hi, cos_lo), (sin_hi, sin_lo) = waves_at(g, lambda n, span: coarse[n, span, here], fine_of)
            where_to = pl.ds(pl.multiple_of(g * GROUP, GROUP), GROUP)
            new_cos = dot(cos_hi, even_hi) + dot(cos_lo, even_hi) + dot(cos_hi, even_lo)
            new_sin = dot(sin_hi, odd_hi) + dot(sin_lo, odd_hi) + dot(sin_hi, odd_lo)

            @pl.when(k == 0)
            def _():
                part_cos[where_to, :] = new_cos
                part_sin[where_to, :] = new_sin

            @pl.when(k > 0)
            def _():
                part_cos[where_to, :] += new_cos
                part_sin[where_to, :] += new_sin

            return carry

        lax.fori_loop(0, half_lon // GROUP, one_group, 0)
        return carry

    lax.fori_loop(0, chunks // 2 - 1, two_chunks, 0)

    def angles_ahead(c, h):
        chunk_here = pl.ds(c * 128, 128)

        def doubled(values):
            kept = iota(values.shape, 1) < 64
            moved = pltpu.roll(values, 64, 1)
            return jnp.where(kept, values, moved) if h == 0 else jnp.where(kept, moved, values)

        fine_of = tuple(doubled(fine[n, :, chunk_here]) for n in range(2))
        low = iota((GROUP, 128), 1) < 64

        def one_group(g, carry):
            both = waves_at(g, lambda n, span: doubled(coarse[n, span, chunk_here]), fine_of)
            where_to = pl.ds(pl.multiple_of(g * GROUP, GROUP), GROUP)
            for n, (high, part) in enumerate(both):
                ready[h, n, where_to, :128] = jnp.where(low, high, part)
                ready[h, n, where_to, 128:] = high
            return carry

        lax.fori_loop(0, half_lon // GROUP, one_group, 0)

    def half_chunk(c, h, last):
        here = pl.ds((c * 2 + h) * 64, 64)
        (even_hi, even_lo), (odd_hi, odd_lo) = turned([(d, span_of(c, h)) for d in range(narrow)], here)
        even = jnp.concatenate([even_hi, even_hi, even_lo, jnp.zeros_like(even_lo)], axis=0)
        odd = jnp.concatenate([odd_hi, odd_hi, odd_lo, jnp.zeros_like(odd_lo)], axis=0)
        sign = jnp.where(iota((LAST, 128), 1) < 64, 1.0, -1.0)

        def one_group(g, carry):
            where_to = pl.ds(pl.multiple_of(g * LAST, LAST), LAST)
            new_cos = dot(ready[h, 0, where_to, :], even)
            new_sin = dot(ready[h, 1, where_to, :], odd)
            if not last:
                part_cos[where_to, :] += new_cos
                part_sin[where_to, :] += new_sin
                return carry
            most = [None, None]
            least = [None, None]
            for t in range(steps_here):
                lanes = slice(t * 128, (t + 1) * 128)
                even_part = part_cos[where_to, lanes] + new_cos[:, lanes]
                odd_part = part_sin[where_to, lanes] + new_sin[:, lanes]
                for side, full in enumerate((even_part + odd_part, even_part - odd_part)):
                    most[side] = full if t == 0 else jnp.maximum(most[side], full)
                    least[side] = full if t == 0 else jnp.minimum(least[side], full)
            for side in range(2):
                span = pl.ds(pl.multiple_of(side * half_lon + g * LAST, LAST), LAST)
                best = jnp.maximum(most[side], least[side] * sign)
                best = best.reshape(LAST // 8, 8, 128)
                for i, step in enumerate((1, 2, 4)):
                    best = jnp.maximum(
                        best, pltpu.roll(best, 8 - step, 1) + apart[i, span, :].reshape(LAST // 8, 8, 128)
                    )
                field[span, :] = best.reshape(LAST, 128)
            return carry

        lax.fori_loop(0, half_lon // LAST, one_group, 0)

    angles_ahead(chunks - 2, 0)
    angles_ahead(chunks - 2, 1)
    arrive(chunks - 2, 2)
    half_chunk(chunks - 2, 0, False)
    half_chunk(chunks - 2, 1, False)
    angles_ahead(chunks - 1, 0)
    angles_ahead(chunks - 1, 1)
    arrive(chunks - 1, 0)
    half_chunk(chunks - 1, 0, False)
    arrive(chunks - 1, 1)
    half_chunk(chunks - 1, 1, True)

    def chosen(picks, values, missing):
        high, low = split(values)
        both = dot(picks, jnp.concatenate([high, low], axis=1))
        return both[:, :128] + both[:, 128:] + missing

    parts = []
    for side in range(2):
        starts = field[pl.ds(side * half_lon, blocks, stride=8), :]
        for i, step in enumerate((1, 2, 4)):
            starts = jnp.maximum(starts, pltpu.roll(starts, blocks - step, 0) + apart_blocks[side, i])
        parts.append(chosen(pick_blocks[side], starts, absent[2 * side + 1]))
        parts.append(chosen(pick[side], field[pl.ds(side * half_lon, half_lon), :], absent[2 * side]))
    peaks[...] = jnp.maximum(jnp.maximum(parts[0], parts[1]), jnp.maximum(parts[2], parts[3]))

    def exchange(ahead, arriving):
        other = lax.rem(me_wide + ahead, wide)
        return pltpu.make_async_remote_copy(
            src_ref=peaks.at[pl.ds(pl.multiple_of(other * REG_DEV, REG_DEV), REG_DEV)],
            dst_ref=peaks_in.at[other if arriving else me_wide],
            send_sem=wide_send.at[other], recv_sem=wide_recv.at[other if arriving else me_wide],
            device_id={"wide": other}, device_id_type=MESH,
        )

    for ahead in range(wide - 1, 0, -1):
        exchange(ahead, False).start()
    for ahead in range(1, narrow):
        for kind in range(2):
            send(0, ahead, kind).wait_send()
            send(chunks - 1, ahead, kind).wait_send()
        send(1, ahead, 2).wait_send()
        send(chunks - 2, ahead, 2).wait_send()
        for c in range(2, chunks - 2, 2):
            send(c, ahead, 3).wait_send()
    best = peaks[pl.ds(pl.multiple_of(me_wide * REG_DEV, REG_DEV), REG_DEV), :]
    for ahead in range(1, wide):
        exchange(ahead, True).wait_recv()
        best = jnp.maximum(best, peaks_in[lax.rem(me_wide + ahead, wide)])
    for n in range(2 * members):
        out_ref[n] = best[:, n * lat_here:(n + 1) * lat_here]

    for ahead in range(1, wide):
        exchange(ahead, False).wait_send()


def per_device(spectra, legendre, pair_of_slot, lat_owner, region_of_lon):
    members, steps_here, slot_count, _, length = spectra.shape
    lat = legendre.shape[2]
    narrow, wide = lax.axis_size("narrow"), lax.axis_size("wide")
    lat_here = lat // narrow
    lon = region_of_lon.shape[0]
    rows = members * steps_here * 2
    chunks = slot_count // CHUNK
    regions = REG_DEV * wide
    lanes = steps_here * 128
    dims = (narrow, wide, chunks, rows, members, steps_here, lat_here, lon)
    vmem = pl.BlockSpec(memory_space=pltpu.VMEM)
    hbm = pl.BlockSpec(memory_space=pl.ANY)
    best = pl.pallas_call(
        functools.partial(fields_kernel, dims),
        in_specs=[pl.BlockSpec(memory_space=pltpu.SMEM), vmem, vmem, hbm, hbm],
        out_specs=vmem,
        out_shape=jax.ShapeDtypeStruct((2 * members, REG_DEV, lat_here), jnp.float32),
        scratch_shapes=[
            pltpu.VMEM((2, length, CHUNK // 2, lat), jnp.bfloat16),
            pltpu.VMEM((2, members, steps_here, CHUNK, 2, length), jnp.bfloat16),
            pltpu.VMEM((HALF, rows, length), jnp.bfloat16),
            pltpu.VMEM((2, M * 4, 128), jnp.float32),
            pltpu.VMEM((CHUNK // 2, 128), jnp.float32),
            pltpu.VMEM((CHUNK * rows, 128), jnp.float32),
            pltpu.VMEM((2 * members * lat, narrow * 128), jnp.bfloat16),
            pltpu.VMEM((narrow, chunks * 2 * CHUNK, lanes), jnp.float32),
            pltpu.VMEM((narrow, chunks * 2 * CHUNK, lanes), jnp.float32),
            pltpu.VMEM((2, 2, lon // 2, 256), jnp.bfloat16),
            pltpu.VMEM((4, chunks * 128, 128), jnp.float32),
            pltpu.VMEM((2, FINE, chunks * 128), jnp.float32),
            pltpu.VMEM((2, FINE, chunks * 128), jnp.float32),
            pltpu.VMEM((lon // 2, lanes), jnp.float32),
            pltpu.VMEM((lon // 2, lanes), jnp.float32),
            pltpu.VMEM((lon, 128), jnp.float32),
            pltpu.VMEM((3, lon, 128), jnp.float32),
            pltpu.VMEM((2, 3, lon // 16, 128), jnp.float32),
            pltpu.VMEM((2, regions, lon // 2), jnp.bfloat16),
            pltpu.VMEM((2, regions, lon // 16), jnp.bfloat16),
            pltpu.VMEM((4, regions, 128), jnp.float32),
            pltpu.VMEM((regions, 128), jnp.float32),
            pltpu.VMEM((wide, REG_DEV, 128), jnp.float32),
            pltpu.SemaphoreType.DMA((1 + FETCHES, 2)),
            pltpu.SemaphoreType.DMA((2, chunks, narrow)),
            pltpu.SemaphoreType.DMA((2, chunks, narrow)),
            pltpu.SemaphoreType.DMA((wide,)),
            pltpu.SemaphoreType.DMA((wide,)),
        ],
        compiler_params=pltpu.CompilerParams(
            collective_id=0, has_side_effects=True, vmem_limit_bytes=60 * 1024 * 1024
        ),
    )(
        pair_of_slot, lat_owner.reshape(1, lat), region_of_lon.reshape(-1, 128), spectra,
        jnp.transpose(legendre, (1, 0, 2)),
    )
    best = jnp.transpose(best, (0, 2, 1))
    return (best[:members], best[members:])


def solution(mesh):
    in_specs = (
        P(None, ("groups", "wide"), "narrow", None, None),
        P("narrow", None, None),
        P(),
        P(),
        P(),
    )
    out_specs = (P("groups", "narrow", "wide"), P("groups", "narrow", "wide"))

    def body(spectra, legendre, *rest):
        members, steps_here, slot_count = spectra.shape[:3]
        lat_here = legendre.shape[2] // mesh.shape["narrow"]
        packs = steps_here * lat_here == 128 and 2 * members * lat_here == 128
        packs = packs and slot_count % (2 * CHUNK) == 0 and slot_count >= 4 * CHUNK
        packs = packs and legendre.shape[2] == 128 and mesh.shape["narrow"] * CHUNK == 64
        packs = packs and rest[2].shape[0] == 2 * FINE * FINE
        chosen = per_device if packs else per_device_plain
        return chosen(spectra, legendre, *rest)

    return jax.shard_map(
        body, mesh=mesh, in_specs=in_specs, out_specs=out_specs, check_vma=False
    )
```

```python
import functools
import math

import jax
import jax.numpy as jnp
from jax import lax
from jax.experimental import pallas as pl
from jax.experimental.pallas import tpu as pltpu
from jax.sharding import PartitionSpec as P

M = 1280
LON = 2048
REG_DEV = 16
LON_FULL = 5120


def synthesize(operand, waves, start, width):
    columns = start + jnp.arange(width, dtype=jnp.int32)
    phase = waves[:, None] * columns[None, :] % LON_FULL
    angle = phase.astype(jnp.float32) * (2.0 * math.pi / LON_FULL)
    cosine = jnp.cos(angle)
    sine = jnp.sin(angle)
    rate = (waves.astype(jnp.float32) / M)[:, None]
    upper = jnp.concatenate([cosine, -rate * sine], axis=1)
    lower = jnp.concatenate([-sine, -rate * cosine], axis=1)
    table = jnp.concatenate([upper, lower], axis=0) * M ** (-0.5)
    return jnp.dot(operand, table, precision=lax.Precision.HIGHEST)


def synthesize_all(operand, waves):
    width = min(512, LON)
    starts = jnp.arange(LON // width, dtype=jnp.int32) * width

    def one_block(begin):
        return synthesize(operand, waves, begin, width)

    blocks = lax.map(one_block, starts)
    blocks = blocks.reshape(blocks.shape[0], blocks.shape[1], 2, width)
    value = jnp.transpose(blocks[:, :, 0], (1, 0, 2)).reshape(operand.shape[0], LON)
    slope = jnp.transpose(blocks[:, :, 1], (1, 0, 2)).reshape(operand.shape[0], LON)
    return (value, slope)


def region_peak(values, region_of_lon, wanted):
    hits = region_of_lon[:, None] == wanted[None, :]
    masked = jnp.where(hits[None, None], values[..., None], -1e30)
    return masked.max(axis=2)


def per_device_plain(spectra, legendre, pair_of_slot, lat_owner, region_of_lon):
    members = spectra.shape[0]
    steps_here = spectra.shape[1]
    slot_count = spectra.shape[2]
    length = spectra.shape[4]
    half_count = legendre.shape[0]
    lat_half = legendre.shape[2] // 2
    here = lax.axis_index("narrow")
    paired = lax.dynamic_slice_in_dim(pair_of_slot, here * slot_count, slot_count)
    position = jnp.arange(length, dtype=jnp.int32)[None, :]
    first_len = (M - paired)[:, None]
    leading = position < first_len
    offset = jnp.where(leading, position, position - first_len)
    even_term = offset % 2 == 0
    masks = jnp.stack(
        [leading & even_term, leading & ~even_term, ~leading & even_term, ~leading & ~even_term],
        axis=1,
    ).astype(jnp.bfloat16)
    ordered = jnp.transpose(spectra, (2, 0, 1, 3, 4))
    masked = masks[:, :, None, None, None, :] * ordered[:, None]
    masked = masked.reshape(half_count, 2, -1, length)
    table = legendre.reshape(half_count, length, 2, lat_half)
    sums = jnp.einsum("abrl,albj->abrj", masked, table, preferred_element_type=jnp.float32)
    sums = sums.reshape(slot_count, 4, members, steps_here, 2, lat_half)
    north_lead = sums[:, 0] + sums[:, 1]
    south_lead = sums[:, 0] - sums[:, 1]
    north_tail = sums[:, 2] + sums[:, 3]
    south_tail = sums[:, 2] - sums[:, 3]
    lead = jnp.concatenate([north_lead, jnp.flip(south_lead, axis=-1)], axis=-1)
    tail = jnp.concatenate([north_tail, jnp.flip(south_tail, axis=-1)], axis=-1)
    waved = jnp.stack([lead, tail], axis=1).reshape(2 * slot_count, members, steps_here, 2, -1)
    order = jnp.argsort(lat_owner, stable=True)
    waved = jnp.take(waved, order, axis=4)
    arrived = lax.all_to_all(waved, "narrow", split_axis=4, concat_axis=0, tiled=True)
    waves = jnp.stack([pair_of_slot, M - 1 - pair_of_slot], axis=1).reshape(-1)
    lat_here = arrived.shape[4]
    operand = jnp.transpose(arrived, (1, 2, 4, 3, 0)).reshape(members * steps_here * lat_here, -1)
    value, slope = synthesize_all(operand, waves)
    value = value.reshape(members, steps_here, lat_here, LON).max(axis=1)
    slope = jnp.abs(slope).reshape(members, steps_here, lat_here, LON).max(axis=1)
    wide_count = lax.axis_size("wide")
    mine_start = lax.axis_index("wide") * REG_DEV
    wanted = jnp.arange(REG_DEV * wide_count, dtype=jnp.int32)
    peaks = region_peak(value, region_of_lon, wanted)
    slopes = region_peak(slope, region_of_lon, wanted)
    peaks, slopes = lax.pmax((peaks, slopes), "wide")
    peak = lax.dynamic_slice_in_dim(peaks, mine_start, REG_DEV, 2)
    peak_slope = lax.dynamic_slice_in_dim(slopes, mine_start, REG_DEV, 2)
    return (peak, peak_slope)


CHUNK = 16
HALF = 8
FINE = 32
GROUP = 256
FETCHES = 4
LAST = 512
WIDEN = 32
MESH = pl.DeviceIdType.MESH


def split(values):
    high = values.astype(jnp.bfloat16)
    low = (values - high.astype(jnp.float32)).astype(jnp.bfloat16)
    return high, low


def dot(left, right):
    return jnp.dot(left, right, preferred_element_type=jnp.float32)


def turn(count):
    quarter = LON_FULL // 2
    whole = jnp.floor(count * (1.0 / quarter) + 0.5)
    angle = (count - whole * quarter) * (math.pi / LON_FULL)
    square = angle * angle
    sine = angle * (1.0 + square * (-1 / 6 + square * (1 / 120 + square * (-1 / 5040 + square * (1 / 362880)))))
    cosine = 1.0 + square * (
        -1 / 2 + square * (1 / 24 + square * (-1 / 720 + square * (1 / 40320 + square * (-1 / 3628800))))
    )
    turns = whole.astype(jnp.int32)
    swap = (turns & 1) == 1
    cos_sign = jnp.where(((turns + 1) & 2) == 2, -1.0, 1.0)
    sin_sign = jnp.where((turns & 2) == 2, -1.0, 1.0)
    return cos_sign * jnp.where(swap, sine, cosine), sin_sign * jnp.where(swap, cosine, sine)


def iota(shape, dim):
    return lax.broadcasted_iota(jnp.int32, shape, dim)


def pieces_of(chunks):
    pieces = [(0, 0), (0, 1), (1, 2)]
    pieces += [(c, 3) for c in range(2, chunks - 2, 2)]
    return pieces + [(chunks - 2, 2), (chunks - 1, 0), (chunks - 1, 1)]


def fields_kernel(
    dims, pair_hbm, owner_hbm, region_hbm, x_hbm, table_hbm, out_ref,
    pair_ref, owner_ref, region_ref,
    table_buf, x_buf, lined, spread, last_row, sums, place, sent, held, ready, coef, coarse, fine, part_cos, part_sin, field,
    apart, apart_blocks, pick, pick_blocks, absent, peaks, peaks_in,
    fetch_sem, small_sem, send_sem, recv_sem, wide_send, wide_recv,
):
    narrow, wide, chunks, rows, members, steps_here, lat_here, lon = dims
    me = lax.axis_index("narrow")
    me_wide = lax.axis_index("wide")
    slot_count = chunks * CHUNK
    pairs = CHUNK // 2
    half_lon = lon // 2
    lat = narrow * lat_here

    part = M // FETCHES
    parts_of = [pl.ds(n * part, part + (n == FETCHES - 1)) for n in range(FETCHES)]

    def fetches(c, slot):
        return (
            *(
                pltpu.make_async_copy(
                    table_hbm.at[span, pl.ds(pl.multiple_of(c * pairs, pairs), pairs), :], table_buf.at[slot, span],
                    fetch_sem.at[1 + n, slot],
                )
                for n, span in enumerate(parts_of)
            ),
            pltpu.make_async_copy(
                x_hbm.at[:, :, pl.ds(c * CHUNK, CHUNK), :, :], x_buf.at[slot], fetch_sem.at[0, slot]
            ),
        )

    PIECES = pieces_of(chunks)

    def start_fetch(c, slot):
        for copy in fetches(c, slot):
            copy.start()

    def partner(ahead):
        return lax.rem(me + ahead, narrow)

    order = (2, 1, 3) if narrow == 4 else tuple(range(1, narrow))

    def rows_of(c, kind):
        if kind < 2:
            return pl.ds(pl.multiple_of(c * 2 * CHUNK + kind * CHUNK, CHUNK), CHUNK), kind
        return pl.ds(pl.multiple_of(c * 2 * CHUNK, 2 * CHUNK), (kind - 1) * 2 * CHUNK), 0

    def send(c, ahead, kind):
        target = partner(ahead)
        span, at = rows_of(c, kind)
        return pltpu.make_async_remote_copy(
            src_ref=sent.at[target, span], dst_ref=held.at[me, span],
            send_sem=send_sem.at[at, c, target], recv_sem=recv_sem.at[at, c, me],
            device_id={"narrow": target}, device_id_type=MESH,
        )

    def arrive(c, kind):
        for ahead in range(1, narrow):
            origin = partner(ahead)
            span, at = rows_of(c, kind)
            pltpu.make_async_remote_copy(
                src_ref=sent.at[origin, span], dst_ref=held.at[origin, span],
                send_sem=send_sem.at[at, c, origin], recv_sem=recv_sem.at[at, c, origin],
                device_id={"narrow": origin}, device_id_type=MESH,
            ).wait_recv()

    start_fetch(0, 0)
    small = [
        pltpu.make_async_copy(source, goal, small_sem.at[n])
        for n, (source, goal) in enumerate(
            ((owner_hbm, owner_ref), (pair_hbm, pair_ref), (region_hbm, region_ref))
        )
    ]
    for copy in small:
        copy.start()
    barrier = pltpu.get_barrier_semaphore()
    for ahead in range(1, narrow):
        pl.semaphore_signal(barrier, inc=1, device_id={"narrow": partner(ahead)}, device_id_type=MESH)
    for ahead in range(1, wide):
        pl.semaphore_signal(
            barrier, inc=1, device_id={"wide": lax.rem(me_wide + ahead, wide)}, device_id_type=MESH
        )

    for copy in small:
        copy.wait()

    lane = iota((lat, lat), 1)
    below = iota((lat, lat), 0)
    below = jnp.where(below < lat // 2, below, 3 * lat // 2 - 1 - below)
    owners = jnp.broadcast_to(owner_ref[...], (lat, lat)).astype(jnp.float32)
    owner = jnp.sum(jnp.where(lane == below, owners, 0.0), axis=1, keepdims=True)
    ahead_of = (owners < owner) | ((owners == owner) & (lane < below))
    rank = jnp.sum(jnp.where(ahead_of, 1.0, 0.0), axis=1, keepdims=True).astype(jnp.int32)
    column = iota((lat, narrow * 128), 1)
    goal = (column // 128) * lat_here + column % lat_here
    for n in range(2 * members):
        wanted = (goal == rank) & ((column // lat_here) % (2 * members) == n)
        place[n * lat:(n + 1) * lat, :] = jnp.where(wanted, 1.0, 0.0).astype(jnp.bfloat16)

    position = iota((1, M), 1)
    sign = (1 - 2 * (position & 1)).astype(jnp.float32).astype(jnp.bfloat16)
    half_lane = iota((rows, 128), 1)
    block = M // 8

    def one_pair(c, slot, h, u):
        at = h * (HALF // 2) + u
        parts = []
        extras = []
        for half in range(2):
            inside = 2 * at + half
            lines = 2 * u + half
            first_len = M - pair_ref[me * slot_count + c * CHUNK + inside]
            leading = (position < first_len).astype(jnp.float32).astype(jnp.bfloat16)
            flip = (1 - 2 * (first_len & 1)).astype(jnp.float32)
            for e in range(members):
                for t in range(steps_here):
                    row = 2 * (e * steps_here + t)
                    lined[lines, row:row + 2, :] = x_buf[slot, e, t, inside]
            body = lined[lines, :, :M]
            first_part = body * leading
            parts.extend((first_part, first_part * sign, body, body * sign))
            last = lined[lines, :, M:].astype(jnp.float32)
            extras.append((last, flip))
        table = spread[h, pl.ds(u, M, stride=4), :].astype(jnp.bfloat16)
        out = dot(jnp.concatenate(parts, axis=0), table)
        edge = last_row[pl.ds(at, 1), :]
        for half in range(2):
            base = half * 4 * rows
            piece = [out[base + v * rows:base + (v + 1) * rows] for v in range(4)]
            last, flip = extras[half]
            term = last * edge
            piece[2] = piece[2] - piece[0] + term
            piece[3] = (piece[3] - piece[1] + term) * flip
            for tail_at in range(2):
                north, south = piece[2 * tail_at], piece[2 * tail_at + 1]
                if half == 0:
                    both = jnp.where(half_lane < 64, north, pltpu.roll(south, 64, 1))
                else:
                    both = jnp.where(half_lane < 64, pltpu.roll(north, 64, 1), south)
                at_row = (tail_at * HALF + 2 * u + half) * rows
                sums[at_row:at_row + rows, :] = both

    def one_half(c, slot, h):
        for u in range(HALF // 2):
            one_pair(c, slot, h, u)
        highs, lows = [], []
        for t in range(steps_here):
            wide_rows = jnp.concatenate(
                [
                    sums[pl.ds((e * steps_here + t) * 2 + part, CHUNK, stride=rows), :]
                    for part in range(2) for e in range(members)
                ],
                axis=1,
            )
            high, low = split(wide_rows)
            highs.append(high)
            lows.append(low)
        both = dot(jnp.concatenate(highs + lows, axis=0), place[...])
        moved = both[:steps_here * CHUNK] + both[steps_here * CHUNK:]
        where_to = pl.ds(pl.multiple_of((2 * c + h) * CHUNK, CHUNK), CHUNK)
        for t in range(steps_here):
            for d in range(narrow):
                sent[d, where_to, t * 128:(t + 1) * 128] = (
                    moved[t * CHUNK:(t + 1) * CHUNK, d * 128:(d + 1) * 128]
                )
        held[me, where_to, :] = sent[me, where_to, :]

        def send_when(when, first, kind):
            @pl.when(when)
            def _():
                for ahead in order:
                    send(first, ahead, kind).start()

        @pl.when((c == 0) & (h == 0))
        def _():
            pl.semaphore_wait(barrier, narrow - 1 + wide - 1)

        for first, kind in PIECES:
            after = first + (kind == 3)
            send_when((c == first) & (h == 0) if kind == 0 else (c == after) & (h == 1), first, kind)

    def tables(c):
        lanes = iota((8, 128), 1)
        base = lanes & ~HALF
        lead = jnp.zeros((8, 128), jnp.int32)
        for h in range(2):
            for d in range(narrow):
                for s in range(HALF):
                    at = (h * narrow + d) * CHUNK + s
                    lead = jnp.where(base == at, pair_ref[d * slot_count + c * CHUNK + h * HALF + s], lead)
        wave = jnp.where((lanes & HALF) == HALF, M - 1 - lead, lead).astype(jnp.float32)
        here = pl.ds(pl.multiple_of(c * 128, 128), 128)
        rows_of = jnp.broadcast_to(wave[:1], (FINE, 128))
        index = iota((FINE, 128), 0).astype(jnp.float32)
        cosine, sine = turn(rows_of * (index * (2.0 * FINE)))
        coarse[0, :, here] = cosine
        coarse[1, :, here] = sine
        cosine, sine = turn(rows_of * (index * 2.0 + 1.0))
        fine[0, :, here] = cosine
        fine[1, :, here] = sine
        down = jnp.transpose(jnp.broadcast_to(wave[:1], (128, 128)))
        cosine, sine = turn(down * (lon - 1.0))
        low = iota((128, 128), 1) < 64
        cosine = cosine * (M ** -0.5)
        sine = sine * (M ** -0.5)
        rate = down * (1.0 / M)
        coef[0, here, :] = cosine * jnp.where(low, 1.0, -rate)
        coef[1, here, :] = sine * jnp.where(low, -1.0, -rate)
        coef[2, here, :] = sine * jnp.where(low, 1.0, -rate)
        coef[3, here, :] = cosine * jnp.where(low, 1.0, rate)

    def one_chunk(c, carry):
        slot = lax.rem(c, 2)
        x_copy, *table_copies = reversed(fetches(c, slot))
        x_copy.wait()
        table_copies = table_copies[::-1]

        @pl.when(c > 0)
        def _():
            for copy in table_copies:
                copy.wait()

            @pl.when(c + 1 < chunks)
            def _():
                start_fetch(c + 1, 1 - slot)

        def widen(groups, arriving=()):
            def some(n, carry):
                for v in range(block // WIDEN):
                    at = n * block + v * WIDEN
                    part = table_buf[slot, pl.ds(at, WIDEN)].astype(jnp.float32).reshape(WIDEN // 2, 2, pairs, 128)
                    first, second = part[:, 0], part[:, 1]
                    upper = iota(first.shape, 1) < 4
                    where_to = pl.ds(pl.multiple_of(at * 4, 8), WIDEN * 4)
                    if 0 in groups:
                        merged = jnp.where(upper, first, pltpu.roll(second, 4, 1))
                        spread[0, where_to, :] = merged.reshape(WIDEN * 4, 128)
                    if 1 in groups:
                        merged = jnp.where(upper, pltpu.roll(first, 4, 1), second)
                        spread[1, where_to, :] = merged.reshape(WIDEN * 4, 128)
                return carry

            if not arriving:
                lax.fori_loop(0, 8, some, 0)
            each = 8 // max(len(arriving), 1)
            for n, copy in enumerate(arriving):
                copy.wait()
                lax.fori_loop(n * each, (n + 1) * each, some, 0)

        @pl.when(c > 0)
        def _():
            widen((0, 1))

        def halves(h, carry):
            @pl.when((c == 0) & (h == 0))
            def _():
                widen((0,), table_copies)
                start_fetch(1, 1)

            @pl.when(h == 0)
            def _():
                last_row[...] = table_buf[slot, M].astype(jnp.float32)

            @pl.when((c == 0) & (h == 1))
            def _():
                widen((1,))

            one_half(c, slot, h)
            return carry

        lax.fori_loop(0, 2, halves, 0)
        tables(c)
        return carry

    lax.fori_loop(0, chunks, one_chunk, 0)

    def turned(pieces, here):
        evens, odds = [], []
        c1, s1, c2, s2 = (coef[n, here, :] for n in range(4))
        for t in range(steps_here):
            data = jnp.concatenate([held[d, span, t * 128:(t + 1) * 128] for d, span in pieces], axis=0)
            other = pltpu.roll(data, 64, 1)
            evens.append(data * c1 + other * s1)
            odds.append(data * c2 + other * s2)
        return split(jnp.concatenate(evens, axis=1)), split(jnp.concatenate(odds, axis=1))

    def waves_at(g, coarse_of, fine_of):
        cosines, sines = [], []
        many = GROUP // FINE
        span = pl.ds(pl.multiple_of(g * many, many), many)
        cu, su = coarse_of(0, span), coarse_of(1, span)
        c2, s2 = fine_of
        for u in range(many):
            c1, s1 = cu[u:u + 1], su[u:u + 1]
            cosines.append(c1 * c2 - s1 * s2)
            sines.append(s1 * c2 + c1 * s2)
        return split(jnp.concatenate(cosines, axis=0)), split(jnp.concatenate(sines, axis=0))

    def span_of(c, h):
        return pl.ds(pl.multiple_of((2 * c + h) * CHUNK, CHUNK), CHUNK)

    regions = wide * REG_DEV
    blocks = half_lon // 8

    def region_tables():
        number = iota((regions, 128), 0)
        begin = jnp.zeros((regions, 128), jnp.int32)
        end = begin
        for n in range(lon // 128):
            ids = region_ref[n:n + 1, :]
            begin = begin + jnp.where(ids < number, 1, 0)
            end = end + jnp.where(ids <= number, 1, 0)
        reach = 64
        while reach:
            begin = begin + pltpu.roll(begin, reach, 1)
            end = end + pltpu.roll(end, reach, 1)
            reach //= 2
        lanes = iota((regions, 128), 1)
        for side in range(2):
            if side == 0:
                first, last = half_lon - jnp.minimum(end, half_lon), half_lon - jnp.minimum(begin, half_lon)
            else:
                first, last = jnp.maximum(begin, half_lon) - half_lon, jnp.maximum(end, half_lon) - half_lon
            here = first < last
            for n in range(half_lon // 128):
                hit = (lanes + n * 128 == first) & here
                pick[side, :, n * 128:(n + 1) * 128] = jnp.where(hit, 1.0, 0.0).astype(jnp.bfloat16)
            start = (first + 7) >> 3
            whole = start * 8 < last
            pick_blocks[side] = jnp.where((lanes == start) & whole, 1.0, 0.0).astype(jnp.bfloat16)
            absent[2 * side] = jnp.where(here, 0.0, -1e30)
            absent[2 * side + 1] = jnp.where(whole, 0.0, -1e30)
        across, down = iota((128, 128), 1), iota((128, 128), 0)
        mirror = jnp.where(across + down == 127, 1.0, 0.0).astype(jnp.bfloat16)
        ids = region_ref[...].astype(jnp.float32)
        flipped = dot(ids.astype(jnp.bfloat16), mirror)
        tiles = half_lon // 128
        sub = iota((16, 8, 128), 1)
        for side in range(2):
            for n in range(tiles):
                source = flipped[tiles - 1 - n:tiles - n] if side == 0 else ids[tiles + n:tiles + n + 1]
                column = jnp.transpose(jnp.broadcast_to(source, (128, 128)))
                span = pl.ds(side * half_lon + n * 128, 128)
                field[span, :] = column
                column = column.reshape(16, 8, 128)
                for i, step in enumerate((1, 2, 4)):
                    same = (pltpu.roll(column, 8 - step, 1) == column) & (sub + step < 8)
                    apart[i, span, :] = jnp.where(same, 0.0, -1e30).reshape(128, 128)
            starts = field[pl.ds(side * half_lon, blocks, stride=8), :]
            for i, step in enumerate((1, 2, 4)):
                same = (pltpu.roll(starts, blocks - step, 0) == starts) & (iota((blocks, 128), 0) + step < blocks)
                apart_blocks[side, i] = jnp.where(same, 0.0, -1e30)

    region_tables()

    def two_chunks(k, carry):
        first = 2 * k

        def arrive_when(when, piece):
            @pl.when(when)
            def _():
                arrive(*piece)

        for piece in PIECES:
            if piece[0] < chunks - 2:
                arrive_when(k == piece[0] // 2, piece)

        here = pl.ds(pl.multiple_of(first * 128, 256), 256)
        pieces = [(d, span_of(first + n, h)) for n in range(2) for h in range(2) for d in range(narrow)]
        (even_hi, even_lo), (odd_hi, odd_lo) = turned(pieces, here)
        fine_of = fine[0, :, here], fine[1, :, here]

        def one_group(g, carry):
            (cos_hi, cos_lo), (sin_hi, sin_lo) = waves_at(g, lambda n, span: coarse[n, span, here], fine_of)
            where_to = pl.ds(pl.multiple_of(g * GROUP, GROUP), GROUP)
            new_cos = dot(cos_hi, even_hi) + dot(cos_lo, even_hi) + dot(cos_hi, even_lo)
            new_sin = dot(sin_hi, odd_hi) + dot(sin_lo, odd_hi) + dot(sin_hi, odd_lo)

            @pl.when(k == 0)
            def _():
                part_cos[where_to, :] = new_cos
                part_sin[where_to, :] = new_sin

            @pl.when(k > 0)
            def _():
                part_cos[where_to, :] += new_cos
                part_sin[where_to, :] += new_sin

            return carry

        lax.fori_loop(0, half_lon // GROUP, one_group, 0)
        return carry

    lax.fori_loop(0, chunks // 2 - 1, two_chunks, 0)

    def angles_ahead(c, h):
        chunk_here = pl.ds(c * 128, 128)

        def doubled(values):
            kept = iota(values.shape, 1) < 64
            moved = pltpu.roll(values, 64, 1)
            return jnp.where(kept, values, moved) if h == 0 else jnp.where(kept, moved, values)

        fine_of = tuple(doubled(fine[n, :, chunk_here]) for n in range(2))
        low = iota((GROUP, 128), 1) < 64

        def one_group(g, carry):
            both = waves_at(g, lambda n, span: doubled(coarse[n, span, chunk_here]), fine_of)
            where_to = pl.ds(pl.multiple_of(g * GROUP, GROUP), GROUP)
            for n, (high, part) in enumerate(both):
                ready[h, n, where_to, :128] = jnp.where(low, high, part)
                ready[h, n, where_to, 128:] = high
            return carry

        lax.fori_loop(0, half_lon // GROUP, one_group, 0)

    def half_chunk(c, h, last):
        here = pl.ds((c * 2 + h) * 64, 64)
        (even_hi, even_lo), (odd_hi, odd_lo) = turned([(d, span_of(c, h)) for d in range(narrow)], here)
        even = jnp.concatenate([even_hi, even_hi, even_lo, jnp.zeros_like(even_lo)], axis=0)
        odd = jnp.concatenate([odd_hi, odd_hi, odd_lo, jnp.zeros_like(odd_lo)], axis=0)
        sign = jnp.where(iota((LAST, 128), 1) < 64, 1.0, -1.0)

        def one_group(g, carry):
            where_to = pl.ds(pl.multiple_of(g * LAST, LAST), LAST)
            new_cos = dot(ready[h, 0, where_to, :], even)
            new_sin = dot(ready[h, 1, where_to, :], odd)
            if not last:
                part_cos[where_to, :] += new_cos
                part_sin[where_to, :] += new_sin
                return carry
            most = [None, None]
            least = [None, None]
            for t in range(steps_here):
                lanes = slice(t * 128, (t + 1) * 128)
                even_part = part_cos[where_to, lanes] + new_cos[:, lanes]
                odd_part = part_sin[where_to, lanes] + new_sin[:, lanes]
                for side, full in enumerate((even_part + odd_part, even_part - odd_part)):
                    most[side] = full if t == 0 else jnp.maximum(most[side], full)
                    least[side] = full if t == 0 else jnp.minimum(least[side], full)
            for side in range(2):
                span = pl.ds(pl.multiple_of(side * half_lon + g * LAST, LAST), LAST)
                best = jnp.maximum(most[side], least[side] * sign)
                best = best.reshape(LAST // 8, 8, 128)
                for i, step in enumerate((1, 2, 4)):
                    best = jnp.maximum(
                        best, pltpu.roll(best, 8 - step, 1) + apart[i, span, :].reshape(LAST // 8, 8, 128)
                    )
                field[span, :] = best.reshape(LAST, 128)
            return carry

        lax.fori_loop(0, half_lon // LAST, one_group, 0)

    angles_ahead(chunks - 2, 0)
    angles_ahead(chunks - 2, 1)
    for piece in PIECES:
        if piece[0] == chunks - 2:
            arrive(*piece)
    half_chunk(chunks - 2, 0, False)
    half_chunk(chunks - 2, 1, False)
    angles_ahead(chunks - 1, 0)
    angles_ahead(chunks - 1, 1)
    arrive(chunks - 1, 0)
    half_chunk(chunks - 1, 0, False)
    arrive(chunks - 1, 1)
    half_chunk(chunks - 1, 1, True)

    def chosen(picks, values, missing):
        high, low = split(values)
        both = dot(picks, jnp.concatenate([high, low], axis=1))
        return both[:, :128] + both[:, 128:] + missing

    parts = []
    for side in range(2):
        starts = field[pl.ds(side * half_lon, blocks, stride=8), :]
        for i, step in enumerate((1, 2, 4)):
            starts = jnp.maximum(starts, pltpu.roll(starts, blocks - step, 0) + apart_blocks[side, i])
        parts.append(chosen(pick_blocks[side], starts, absent[2 * side + 1]))
        parts.append(chosen(pick[side], field[pl.ds(side * half_lon, half_lon), :], absent[2 * side]))
    peaks[...] = jnp.maximum(jnp.maximum(parts[0], parts[1]), jnp.maximum(parts[2], parts[3]))

    def exchange(ahead, arriving):
        other = lax.rem(me_wide + ahead, wide)
        return pltpu.make_async_remote_copy(
            src_ref=peaks.at[pl.ds(pl.multiple_of(other * REG_DEV, REG_DEV), REG_DEV)],
            dst_ref=peaks_in.at[other if arriving else me_wide],
            send_sem=wide_send.at[other], recv_sem=wide_recv.at[other if arriving else me_wide],
            device_id={"wide": other}, device_id_type=MESH,
        )

    for ahead in range(wide - 1, 0, -1):
        exchange(ahead, False).start()
    for ahead in range(1, narrow):
        for first, kind in PIECES:
            send(first, ahead, kind).wait_send()
    best = peaks[pl.ds(pl.multiple_of(me_wide * REG_DEV, REG_DEV), REG_DEV), :]
    for ahead in range(1, wide):
        exchange(ahead, True).wait_recv()
        best = jnp.maximum(best, peaks_in[lax.rem(me_wide + ahead, wide)])
    for n in range(2 * members):
        out_ref[n] = best[:, n * lat_here:(n + 1) * lat_here]

    for ahead in range(1, wide):
        exchange(ahead, False).wait_send()


def per_device(spectra, legendre, pair_of_slot, lat_owner, region_of_lon):
    members, steps_here, slot_count, _, length = spectra.shape
    lat = legendre.shape[2]
    narrow, wide = lax.axis_size("narrow"), lax.axis_size("wide")
    lat_here = lat // narrow
    lon = region_of_lon.shape[0]
    rows = members * steps_here * 2
    chunks = slot_count // CHUNK
    regions = REG_DEV * wide
    lanes = steps_here * 128
    dims = (narrow, wide, chunks, rows, members, steps_here, lat_here, lon)
    vmem = pl.BlockSpec(memory_space=pltpu.VMEM)
    hbm = pl.BlockSpec(memory_space=pl.ANY)
    best = pl.pallas_call(
        functools.partial(fields_kernel, dims),
        in_specs=[hbm] * 5,
        out_specs=vmem,
        out_shape=jax.ShapeDtypeStruct((2 * members, REG_DEV, lat_here), jnp.float32),
        scratch_shapes=[
            pltpu.SMEM((slot_count * narrow,), jnp.int32),
            pltpu.VMEM((1, lat), jnp.int32),
            pltpu.VMEM((lon // 128, 128), jnp.int32),
            pltpu.VMEM((2, length, CHUNK // 2, lat), jnp.bfloat16),
            pltpu.VMEM((2, members, steps_here, CHUNK, 2, length), jnp.bfloat16),
            pltpu.VMEM((HALF, rows, length), jnp.bfloat16),
            pltpu.VMEM((2, M * 4, 128), jnp.float32),
            pltpu.VMEM((CHUNK // 2, 128), jnp.float32),
            pltpu.VMEM((CHUNK * rows, 128), jnp.float32),
            pltpu.VMEM((2 * members * lat, narrow * 128), jnp.bfloat16),
            pltpu.VMEM((narrow, chunks * 2 * CHUNK, lanes), jnp.float32),
            pltpu.VMEM((narrow, chunks * 2 * CHUNK, lanes), jnp.float32),
            pltpu.VMEM((2, 2, lon // 2, 256), jnp.bfloat16),
            pltpu.VMEM((4, chunks * 128, 128), jnp.float32),
            pltpu.VMEM((2, FINE, chunks * 128), jnp.float32),
            pltpu.VMEM((2, FINE, chunks * 128), jnp.float32),
            pltpu.VMEM((lon // 2, lanes), jnp.float32),
            pltpu.VMEM((lon // 2, lanes), jnp.float32),
            pltpu.VMEM((lon, 128), jnp.float32),
            pltpu.VMEM((3, lon, 128), jnp.float32),
            pltpu.VMEM((2, 3, lon // 16, 128), jnp.float32),
            pltpu.VMEM((2, regions, lon // 2), jnp.bfloat16),
            pltpu.VMEM((2, regions, lon // 16), jnp.bfloat16),
            pltpu.VMEM((4, regions, 128), jnp.float32),
            pltpu.VMEM((regions, 128), jnp.float32),
            pltpu.VMEM((wide, REG_DEV, 128), jnp.float32),
            pltpu.SemaphoreType.DMA((1 + FETCHES, 2)),
            pltpu.SemaphoreType.DMA((3,)),
            pltpu.SemaphoreType.DMA((2, chunks, narrow)),
            pltpu.SemaphoreType.DMA((2, chunks, narrow)),
            pltpu.SemaphoreType.DMA((wide,)),
            pltpu.SemaphoreType.DMA((wide,)),
        ],
        compiler_params=pltpu.CompilerParams(
            collective_id=0, has_side_effects=True, vmem_limit_bytes=60 * 1024 * 1024
        ),
    )(
        pair_of_slot, lat_owner.reshape(1, lat), region_of_lon.reshape(-1, 128), spectra,
        jnp.transpose(legendre, (1, 0, 2)),
    )
    best = jnp.transpose(best, (0, 2, 1))
    return (best[:members], best[members:])


def solution(mesh):
    in_specs = (
        P(None, ("groups", "wide"), "narrow", None, None),
        P("narrow", None, None),
        P(),
        P(),
        P(),
    )
    out_specs = (P("groups", "narrow", "wide"), P("groups", "narrow", "wide"))

    def body(spectra, legendre, *rest):
        members, steps_here, slot_count = spectra.shape[:3]
        lat_here = legendre.shape[2] // mesh.shape["narrow"]
        packs = steps_here * lat_here == 128 and 2 * members * lat_here == 128
        packs = packs and slot_count % (2 * CHUNK) == 0 and slot_count >= 4 * CHUNK
        packs = packs and legendre.shape[2] == 128 and mesh.shape["narrow"] * CHUNK == 64
        packs = packs and rest[2].shape[0] == 2 * FINE * FINE
        chosen = per_device if packs else per_device_plain
        return chosen(spectra, legendre, *rest)

    return jax.shard_map(
        body, mesh=mesh, in_specs=in_specs, out_specs=out_specs, check_vma=False
    )
```

```python
import functools
import math

import jax
import jax.numpy as jnp
from jax import lax
from jax.experimental import pallas as pl
from jax.experimental.pallas import tpu as pltpu
from jax.sharding import PartitionSpec as P

M = 1280
LON = 2048
REG_DEV = 16
LON_FULL = 5120


def synthesize(operand, waves, start, width):
    columns = start + jnp.arange(width, dtype=jnp.int32)
    phase = waves[:, None] * columns[None, :] % LON_FULL
    angle = phase.astype(jnp.float32) * (2.0 * math.pi / LON_FULL)
    cosine = jnp.cos(angle)
    sine = jnp.sin(angle)
    rate = (waves.astype(jnp.float32) / M)[:, None]
    upper = jnp.concatenate([cosine, -rate * sine], axis=1)
    lower = jnp.concatenate([-sine, -rate * cosine], axis=1)
    table = jnp.concatenate([upper, lower], axis=0) * M ** (-0.5)
    return jnp.dot(operand, table, precision=lax.Precision.HIGHEST)


def synthesize_all(operand, waves):
    width = min(512, LON)
    starts = jnp.arange(LON // width, dtype=jnp.int32) * width

    def one_block(begin):
        return synthesize(operand, waves, begin, width)

    blocks = lax.map(one_block, starts)
    blocks = blocks.reshape(blocks.shape[0], blocks.shape[1], 2, width)
    value = jnp.transpose(blocks[:, :, 0], (1, 0, 2)).reshape(operand.shape[0], LON)
    slope = jnp.transpose(blocks[:, :, 1], (1, 0, 2)).reshape(operand.shape[0], LON)
    return (value, slope)


def region_peak(values, region_of_lon, wanted):
    hits = region_of_lon[:, None] == wanted[None, :]
    masked = jnp.where(hits[None, None], values[..., None], -1e30)
    return masked.max(axis=2)


def per_device_plain(spectra, legendre, pair_of_slot, lat_owner, region_of_lon):
    members = spectra.shape[0]
    steps_here = spectra.shape[1]
    slot_count = spectra.shape[2]
    length = spectra.shape[4]
    half_count = legendre.shape[0]
    lat_half = legendre.shape[2] // 2
    here = lax.axis_index("narrow")
    paired = lax.dynamic_slice_in_dim(pair_of_slot, here * slot_count, slot_count)
    position = jnp.arange(length, dtype=jnp.int32)[None, :]
    first_len = (M - paired)[:, None]
    leading = position < first_len
    offset = jnp.where(leading, position, position - first_len)
    even_term = offset % 2 == 0
    masks = jnp.stack(
        [leading & even_term, leading & ~even_term, ~leading & even_term, ~leading & ~even_term],
        axis=1,
    ).astype(jnp.bfloat16)
    ordered = jnp.transpose(spectra, (2, 0, 1, 3, 4))
    masked = masks[:, :, None, None, None, :] * ordered[:, None]
    masked = masked.reshape(half_count, 2, -1, length)
    table = legendre.reshape(half_count, length, 2, lat_half)
    sums = jnp.einsum("abrl,albj->abrj", masked, table, preferred_element_type=jnp.float32)
    sums = sums.reshape(slot_count, 4, members, steps_here, 2, lat_half)
    north_lead = sums[:, 0] + sums[:, 1]
    south_lead = sums[:, 0] - sums[:, 1]
    north_tail = sums[:, 2] + sums[:, 3]
    south_tail = sums[:, 2] - sums[:, 3]
    lead = jnp.concatenate([north_lead, jnp.flip(south_lead, axis=-1)], axis=-1)
    tail = jnp.concatenate([north_tail, jnp.flip(south_tail, axis=-1)], axis=-1)
    waved = jnp.stack([lead, tail], axis=1).reshape(2 * slot_count, members, steps_here, 2, -1)
    order = jnp.argsort(lat_owner, stable=True)
    waved = jnp.take(waved, order, axis=4)
    arrived = lax.all_to_all(waved, "narrow", split_axis=4, concat_axis=0, tiled=True)
    waves = jnp.stack([pair_of_slot, M - 1 - pair_of_slot], axis=1).reshape(-1)
    lat_here = arrived.shape[4]
    operand = jnp.transpose(arrived, (1, 2, 4, 3, 0)).reshape(members * steps_here * lat_here, -1)
    value, slope = synthesize_all(operand, waves)
    value = value.reshape(members, steps_here, lat_here, LON).max(axis=1)
    slope = jnp.abs(slope).reshape(members, steps_here, lat_here, LON).max(axis=1)
    wide_count = lax.axis_size("wide")
    mine_start = lax.axis_index("wide") * REG_DEV
    wanted = jnp.arange(REG_DEV * wide_count, dtype=jnp.int32)
    peaks = region_peak(value, region_of_lon, wanted)
    slopes = region_peak(slope, region_of_lon, wanted)
    peaks, slopes = lax.pmax((peaks, slopes), "wide")
    peak = lax.dynamic_slice_in_dim(peaks, mine_start, REG_DEV, 2)
    peak_slope = lax.dynamic_slice_in_dim(slopes, mine_start, REG_DEV, 2)
    return (peak, peak_slope)


CHUNK = 16
HALF = 8
FINE = 32
GROUP = 512
FETCHES = 4
LAST = 512
WIDEN = 32
MESH = pl.DeviceIdType.MESH


def split(values):
    high = values.astype(jnp.bfloat16)
    low = (values - high.astype(jnp.float32)).astype(jnp.bfloat16)
    return high, low


def dot(left, right):
    return jnp.dot(left, right, preferred_element_type=jnp.float32)


def turn(count):
    quarter = LON_FULL // 2
    whole = jnp.floor(count * (1.0 / quarter) + 0.5)
    angle = (count - whole * quarter) * (math.pi / LON_FULL)
    square = angle * angle
    sine = angle * (1.0 + square * (-1 / 6 + square * (1 / 120 + square * (-1 / 5040 + square * (1 / 362880)))))
    cosine = 1.0 + square * (
        -1 / 2 + square * (1 / 24 + square * (-1 / 720 + square * (1 / 40320 + square * (-1 / 3628800))))
    )
    turns = whole.astype(jnp.int32)
    swap = (turns & 1) == 1
    cos_sign = jnp.where(((turns + 1) & 2) == 2, -1.0, 1.0)
    sin_sign = jnp.where((turns & 2) == 2, -1.0, 1.0)
    return cos_sign * jnp.where(swap, sine, cosine), sin_sign * jnp.where(swap, cosine, sine)


def iota(shape, dim):
    return lax.broadcasted_iota(jnp.int32, shape, dim)


def pieces_of(chunks):
    pieces = [(0, 0), (0, 1), (1, 2)]
    pieces += [(c, 3) for c in range(2, chunks - 2, 2)]
    return pieces + [(chunks - 2, 2), (chunks - 1, 0), (chunks - 1, 1)]


def fields_kernel(
    dims, pair_hbm, owner_hbm, region_hbm, x_hbm, table_hbm, out_ref,
    pair_ref, owner_ref, region_ref,
    table_buf, x_buf, lined, spread, last_row, sums, place, sent, held, ready, coef, coarse, fine, part_cos, part_sin, field,
    apart, apart_blocks, pick, pick_blocks, absent, peaks, peaks_in,
    fetch_sem, small_sem, send_sem, recv_sem, wide_send, wide_recv,
):
    narrow, wide, chunks, rows, members, steps_here, lat_here, lon = dims
    me = lax.axis_index("narrow")
    me_wide = lax.axis_index("wide")
    slot_count = chunks * CHUNK
    pairs = CHUNK // 2
    half_lon = lon // 2
    lat = narrow * lat_here

    part = M // FETCHES
    parts_of = [pl.ds(n * part, part + (n == FETCHES - 1)) for n in range(FETCHES)]

    def fetches(c, slot):
        return (
            *(
                pltpu.make_async_copy(
                    table_hbm.at[span, pl.ds(pl.multiple_of(c * pairs, pairs), pairs), :], table_buf.at[slot, span],
                    fetch_sem.at[1 + n, slot],
                )
                for n, span in enumerate(parts_of)
            ),
            pltpu.make_async_copy(
                x_hbm.at[:, :, pl.ds(c * CHUNK, CHUNK), :, :], x_buf.at[slot], fetch_sem.at[0, slot]
            ),
        )

    PIECES = pieces_of(chunks)

    def start_fetch(c, slot):
        for copy in fetches(c, slot):
            copy.start()

    def partner(ahead):
        return lax.rem(me + ahead, narrow)

    order = (2, 1, 3) if narrow == 4 else tuple(range(1, narrow))

    def rows_of(c, kind):
        if kind < 2:
            return pl.ds(pl.multiple_of(c * 2 * CHUNK + kind * CHUNK, CHUNK), CHUNK), kind
        return pl.ds(pl.multiple_of(c * 2 * CHUNK, 2 * CHUNK), (kind - 1) * 2 * CHUNK), 0

    def send(c, target, kind):
        span, at = rows_of(c, kind)
        return pltpu.make_async_remote_copy(
            src_ref=sent.at[target, span], dst_ref=held.at[me, span],
            send_sem=send_sem.at[at, c, target], recv_sem=recv_sem.at[at, c, me],
            device_id={"narrow": target}, device_id_type=MESH,
        )

    def arrive(c, kind):
        for ahead in range(1, narrow):
            origin = partner(ahead)
            span, at = rows_of(c, kind)
            pltpu.make_async_remote_copy(
                src_ref=sent.at[origin, span], dst_ref=held.at[origin, span],
                send_sem=send_sem.at[at, c, origin], recv_sem=recv_sem.at[at, c, origin],
                device_id={"narrow": origin}, device_id_type=MESH,
            ).wait_recv()

    start_fetch(0, 0)
    small = [
        pltpu.make_async_copy(source, goal, small_sem.at[n])
        for n, (source, goal) in enumerate(
            ((owner_hbm, owner_ref), (pair_hbm, pair_ref), (region_hbm, region_ref))
        )
    ]
    for copy in small:
        copy.start()
    barrier = pltpu.get_barrier_semaphore()
    for ahead in range(1, narrow):
        pl.semaphore_signal(barrier, inc=1, device_id={"narrow": partner(ahead)}, device_id_type=MESH)
    for ahead in range(1, wide):
        pl.semaphore_signal(
            barrier, inc=1, device_id={"wide": lax.rem(me_wide + ahead, wide)}, device_id_type=MESH
        )

    for copy in small:
        copy.wait()

    lane = iota((lat, lat), 1)
    below = iota((lat, lat), 0)
    below = jnp.where(below < lat // 2, below, 3 * lat // 2 - 1 - below)
    owners = jnp.broadcast_to(owner_ref[...], (lat, lat)).astype(jnp.float32)
    owner = jnp.sum(jnp.where(lane == below, owners, 0.0), axis=1, keepdims=True)
    ahead_of = (owners < owner) | ((owners == owner) & (lane < below))
    rank = jnp.sum(jnp.where(ahead_of, 1.0, 0.0), axis=1, keepdims=True).astype(jnp.int32)
    column = iota((lat, narrow * 128), 1)
    goal = (column // 128) * lat_here + column % lat_here
    for n in range(2 * members):
        wanted = (goal == rank) & ((column // lat_here) % (2 * members) == n)
        place[n * lat:(n + 1) * lat, :] = jnp.where(wanted, 1.0, 0.0).astype(jnp.bfloat16)

    position = iota((1, M), 1)
    sign = (1 - 2 * (position & 1)).astype(jnp.float32).astype(jnp.bfloat16)
    half_lane = iota((rows, 128), 1)
    block = M // 8

    def one_pair(c, slot, h, u):
        at = h * (HALF // 2) + u
        parts = []
        extras = []
        for half in range(2):
            inside = 2 * at + half
            lines = 2 * u + half
            first_len = M - pair_ref[me * slot_count + c * CHUNK + inside]
            leading = (position < first_len).astype(jnp.float32).astype(jnp.bfloat16)
            flip = (1 - 2 * (first_len & 1)).astype(jnp.float32)
            for e in range(members):
                for t in range(steps_here):
                    row = 2 * (e * steps_here + t)
                    lined[lines, row:row + 2, :] = x_buf[slot, e, t, inside]
            body = lined[lines, :, :M]
            first_part = body * leading
            parts.extend((first_part, first_part * sign, body, body * sign))
            last = lined[lines, :, M:].astype(jnp.float32)
            extras.append((last, flip))
        table = spread[h, pl.ds(u, M, stride=4), :].astype(jnp.bfloat16)
        out = dot(jnp.concatenate(parts, axis=0), table)
        edge = last_row[pl.ds(at, 1), :]
        for half in range(2):
            base = half * 4 * rows
            piece = [out[base + v * rows:base + (v + 1) * rows] for v in range(4)]
            last, flip = extras[half]
            term = last * edge
            piece[2] = piece[2] - piece[0] + term
            piece[3] = (piece[3] - piece[1] + term) * flip
            for tail_at in range(2):
                north, south = piece[2 * tail_at], piece[2 * tail_at + 1]
                if half == 0:
                    both = jnp.where(half_lane < 64, north, pltpu.roll(south, 64, 1))
                else:
                    both = jnp.where(half_lane < 64, pltpu.roll(north, 64, 1), south)
                at_row = (tail_at * HALF + 2 * u + half) * rows
                sums[at_row:at_row + rows, :] = both

    def one_half(c, slot, h):
        for u in range(HALF // 2):
            one_pair(c, slot, h, u)
        highs, lows = [], []
        for t in range(steps_here):
            wide_rows = jnp.concatenate(
                [
                    sums[pl.ds((e * steps_here + t) * 2 + part, CHUNK, stride=rows), :]
                    for part in range(2) for e in range(members)
                ],
                axis=1,
            )
            high, low = split(wide_rows)
            highs.append(high)
            lows.append(low)
        both = dot(jnp.concatenate(highs + lows, axis=0), place[...])
        moved = both[:steps_here * CHUNK] + both[steps_here * CHUNK:]
        where_to = pl.ds(pl.multiple_of((2 * c + h) * CHUNK, CHUNK), CHUNK)
        for t in range(steps_here):
            for d in range(narrow):
                sent[d, where_to, t * 128:(t + 1) * 128] = (
                    moved[t * CHUNK:(t + 1) * CHUNK, d * 128:(d + 1) * 128]
                )
        held[me, where_to, :] = sent[me, where_to, :]

        @pl.when((c == 0) & (h == 0))
        def _():
            pl.semaphore_wait(barrier, narrow - 1 + wide - 1)

        def sends(group, targets):
            for target in targets:
                @pl.when(me != target)
                def _():
                    for first, kind in group:
                        send(first, target, kind).start()

        for piece in PIECES:
            first, kind = piece
            after = first + (kind == 3)
            done = (c == first) & (h == 0) if kind == 0 else (c == after) & (h == 1)

            @pl.when(done)
            def _():
                if first >= chunks - 2:
                    sends([piece], range(0, narrow, 2))
                else:
                    for ahead in order:
                        send(first, partner(ahead), kind).start()

        @pl.when((c == chunks - 1) & (h == 1))
        def _():
            sends([piece for piece in PIECES if piece[0] >= chunks - 2], range(1, narrow, 2))

    def tables(c):
        lanes = iota((8, 128), 1)
        base = lanes & ~HALF
        lead = jnp.zeros((8, 128), jnp.int32)
        for h in range(2):
            for d in range(narrow):
                for s in range(HALF):
                    at = (h * narrow + d) * CHUNK + s
                    lead = jnp.where(base == at, pair_ref[d * slot_count + c * CHUNK + h * HALF + s], lead)
        wave = jnp.where((lanes & HALF) == HALF, M - 1 - lead, lead).astype(jnp.float32)
        here = pl.ds(pl.multiple_of(c * 128, 128), 128)
        rows_of = jnp.broadcast_to(wave[:1], (FINE, 128))
        index = iota((FINE, 128), 0).astype(jnp.float32)
        cosine, sine = turn(rows_of * (index * (2.0 * FINE)))
        coarse[0, :, here] = cosine
        coarse[1, :, here] = sine
        cosine, sine = turn(rows_of * (index * 2.0 + 1.0))
        fine[0, :, here] = cosine
        fine[1, :, here] = sine
        down = jnp.transpose(jnp.broadcast_to(wave[:1], (128, 128)))
        cosine, sine = turn(down * (lon - 1.0))
        low = iota((128, 128), 1) < 64
        cosine = cosine * (M ** -0.5)
        sine = sine * (M ** -0.5)
        rate = down * (1.0 / M)
        coef[0, here, :] = cosine * jnp.where(low, 1.0, -rate)
        coef[1, here, :] = sine * jnp.where(low, -1.0, -rate)
        coef[2, here, :] = sine * jnp.where(low, 1.0, -rate)
        coef[3, here, :] = cosine * jnp.where(low, 1.0, rate)

    def one_chunk(c, carry):
        slot = lax.rem(c, 2)
        x_copy, *table_copies = reversed(fetches(c, slot))
        x_copy.wait()
        table_copies = table_copies[::-1]

        @pl.when(c > 0)
        def _():
            for copy in table_copies:
                copy.wait()

            @pl.when(c + 1 < chunks)
            def _():
                start_fetch(c + 1, 1 - slot)

        def widen(groups, arriving=()):
            def some(n, carry):
                for v in range(block // WIDEN):
                    at = n * block + v * WIDEN
                    part = table_buf[slot, pl.ds(at, WIDEN)].astype(jnp.float32).reshape(WIDEN // 2, 2, pairs, 128)
                    first, second = part[:, 0], part[:, 1]
                    upper = iota(first.shape, 1) < 4
                    where_to = pl.ds(pl.multiple_of(at * 4, 8), WIDEN * 4)
                    if 0 in groups:
                        merged = jnp.where(upper, first, pltpu.roll(second, 4, 1))
                        spread[0, where_to, :] = merged.reshape(WIDEN * 4, 128)
                    if 1 in groups:
                        merged = jnp.where(upper, pltpu.roll(first, 4, 1), second)
                        spread[1, where_to, :] = merged.reshape(WIDEN * 4, 128)
                return carry

            if not arriving:
                lax.fori_loop(0, 8, some, 0)
            each = 8 // max(len(arriving), 1)
            for n, copy in enumerate(arriving):
                copy.wait()
                lax.fori_loop(n * each, (n + 1) * each, some, 0)

        @pl.when(c > 0)
        def _():
            widen((0, 1))

        def halves(h, carry):
            @pl.when((c == 0) & (h == 0))
            def _():
                widen((0,), table_copies)
                start_fetch(1, 1)

            @pl.when(h == 0)
            def _():
                last_row[...] = table_buf[slot, M].astype(jnp.float32)

            @pl.when((c == 0) & (h == 1))
            def _():
                widen((1,))

            one_half(c, slot, h)
            return carry

        lax.fori_loop(0, 2, halves, 0)
        tables(c)
        return carry

    lax.fori_loop(0, chunks, one_chunk, 0)

    def turned(pieces, here):
        evens, odds = [], []
        c1, s1, c2, s2 = (coef[n, here, :] for n in range(4))
        for t in range(steps_here):
            data = jnp.concatenate([held[d, span, t * 128:(t + 1) * 128] for d, span in pieces], axis=0)
            other = pltpu.roll(data, 64, 1)
            evens.append(data * c1 + other * s1)
            odds.append(data * c2 + other * s2)
        return split(jnp.concatenate(evens, axis=1)), split(jnp.concatenate(odds, axis=1))

    def waves_at(g, coarse_of, fine_of):
        cosines, sines = [], []
        many = GROUP // FINE
        span = pl.ds(pl.multiple_of(g * many, many), many)
        cu, su = coarse_of(0, span), coarse_of(1, span)
        c2, s2 = fine_of
        for u in range(many):
            c1, s1 = cu[u:u + 1], su[u:u + 1]
            cosines.append(c1 * c2 - s1 * s2)
            sines.append(s1 * c2 + c1 * s2)
        return split(jnp.concatenate(cosines, axis=0)), split(jnp.concatenate(sines, axis=0))

    def span_of(c, h):
        return pl.ds(pl.multiple_of((2 * c + h) * CHUNK, CHUNK), CHUNK)

    regions = wide * REG_DEV
    blocks = half_lon // 8

    def region_tables():
        number = iota((regions, 128), 0)
        begin = jnp.zeros((regions, 128), jnp.int32)
        end = begin
        for n in range(lon // 128):
            ids = region_ref[n:n + 1, :]
            begin = begin + jnp.where(ids < number, 1, 0)
            end = end + jnp.where(ids <= number, 1, 0)
        reach = 64
        while reach:
            begin = begin + pltpu.roll(begin, reach, 1)
            end = end + pltpu.roll(end, reach, 1)
            reach //= 2
        lanes = iota((regions, 128), 1)
        for side in range(2):
            if side == 0:
                first, last = half_lon - jnp.minimum(end, half_lon), half_lon - jnp.minimum(begin, half_lon)
            else:
                first, last = jnp.maximum(begin, half_lon) - half_lon, jnp.maximum(end, half_lon) - half_lon
            here = first < last
            for n in range(half_lon // 128):
                hit = (lanes + n * 128 == first) & here
                pick[side, :, n * 128:(n + 1) * 128] = jnp.where(hit, 1.0, 0.0).astype(jnp.bfloat16)
            start = (first + 7) >> 3
            whole = start * 8 < last
            pick_blocks[side] = jnp.where((lanes == start) & whole, 1.0, 0.0).astype(jnp.bfloat16)
            absent[2 * side] = jnp.where(here, 0.0, -1e30)
            absent[2 * side + 1] = jnp.where(whole, 0.0, -1e30)
        across, down = iota((128, 128), 1), iota((128, 128), 0)
        mirror = jnp.where(across + down == 127, 1.0, 0.0).astype(jnp.bfloat16)
        ids = region_ref[...].astype(jnp.float32)
        flipped = dot(ids.astype(jnp.bfloat16), mirror)
        tiles = half_lon // 128
        sub = iota((16, 8, 128), 1)
        for side in range(2):
            for n in range(tiles):
                source = flipped[tiles - 1 - n:tiles - n] if side == 0 else ids[tiles + n:tiles + n + 1]
                column = jnp.transpose(jnp.broadcast_to(source, (128, 128)))
                span = pl.ds(side * half_lon + n * 128, 128)
                field[span, :] = column
                column = column.reshape(16, 8, 128)
                for i, step in enumerate((1, 2, 4)):
                    same = (pltpu.roll(column, 8 - step, 1) == column) & (sub + step < 8)
                    apart[i, span, :] = jnp.where(same, 0.0, -1e30).reshape(128, 128)
            starts = field[pl.ds(side * half_lon, blocks, stride=8), :]
            for i, step in enumerate((1, 2, 4)):
                same = (pltpu.roll(starts, blocks - step, 0) == starts) & (iota((blocks, 128), 0) + step < blocks)
                apart_blocks[side, i] = jnp.where(same, 0.0, -1e30)

    region_tables()

    def two_chunks(k, carry):
        first = 2 * k

        def arrive_when(when, piece):
            @pl.when(when)
            def _():
                arrive(*piece)

        for piece in PIECES:
            if piece[0] < chunks - 2:
                arrive_when(k == piece[0] // 2, piece)

        here = pl.ds(pl.multiple_of(first * 128, 256), 256)
        pieces = [(d, span_of(first + n, h)) for n in range(2) for h in range(2) for d in range(narrow)]
        (even_hi, even_lo), (odd_hi, odd_lo) = turned(pieces, here)
        fine_of = fine[0, :, here], fine[1, :, here]

        def one_group(g, carry):
            (cos_hi, cos_lo), (sin_hi, sin_lo) = waves_at(g, lambda n, span: coarse[n, span, here], fine_of)
            where_to = pl.ds(pl.multiple_of(g * GROUP, GROUP), GROUP)
            new_cos = dot(cos_hi, even_hi) + dot(cos_lo, even_hi) + dot(cos_hi, even_lo)
            new_sin = dot(sin_hi, odd_hi) + dot(sin_lo, odd_hi) + dot(sin_hi, odd_lo)

            @pl.when(k == 0)
            def _():
                part_cos[where_to, :] = new_cos
                part_sin[where_to, :] = new_sin

            @pl.when(k > 0)
            def _():
                part_cos[where_to, :] += new_cos
                part_sin[where_to, :] += new_sin

            return carry

        lax.fori_loop(0, half_lon // GROUP, one_group, 0)
        return carry

    lax.fori_loop(0, chunks // 2 - 1, two_chunks, 0)

    def angles_ahead(c, h):
        chunk_here = pl.ds(c * 128, 128)

        def doubled(values):
            kept = iota(values.shape, 1) < 64
            moved = pltpu.roll(values, 64, 1)
            return jnp.where(kept, values, moved) if h == 0 else jnp.where(kept, moved, values)

        fine_of = tuple(doubled(fine[n, :, chunk_here]) for n in range(2))
        low = iota((GROUP, 128), 1) < 64

        def one_group(g, carry):
            both = waves_at(g, lambda n, span: doubled(coarse[n, span, chunk_here]), fine_of)
            where_to = pl.ds(pl.multiple_of(g * GROUP, GROUP), GROUP)
            for n, (high, part) in enumerate(both):
                ready[c % 2, h, n, where_to, :128] = jnp.where(low, high, part)
                ready[c % 2, h, n, where_to, 128:] = high
            return carry

        lax.fori_loop(0, half_lon // GROUP, one_group, 0)

    def half_chunk(c, h, last):
        here = pl.ds((c * 2 + h) * 64, 64)
        (even_hi, even_lo), (odd_hi, odd_lo) = turned([(d, span_of(c, h)) for d in range(narrow)], here)
        even = jnp.concatenate([even_hi, even_hi, even_lo, jnp.zeros_like(even_lo)], axis=0)
        odd = jnp.concatenate([odd_hi, odd_hi, odd_lo, jnp.zeros_like(odd_lo)], axis=0)
        sign = jnp.where(iota((LAST, 128), 1) < 64, 1.0, -1.0)

        def one_group(g, carry):
            where_to = pl.ds(pl.multiple_of(g * LAST, LAST), LAST)
            new_cos = dot(ready[c % 2, h, 0, where_to, :], even)
            new_sin = dot(ready[c % 2, h, 1, where_to, :], odd)
            if not last:
                part_cos[where_to, :] += new_cos
                part_sin[where_to, :] += new_sin
                return carry
            most = [None, None]
            least = [None, None]
            for t in range(steps_here):
                lanes = slice(t * 128, (t + 1) * 128)
                even_part = part_cos[where_to, lanes] + new_cos[:, lanes]
                odd_part = part_sin[where_to, lanes] + new_sin[:, lanes]
                for side, full in enumerate((even_part + odd_part, even_part - odd_part)):
                    most[side] = full if t == 0 else jnp.maximum(most[side], full)
                    least[side] = full if t == 0 else jnp.minimum(least[side], full)
            for side in range(2):
                span = pl.ds(pl.multiple_of(side * half_lon + g * LAST, LAST), LAST)
                best = jnp.maximum(most[side], least[side] * sign)
                best = best.reshape(LAST // 8, 8, 128)
                for i, step in enumerate((1, 2, 4)):
                    best = jnp.maximum(
                        best, pltpu.roll(best, 8 - step, 1) + apart[i, span, :].reshape(LAST // 8, 8, 128)
                    )
                field[span, :] = best.reshape(LAST, 128)
            return carry

        lax.fori_loop(0, half_lon // LAST, one_group, 0)

    angles_ahead(chunks - 2, 0)
    angles_ahead(chunks - 2, 1)
    angles_ahead(chunks - 1, 0)
    angles_ahead(chunks - 1, 1)
    for piece in PIECES:
        if piece[0] == chunks - 2:
            arrive(*piece)
    half_chunk(chunks - 2, 0, False)
    half_chunk(chunks - 2, 1, False)
    arrive(chunks - 1, 0)
    half_chunk(chunks - 1, 0, False)
    arrive(chunks - 1, 1)
    half_chunk(chunks - 1, 1, True)

    def chosen(picks, values, missing):
        high, low = split(values)
        both = dot(picks, jnp.concatenate([high, low], axis=1))
        return both[:, :128] + both[:, 128:] + missing

    parts = []
    for side in range(2):
        starts = field[pl.ds(side * half_lon, blocks, stride=8), :]
        for i, step in enumerate((1, 2, 4)):
            starts = jnp.maximum(starts, pltpu.roll(starts, blocks - step, 0) + apart_blocks[side, i])
        parts.append(chosen(pick_blocks[side], starts, absent[2 * side + 1]))
        parts.append(chosen(pick[side], field[pl.ds(side * half_lon, half_lon), :], absent[2 * side]))
    peaks[...] = jnp.maximum(jnp.maximum(parts[0], parts[1]), jnp.maximum(parts[2], parts[3]))

    def exchange(ahead, arriving):
        other = lax.rem(me_wide + ahead, wide)
        return pltpu.make_async_remote_copy(
            src_ref=peaks.at[pl.ds(pl.multiple_of(other * REG_DEV, REG_DEV), REG_DEV)],
            dst_ref=peaks_in.at[other if arriving else me_wide],
            send_sem=wide_send.at[other], recv_sem=wide_recv.at[other if arriving else me_wide],
            device_id={"wide": other}, device_id_type=MESH,
        )

    for ahead in range(wide - 1, 0, -1):
        exchange(ahead, False).start()
    for ahead in range(1, narrow):
        for first, kind in PIECES:
            send(first, partner(ahead), kind).wait_send()
    best = peaks[pl.ds(pl.multiple_of(me_wide * REG_DEV, REG_DEV), REG_DEV), :]
    for ahead in range(1, wide):
        exchange(ahead, True).wait_recv()
        best = jnp.maximum(best, peaks_in[lax.rem(me_wide + ahead, wide)])
    for n in range(2 * members):
        out_ref[n] = best[:, n * lat_here:(n + 1) * lat_here]

    for ahead in range(1, wide):
        exchange(ahead, False).wait_send()


def per_device(spectra, legendre, pair_of_slot, lat_owner, region_of_lon):
    members, steps_here, slot_count, _, length = spectra.shape
    lat = legendre.shape[2]
    narrow, wide = lax.axis_size("narrow"), lax.axis_size("wide")
    lat_here = lat // narrow
    lon = region_of_lon.shape[0]
    rows = members * steps_here * 2
    chunks = slot_count // CHUNK
    regions = REG_DEV * wide
    lanes = steps_here * 128
    dims = (narrow, wide, chunks, rows, members, steps_here, lat_here, lon)
    vmem = pl.BlockSpec(memory_space=pltpu.VMEM)
    hbm = pl.BlockSpec(memory_space=pl.ANY)
    best = pl.pallas_call(
        functools.partial(fields_kernel, dims),
        in_specs=[hbm] * 5,
        out_specs=vmem,
        out_shape=jax.ShapeDtypeStruct((2 * members, REG_DEV, lat_here), jnp.float32),
        scratch_shapes=[
            pltpu.SMEM((slot_count * narrow,), jnp.int32),
            pltpu.VMEM((1, lat), jnp.int32),
            pltpu.VMEM((lon // 128, 128), jnp.int32),
            pltpu.VMEM((2, length, CHUNK // 2, lat), jnp.bfloat16),
            pltpu.VMEM((2, members, steps_here, CHUNK, 2, length), jnp.bfloat16),
            pltpu.VMEM((HALF, rows, length), jnp.bfloat16),
            pltpu.VMEM((2, M * 4, 128), jnp.float32),
            pltpu.VMEM((CHUNK // 2, 128), jnp.float32),
            pltpu.VMEM((CHUNK * rows, 128), jnp.float32),
            pltpu.VMEM((2 * members * lat, narrow * 128), jnp.bfloat16),
            pltpu.VMEM((narrow, chunks * 2 * CHUNK, lanes), jnp.float32),
            pltpu.VMEM((narrow, chunks * 2 * CHUNK, lanes), jnp.float32),
            pltpu.VMEM((2, 2, 2, lon // 2, 256), jnp.bfloat16),
            pltpu.VMEM((4, chunks * 128, 128), jnp.float32),
            pltpu.VMEM((2, FINE, chunks * 128), jnp.float32),
            pltpu.VMEM((2, FINE, chunks * 128), jnp.float32),
            pltpu.VMEM((lon // 2, lanes), jnp.float32),
            pltpu.VMEM((lon // 2, lanes), jnp.float32),
            pltpu.VMEM((lon, 128), jnp.float32),
            pltpu.VMEM((3, lon, 128), jnp.float32),
            pltpu.VMEM((2, 3, lon // 16, 128), jnp.float32),
            pltpu.VMEM((2, regions, lon // 2), jnp.bfloat16),
            pltpu.VMEM((2, regions, lon // 16), jnp.bfloat16),
            pltpu.VMEM((4, regions, 128), jnp.float32),
            pltpu.VMEM((regions, 128), jnp.float32),
            pltpu.VMEM((wide, REG_DEV, 128), jnp.float32),
            pltpu.SemaphoreType.DMA((1 + FETCHES, 2)),
            pltpu.SemaphoreType.DMA((3,)),
            pltpu.SemaphoreType.DMA((2, chunks, narrow)),
            pltpu.SemaphoreType.DMA((2, chunks, narrow)),
            pltpu.SemaphoreType.DMA((wide,)),
            pltpu.SemaphoreType.DMA((wide,)),
        ],
        compiler_params=pltpu.CompilerParams(
            collective_id=0, has_side_effects=True, vmem_limit_bytes=60 * 1024 * 1024
        ),
    )(
        pair_of_slot, lat_owner.reshape(1, lat), region_of_lon.reshape(-1, 128), spectra,
        jnp.transpose(legendre, (1, 0, 2)),
    )
    best = jnp.transpose(best, (0, 2, 1))
    return (best[:members], best[members:])


def solution(mesh):
    in_specs = (
        P(None, ("groups", "wide"), "narrow", None, None),
        P("narrow", None, None),
        P(),
        P(),
        P(),
    )
    out_specs = (P("groups", "narrow", "wide"), P("groups", "narrow", "wide"))

    def body(spectra, legendre, *rest):
        members, steps_here, slot_count = spectra.shape[:3]
        lat_here = legendre.shape[2] // mesh.shape["narrow"]
        packs = steps_here * lat_here == 128 and 2 * members * lat_here == 128
        packs = packs and slot_count % (2 * CHUNK) == 0 and slot_count >= 4 * CHUNK
        packs = packs and legendre.shape[2] == 128 and mesh.shape["narrow"] * CHUNK == 64
        packs = packs and rest[2].shape[0] == 2 * FINE * FINE
        chosen = per_device if packs else per_device_plain
        return chosen(spectra, legendre, *rest)

    return jax.shard_map(
        body, mesh=mesh, in_specs=in_specs, out_specs=out_specs, check_vma=False
    )
```

```python
import functools
import math

import jax
import jax.numpy as jnp
from jax import lax
from jax.experimental import pallas as pl
from jax.experimental.pallas import tpu as pltpu
from jax.sharding import PartitionSpec as P

M = 1280
LON = 2048
REG_DEV = 16
LON_FULL = 5120


def synthesize(operand, waves, start, width):
    columns = start + jnp.arange(width, dtype=jnp.int32)
    phase = waves[:, None] * columns[None, :] % LON_FULL
    angle = phase.astype(jnp.float32) * (2.0 * math.pi / LON_FULL)
    cosine = jnp.cos(angle)
    sine = jnp.sin(angle)
    rate = (waves.astype(jnp.float32) / M)[:, None]
    upper = jnp.concatenate([cosine, -rate * sine], axis=1)
    lower = jnp.concatenate([-sine, -rate * cosine], axis=1)
    table = jnp.concatenate([upper, lower], axis=0) * M ** (-0.5)
    return jnp.dot(operand, table, precision=lax.Precision.HIGHEST)


def synthesize_all(operand, waves):
    width = min(512, LON)
    starts = jnp.arange(LON // width, dtype=jnp.int32) * width

    def one_block(begin):
        return synthesize(operand, waves, begin, width)

    blocks = lax.map(one_block, starts)
    blocks = blocks.reshape(blocks.shape[0], blocks.shape[1], 2, width)
    value = jnp.transpose(blocks[:, :, 0], (1, 0, 2)).reshape(operand.shape[0], LON)
    slope = jnp.transpose(blocks[:, :, 1], (1, 0, 2)).reshape(operand.shape[0], LON)
    return (value, slope)


def region_peak(values, region_of_lon, wanted):
    hits = region_of_lon[:, None] == wanted[None, :]
    masked = jnp.where(hits[None, None], values[..., None], -1e30)
    return masked.max(axis=2)


def per_device_plain(spectra, legendre, pair_of_slot, lat_owner, region_of_lon):
    members = spectra.shape[0]
    steps_here = spectra.shape[1]
    slot_count = spectra.shape[2]
    length = spectra.shape[4]
    half_count = legendre.shape[0]
    lat_half = legendre.shape[2] // 2
    here = lax.axis_index("narrow")
    paired = lax.dynamic_slice_in_dim(pair_of_slot, here * slot_count, slot_count)
    position = jnp.arange(length, dtype=jnp.int32)[None, :]
    first_len = (M - paired)[:, None]
    leading = position < first_len
    offset = jnp.where(leading, position, position - first_len)
    even_term = offset % 2 == 0
    masks = jnp.stack(
        [leading & even_term, leading & ~even_term, ~leading & even_term, ~leading & ~even_term],
        axis=1,
    ).astype(jnp.bfloat16)
    ordered = jnp.transpose(spectra, (2, 0, 1, 3, 4))
    masked = masks[:, :, None, None, None, :] * ordered[:, None]
    masked = masked.reshape(half_count, 2, -1, length)
    table = legendre.reshape(half_count, length, 2, lat_half)
    sums = jnp.einsum("abrl,albj->abrj", masked, table, preferred_element_type=jnp.float32)
    sums = sums.reshape(slot_count, 4, members, steps_here, 2, lat_half)
    north_lead = sums[:, 0] + sums[:, 1]
    south_lead = sums[:, 0] - sums[:, 1]
    north_tail = sums[:, 2] + sums[:, 3]
    south_tail = sums[:, 2] - sums[:, 3]
    lead = jnp.concatenate([north_lead, jnp.flip(south_lead, axis=-1)], axis=-1)
    tail = jnp.concatenate([north_tail, jnp.flip(south_tail, axis=-1)], axis=-1)
    waved = jnp.stack([lead, tail], axis=1).reshape(2 * slot_count, members, steps_here, 2, -1)
    order = jnp.argsort(lat_owner, stable=True)
    waved = jnp.take(waved, order, axis=4)
    arrived = lax.all_to_all(waved, "narrow", split_axis=4, concat_axis=0, tiled=True)
    waves = jnp.stack([pair_of_slot, M - 1 - pair_of_slot], axis=1).reshape(-1)
    lat_here = arrived.shape[4]
    operand = jnp.transpose(arrived, (1, 2, 4, 3, 0)).reshape(members * steps_here * lat_here, -1)
    value, slope = synthesize_all(operand, waves)
    value = value.reshape(members, steps_here, lat_here, LON).max(axis=1)
    slope = jnp.abs(slope).reshape(members, steps_here, lat_here, LON).max(axis=1)
    wide_count = lax.axis_size("wide")
    mine_start = lax.axis_index("wide") * REG_DEV
    wanted = jnp.arange(REG_DEV * wide_count, dtype=jnp.int32)
    peaks = region_peak(value, region_of_lon, wanted)
    slopes = region_peak(slope, region_of_lon, wanted)
    peaks, slopes = lax.pmax((peaks, slopes), "wide")
    peak = lax.dynamic_slice_in_dim(peaks, mine_start, REG_DEV, 2)
    peak_slope = lax.dynamic_slice_in_dim(slopes, mine_start, REG_DEV, 2)
    return (peak, peak_slope)


CHUNK = 16
HALF = 8
FINE = 32
GROUP = 1024
FETCHES = 4
LAST = 1024
WIDEN = 32
MESH = pl.DeviceIdType.MESH


def split(values):
    high = values.astype(jnp.bfloat16)
    low = (values - high.astype(jnp.float32)).astype(jnp.bfloat16)
    return high, low


def dot(left, right):
    return jnp.dot(left, right, preferred_element_type=jnp.float32)


def turn(count):
    quarter = LON_FULL // 2
    whole = jnp.floor(count * (1.0 / quarter) + 0.5)
    angle = (count - whole * quarter) * (math.pi / LON_FULL)
    square = angle * angle
    sine = angle * (1.0 + square * (-1 / 6 + square * (1 / 120 + square * (-1 / 5040 + square * (1 / 362880)))))
    cosine = 1.0 + square * (
        -1 / 2 + square * (1 / 24 + square * (-1 / 720 + square * (1 / 40320 + square * (-1 / 3628800))))
    )
    turns = whole.astype(jnp.int32)
    swap = (turns & 1) == 1
    cos_sign = jnp.where(((turns + 1) & 2) == 2, -1.0, 1.0)
    sin_sign = jnp.where((turns & 2) == 2, -1.0, 1.0)
    return cos_sign * jnp.where(swap, sine, cosine), sin_sign * jnp.where(swap, cosine, sine)


def iota(shape, dim):
    return lax.broadcasted_iota(jnp.int32, shape, dim)


def pieces_of(chunks):
    pieces = [(0, 0), (0, 1), (1, 2)]
    pieces += [(c, 3) for c in range(2, chunks - 2, 2)]
    return pieces + [(chunks - 2, 2), (chunks - 1, 0), (chunks - 1, 1)]


def fields_kernel(
    dims, pair_hbm, owner_hbm, region_hbm, x_hbm, table_hbm, out_ref,
    pair_ref, owner_ref, region_ref,
    table_buf, x_buf, lined, spread, last_row, sums, place, sent, held, ready, coef, coarse, fine, part_cos, part_sin, field,
    apart, apart_blocks, pick, pick_blocks, absent, peaks, peaks_in,
    fetch_sem, small_sem, send_sem, recv_sem, wide_send, wide_recv,
):
    narrow, wide, chunks, rows, members, steps_here, lat_here, lon = dims
    me = lax.axis_index("narrow")
    me_wide = lax.axis_index("wide")
    slot_count = chunks * CHUNK
    pairs = CHUNK // 2
    half_lon = lon // 2
    lat = narrow * lat_here

    part = M // FETCHES
    parts_of = [pl.ds(n * part, part + (n == FETCHES - 1)) for n in range(FETCHES)]

    def fetches(c, slot):
        return (
            *(
                pltpu.make_async_copy(
                    table_hbm.at[span, pl.ds(pl.multiple_of(c * pairs, pairs), pairs), :], table_buf.at[slot, span],
                    fetch_sem.at[1 + n, slot],
                )
                for n, span in enumerate(parts_of)
            ),
            pltpu.make_async_copy(
                x_hbm.at[:, :, pl.ds(c * CHUNK, CHUNK), :, :], x_buf.at[slot], fetch_sem.at[0, slot]
            ),
        )

    PIECES = pieces_of(chunks)

    def start_fetch(c, slot):
        for copy in fetches(c, slot):
            copy.start()

    def partner(ahead):
        return lax.rem(me + ahead, narrow)

    order = (2, 1, 3) if narrow == 4 else tuple(range(1, narrow))

    def rows_of(c, kind):
        if kind < 2:
            return pl.ds(pl.multiple_of(c * 2 * CHUNK + kind * CHUNK, CHUNK), CHUNK), kind
        return pl.ds(pl.multiple_of(c * 2 * CHUNK, 2 * CHUNK), (kind - 1) * 2 * CHUNK), 0

    def send(c, target, kind):
        span, at = rows_of(c, kind)
        return pltpu.make_async_remote_copy(
            src_ref=sent.at[target, span], dst_ref=held.at[me, span],
            send_sem=send_sem.at[at, c, target], recv_sem=recv_sem.at[at, c, me],
            device_id={"narrow": target}, device_id_type=MESH,
        )

    def arrive(c, kind):
        for ahead in range(1, narrow):
            origin = partner(ahead)
            span, at = rows_of(c, kind)
            pltpu.make_async_remote_copy(
                src_ref=sent.at[origin, span], dst_ref=held.at[origin, span],
                send_sem=send_sem.at[at, c, origin], recv_sem=recv_sem.at[at, c, origin],
                device_id={"narrow": origin}, device_id_type=MESH,
            ).wait_recv()

    start_fetch(0, 0)
    small = [
        pltpu.make_async_copy(source, goal, small_sem.at[n])
        for n, (source, goal) in enumerate(
            ((owner_hbm, owner_ref), (pair_hbm, pair_ref), (region_hbm, region_ref))
        )
    ]
    for copy in small:
        copy.start()
    barrier = pltpu.get_barrier_semaphore()
    for ahead in range(1, narrow):
        pl.semaphore_signal(barrier, inc=1, device_id={"narrow": partner(ahead)}, device_id_type=MESH)
    for ahead in range(1, wide):
        pl.semaphore_signal(
            barrier, inc=1, device_id={"wide": lax.rem(me_wide + ahead, wide)}, device_id_type=MESH
        )

    for copy in small:
        copy.wait()

    lane = iota((lat, lat), 1)
    below = iota((lat, lat), 0)
    below = jnp.where(below < lat // 2, below, 3 * lat // 2 - 1 - below)
    owners = jnp.broadcast_to(owner_ref[...], (lat, lat)).astype(jnp.float32)
    owner = jnp.sum(jnp.where(lane == below, owners, 0.0), axis=1, keepdims=True)
    ahead_of = (owners < owner) | ((owners == owner) & (lane < below))
    rank = jnp.sum(jnp.where(ahead_of, 1.0, 0.0), axis=1, keepdims=True).astype(jnp.int32)
    column = iota((lat, narrow * 128), 1)
    goal = (column // 128) * lat_here + column % lat_here
    for n in range(2 * members):
        wanted = (goal == rank) & ((column // lat_here) % (2 * members) == n)
        place[n * lat:(n + 1) * lat, :] = jnp.where(wanted, 1.0, 0.0).astype(jnp.bfloat16)

    position = iota((1, M), 1)
    sign = (1 - 2 * (position & 1)).astype(jnp.float32).astype(jnp.bfloat16)
    half_lane = iota((rows, 128), 1)
    block = M // 8

    def one_pair(c, slot, h, u):
        at = h * (HALF // 2) + u
        parts = []
        extras = []
        for half in range(2):
            inside = 2 * at + half
            lines = 2 * u + half
            first_len = M - pair_ref[me * slot_count + c * CHUNK + inside]
            leading = (position < first_len).astype(jnp.float32).astype(jnp.bfloat16)
            flip = (1 - 2 * (first_len & 1)).astype(jnp.float32)
            for e in range(members):
                for t in range(steps_here):
                    row = 2 * (e * steps_here + t)
                    lined[lines, row:row + 2, :] = x_buf[slot, e, t, inside]
            body = lined[lines, :, :M]
            first_part = body * leading
            parts.extend((first_part, first_part * sign, body, body * sign))
            last = lined[lines, :, M:].astype(jnp.float32)
            extras.append((last, flip))
        table = spread[h, pl.ds(u, M, stride=4), :].astype(jnp.bfloat16)
        out = dot(jnp.concatenate(parts, axis=0), table)
        edge = last_row[pl.ds(at, 1), :]
        for half in range(2):
            base = half * 4 * rows
            piece = [out[base + v * rows:base + (v + 1) * rows] for v in range(4)]
            last, flip = extras[half]
            term = last * edge
            piece[2] = piece[2] - piece[0] + term
            piece[3] = (piece[3] - piece[1] + term) * flip
            for tail_at in range(2):
                north, south = piece[2 * tail_at], piece[2 * tail_at + 1]
                if half == 0:
                    both = jnp.where(half_lane < 64, north, pltpu.roll(south, 64, 1))
                else:
                    both = jnp.where(half_lane < 64, pltpu.roll(north, 64, 1), south)
                at_row = (tail_at * HALF + 2 * u + half) * rows
                sums[at_row:at_row + rows, :] = both

    def one_half(c, slot, h):
        for u in range(HALF // 2):
            one_pair(c, slot, h, u)
        highs, lows = [], []
        for t in range(steps_here):
            wide_rows = jnp.concatenate(
                [
                    sums[pl.ds((e * steps_here + t) * 2 + part, CHUNK, stride=rows), :]
                    for part in range(2) for e in range(members)
                ],
                axis=1,
            )
            high, low = split(wide_rows)
            highs.append(high)
            lows.append(low)
        both = dot(jnp.concatenate(highs + lows, axis=0), place[...])
        moved = both[:steps_here * CHUNK] + both[steps_here * CHUNK:]
        where_to = pl.ds(pl.multiple_of((2 * c + h) * CHUNK, CHUNK), CHUNK)
        for t in range(steps_here):
            for d in range(narrow):
                sent[d, where_to, t * 128:(t + 1) * 128] = (
                    moved[t * CHUNK:(t + 1) * CHUNK, d * 128:(d + 1) * 128]
                )
        held[me, where_to, :] = sent[me, where_to, :]

        @pl.when((c == 0) & (h == 0))
        def _():
            pl.semaphore_wait(barrier, narrow - 1 + wide - 1)

        def sends(group, targets):
            for target in targets:
                @pl.when(me != target)
                def _():
                    for first, kind in group:
                        send(first, target, kind).start()

        for piece in PIECES:
            first, kind = piece
            after = first + (kind == 3)
            done = (c == first) & (h == 0) if kind == 0 else (c == after) & (h == 1)

            @pl.when(done)
            def _():
                if first >= chunks - 2:
                    sends([piece], range(0, narrow, 2))
                else:
                    for ahead in order:
                        send(first, partner(ahead), kind).start()

        @pl.when((c == chunks - 1) & (h == 1))
        def _():
            sends([piece for piece in PIECES if piece[0] >= chunks - 2], range(1, narrow, 2))

    def tables(c):
        lanes = iota((8, 128), 1)
        base = lanes & ~HALF
        lead = jnp.zeros((8, 128), jnp.int32)
        for h in range(2):
            for d in range(narrow):
                for s in range(HALF):
                    at = (h * narrow + d) * CHUNK + s
                    lead = jnp.where(base == at, pair_ref[d * slot_count + c * CHUNK + h * HALF + s], lead)
        wave = jnp.where((lanes & HALF) == HALF, M - 1 - lead, lead).astype(jnp.float32)
        here = pl.ds(pl.multiple_of(c * 128, 128), 128)
        rows_of = jnp.broadcast_to(wave[:1], (FINE, 128))
        index = iota((FINE, 128), 0).astype(jnp.float32)
        cosine, sine = turn(rows_of * (index * (2.0 * FINE)))
        coarse[0, :, here] = cosine
        coarse[1, :, here] = sine
        cosine, sine = turn(rows_of * (index * 2.0 + 1.0))
        fine[0, :, here] = cosine
        fine[1, :, here] = sine
        down = jnp.transpose(jnp.broadcast_to(wave[:1], (128, 128)))
        cosine, sine = turn(down * (lon - 1.0))
        low = iota((128, 128), 1) < 64
        cosine = cosine * (M ** -0.5)
        sine = sine * (M ** -0.5)
        rate = down * (1.0 / M)
        coef[0, here, :] = cosine * jnp.where(low, 1.0, -rate)
        coef[1, here, :] = sine * jnp.where(low, -1.0, -rate)
        coef[2, here, :] = sine * jnp.where(low, 1.0, -rate)
        coef[3, here, :] = cosine * jnp.where(low, 1.0, rate)

    def one_chunk(c, carry):
        slot = lax.rem(c, 2)
        x_copy, *table_copies = reversed(fetches(c, slot))
        x_copy.wait()
        table_copies = table_copies[::-1]

        @pl.when(c > 0)
        def _():
            for copy in table_copies:
                copy.wait()

            @pl.when(c + 1 < chunks)
            def _():
                start_fetch(c + 1, 1 - slot)

        def widen(groups, arriving=()):
            def some(n, carry):
                for v in range(block // WIDEN):
                    at = n * block + v * WIDEN
                    part = table_buf[slot, pl.ds(at, WIDEN)].astype(jnp.float32).reshape(WIDEN // 2, 2, pairs, 128)
                    first, second = part[:, 0], part[:, 1]
                    upper = iota(first.shape, 1) < 4
                    where_to = pl.ds(pl.multiple_of(at * 4, 8), WIDEN * 4)
                    if 0 in groups:
                        merged = jnp.where(upper, first, pltpu.roll(second, 4, 1))
                        spread[0, where_to, :] = merged.reshape(WIDEN * 4, 128)
                    if 1 in groups:
                        merged = jnp.where(upper, pltpu.roll(first, 4, 1), second)
                        spread[1, where_to, :] = merged.reshape(WIDEN * 4, 128)
                return carry

            if not arriving:
                lax.fori_loop(0, 8, some, 0)
            each = 8 // max(len(arriving), 1)
            for n, copy in enumerate(arriving):
                copy.wait()
                lax.fori_loop(n * each, (n + 1) * each, some, 0)

        @pl.when(c > 0)
        def _():
            widen((0, 1))

        def halves(h, carry):
            @pl.when((c == 0) & (h == 0))
            def _():
                widen((0,), table_copies)
                start_fetch(1, 1)

            @pl.when(h == 0)
            def _():
                last_row[...] = table_buf[slot, M].astype(jnp.float32)

            @pl.when((c == 0) & (h == 1))
            def _():
                widen((1,))

            one_half(c, slot, h)
            return carry

        lax.fori_loop(0, 2, halves, 0)
        tables(c)
        return carry

    lax.fori_loop(0, chunks, one_chunk, 0)

    def turned(pieces, here):
        evens, odds = [], []
        c1, s1, c2, s2 = (coef[n, here, :] for n in range(4))
        for t in range(steps_here):
            data = jnp.concatenate([held[d, span, t * 128:(t + 1) * 128] for d, span in pieces], axis=0)
            other = pltpu.roll(data, 64, 1)
            evens.append(data * c1 + other * s1)
            odds.append(data * c2 + other * s2)
        return split(jnp.concatenate(evens, axis=1)), split(jnp.concatenate(odds, axis=1))

    def waves_at(g, coarse_of, fine_of):
        cosines, sines = [], []
        many = GROUP // FINE
        span = pl.ds(pl.multiple_of(g * many, many), many)
        cu, su = coarse_of(0, span), coarse_of(1, span)
        c2, s2 = fine_of
        for u in range(many):
            c1, s1 = cu[u:u + 1], su[u:u + 1]
            cosines.append(c1 * c2 - s1 * s2)
            sines.append(s1 * c2 + c1 * s2)
        return split(jnp.concatenate(cosines, axis=0)), split(jnp.concatenate(sines, axis=0))

    def span_of(c, h):
        return pl.ds(pl.multiple_of((2 * c + h) * CHUNK, CHUNK), CHUNK)

    regions = wide * REG_DEV
    blocks = half_lon // 8

    def region_tables():
        number = iota((regions, 128), 0)
        begin = jnp.zeros((regions, 128), jnp.int32)
        end = begin
        for n in range(lon // 128):
            ids = region_ref[n:n + 1, :]
            begin = begin + jnp.where(ids < number, 1, 0)
            end = end + jnp.where(ids <= number, 1, 0)
        reach = 64
        while reach:
            begin = begin + pltpu.roll(begin, reach, 1)
            end = end + pltpu.roll(end, reach, 1)
            reach //= 2
        lanes = iota((regions, 128), 1)
        for side in range(2):
            if side == 0:
                first, last = half_lon - jnp.minimum(end, half_lon), half_lon - jnp.minimum(begin, half_lon)
            else:
                first, last = jnp.maximum(begin, half_lon) - half_lon, jnp.maximum(end, half_lon) - half_lon
            here = first < last
            for n in range(half_lon // 128):
                hit = (lanes + n * 128 == first) & here
                pick[side, :, n * 128:(n + 1) * 128] = jnp.where(hit, 1.0, 0.0).astype(jnp.bfloat16)
            start = (first + 7) >> 3
            whole = start * 8 < last
            pick_blocks[side] = jnp.where((lanes == start) & whole, 1.0, 0.0).astype(jnp.bfloat16)
            absent[2 * side] = jnp.where(here, 0.0, -1e30)
            absent[2 * side + 1] = jnp.where(whole, 0.0, -1e30)
        across, down = iota((128, 128), 1), iota((128, 128), 0)
        mirror = jnp.where(across + down == 127, 1.0, 0.0).astype(jnp.bfloat16)
        ids = region_ref[...].astype(jnp.float32)
        flipped = dot(ids.astype(jnp.bfloat16), mirror)
        tiles = half_lon // 128
        sub = iota((16, 8, 128), 1)
        for side in range(2):
            for n in range(tiles):
                source = flipped[tiles - 1 - n:tiles - n] if side == 0 else ids[tiles + n:tiles + n + 1]
                column = jnp.transpose(jnp.broadcast_to(source, (128, 128)))
                span = pl.ds(side * half_lon + n * 128, 128)
                field[span, :] = column
                column = column.reshape(16, 8, 128)
                for i, step in enumerate((1, 2, 4)):
                    same = (pltpu.roll(column, 8 - step, 1) == column) & (sub + step < 8)
                    apart[i, span, :] = jnp.where(same, 0.0, -1e30).reshape(128, 128)
            starts = field[pl.ds(side * half_lon, blocks, stride=8), :]
            for i, step in enumerate((1, 2, 4)):
                same = (pltpu.roll(starts, blocks - step, 0) == starts) & (iota((blocks, 128), 0) + step < blocks)
                apart_blocks[side, i] = jnp.where(same, 0.0, -1e30)

    region_tables()

    def two_chunks(k, carry):
        first = 2 * k

        def arrive_when(when, piece):
            @pl.when(when)
            def _():
                arrive(*piece)

        for piece in PIECES:
            if piece[0] < chunks - 2:
                arrive_when(k == piece[0] // 2, piece)

        here = pl.ds(pl.multiple_of(first * 128, 256), 256)
        pieces = [(d, span_of(first + n, h)) for n in range(2) for h in range(2) for d in range(narrow)]
        (even_hi, even_lo), (odd_hi, odd_lo) = turned(pieces, here)
        fine_of = fine[0, :, here], fine[1, :, here]

        def one_group(g, carry):
            (cos_hi, cos_lo), (sin_hi, sin_lo) = waves_at(g, lambda n, span: coarse[n, span, here], fine_of)
            where_to = pl.ds(pl.multiple_of(g * GROUP, GROUP), GROUP)
            new_cos = dot(cos_hi, even_hi) + dot(cos_lo, even_hi) + dot(cos_hi, even_lo)
            new_sin = dot(sin_hi, odd_hi) + dot(sin_lo, odd_hi) + dot(sin_hi, odd_lo)

            @pl.when(k == 0)
            def _():
                part_cos[where_to, :] = new_cos
                part_sin[where_to, :] = new_sin

            @pl.when(k > 0)
            def _():
                part_cos[where_to, :] += new_cos
                part_sin[where_to, :] += new_sin

            return carry

        lax.fori_loop(0, half_lon // GROUP, one_group, 0)
        return carry

    lax.fori_loop(0, chunks // 2 - 1, two_chunks, 0)

    def angles_ahead(c, h):
        chunk_here = pl.ds(c * 128, 128)

        def doubled(values):
            kept = iota(values.shape, 1) < 64
            moved = pltpu.roll(values, 64, 1)
            return jnp.where(kept, values, moved) if h == 0 else jnp.where(kept, moved, values)

        fine_of = tuple(doubled(fine[n, :, chunk_here]) for n in range(2))
        low = iota((GROUP, 128), 1) < 64

        def one_group(g, carry):
            both = waves_at(g, lambda n, span: doubled(coarse[n, span, chunk_here]), fine_of)
            where_to = pl.ds(pl.multiple_of(g * GROUP, GROUP), GROUP)
            for n, (high, part) in enumerate(both):
                ready[c % 2, h, n, where_to, :128] = jnp.where(low, high, part)
                ready[c % 2, h, n, where_to, 128:] = high
            return carry

        lax.fori_loop(0, half_lon // GROUP, one_group, 0)

    def half_chunk(c, h, last):
        here = pl.ds((c * 2 + h) * 64, 64)
        (even_hi, even_lo), (odd_hi, odd_lo) = turned([(d, span_of(c, h)) for d in range(narrow)], here)
        even = jnp.concatenate([even_hi, even_hi, even_lo, jnp.zeros_like(even_lo)], axis=0)
        odd = jnp.concatenate([odd_hi, odd_hi, odd_lo, jnp.zeros_like(odd_lo)], axis=0)
        sign = jnp.where(iota((LAST, 128), 1) < 64, 1.0, -1.0)

        def one_group(g, carry):
            where_to = pl.ds(pl.multiple_of(g * LAST, LAST), LAST)
            new_cos = dot(ready[c % 2, h, 0, where_to, :], even)
            new_sin = dot(ready[c % 2, h, 1, where_to, :], odd)
            if not last:
                part_cos[where_to, :] += new_cos
                part_sin[where_to, :] += new_sin
                return carry
            most = [None, None]
            least = [None, None]
            for t in range(steps_here):
                lanes = slice(t * 128, (t + 1) * 128)
                even_part = part_cos[where_to, lanes] + new_cos[:, lanes]
                odd_part = part_sin[where_to, lanes] + new_sin[:, lanes]
                for side, full in enumerate((even_part + odd_part, even_part - odd_part)):
                    most[side] = full if t == 0 else jnp.maximum(most[side], full)
                    least[side] = full if t == 0 else jnp.minimum(least[side], full)
            for side in range(2):
                span = pl.ds(pl.multiple_of(side * half_lon + g * LAST, LAST), LAST)
                best = jnp.maximum(most[side], least[side] * sign)
                best = best.reshape(LAST // 8, 8, 128)
                for i, step in enumerate((1, 2, 4)):
                    best = jnp.maximum(
                        best, pltpu.roll(best, 8 - step, 1) + apart[i, span, :].reshape(LAST // 8, 8, 128)
                    )
                field[span, :] = best.reshape(LAST, 128)
            return carry

        lax.fori_loop(0, half_lon // LAST, one_group, 0)

    angles_ahead(chunks - 2, 0)
    angles_ahead(chunks - 2, 1)
    angles_ahead(chunks - 1, 0)
    angles_ahead(chunks - 1, 1)
    for piece in PIECES:
        if piece[0] == chunks - 2:
            arrive(*piece)
    half_chunk(chunks - 2, 0, False)
    half_chunk(chunks - 2, 1, False)
    arrive(chunks - 1, 0)
    half_chunk(chunks - 1, 0, False)
    arrive(chunks - 1, 1)
    half_chunk(chunks - 1, 1, True)

    def chosen(picks, values, missing):
        high, low = split(values)
        both = dot(picks, jnp.concatenate([high, low], axis=1))
        return both[:, :128] + both[:, 128:] + missing

    parts = []
    for side in range(2):
        starts = field[pl.ds(side * half_lon, blocks, stride=8), :]
        for i, step in enumerate((1, 2, 4)):
            starts = jnp.maximum(starts, pltpu.roll(starts, blocks - step, 0) + apart_blocks[side, i])
        parts.append(chosen(pick_blocks[side], starts, absent[2 * side + 1]))
        parts.append(chosen(pick[side], field[pl.ds(side * half_lon, half_lon), :], absent[2 * side]))
    peaks[...] = jnp.maximum(jnp.maximum(parts[0], parts[1]), jnp.maximum(parts[2], parts[3]))

    def exchange(ahead, arriving):
        other = lax.rem(me_wide + ahead, wide)
        return pltpu.make_async_remote_copy(
            src_ref=peaks.at[pl.ds(pl.multiple_of(other * REG_DEV, REG_DEV), REG_DEV)],
            dst_ref=peaks_in.at[other if arriving else me_wide],
            send_sem=wide_send.at[other], recv_sem=wide_recv.at[other if arriving else me_wide],
            device_id={"wide": other}, device_id_type=MESH,
        )

    for ahead in range(wide - 1, 0, -1):
        exchange(ahead, False).start()
    for ahead in range(1, narrow):
        for first, kind in PIECES:
            send(first, partner(ahead), kind).wait_send()
    best = peaks[pl.ds(pl.multiple_of(me_wide * REG_DEV, REG_DEV), REG_DEV), :]
    for ahead in range(1, wide):
        exchange(ahead, True).wait_recv()
        best = jnp.maximum(best, peaks_in[lax.rem(me_wide + ahead, wide)])
    for n in range(2 * members):
        out_ref[n] = best[:, n * lat_here:(n + 1) * lat_here]

    for ahead in range(1, wide):
        exchange(ahead, False).wait_send()


def per_device(spectra, legendre, pair_of_slot, lat_owner, region_of_lon):
    members, steps_here, slot_count, _, length = spectra.shape
    lat = legendre.shape[2]
    narrow, wide = lax.axis_size("narrow"), lax.axis_size("wide")
    lat_here = lat // narrow
    lon = region_of_lon.shape[0]
    rows = members * steps_here * 2
    chunks = slot_count // CHUNK
    regions = REG_DEV * wide
    lanes = steps_here * 128
    dims = (narrow, wide, chunks, rows, members, steps_here, lat_here, lon)
    vmem = pl.BlockSpec(memory_space=pltpu.VMEM)
    hbm = pl.BlockSpec(memory_space=pl.ANY)
    best = pl.pallas_call(
        functools.partial(fields_kernel, dims),
        in_specs=[hbm] * 5,
        out_specs=vmem,
        out_shape=jax.ShapeDtypeStruct((2 * members, REG_DEV, lat_here), jnp.float32),
        scratch_shapes=[
            pltpu.SMEM((slot_count * narrow,), jnp.int32),
            pltpu.VMEM((1, lat), jnp.int32),
            pltpu.VMEM((lon // 128, 128), jnp.int32),
            pltpu.VMEM((2, length, CHUNK // 2, lat), jnp.bfloat16),
            pltpu.VMEM((2, members, steps_here, CHUNK, 2, length), jnp.bfloat16),
            pltpu.VMEM((HALF, rows, length), jnp.bfloat16),
            pltpu.VMEM((2, M * 4, 128), jnp.float32),
            pltpu.VMEM((CHUNK // 2, 128), jnp.float32),
            pltpu.VMEM((CHUNK * rows, 128), jnp.float32),
            pltpu.VMEM((2 * members * lat, narrow * 128), jnp.bfloat16),
            pltpu.VMEM((narrow, chunks * 2 * CHUNK, lanes), jnp.float32),
            pltpu.VMEM((narrow, chunks * 2 * CHUNK, lanes), jnp.float32),
            pltpu.VMEM((2, 2, 2, lon // 2, 256), jnp.bfloat16),
            pltpu.VMEM((4, chunks * 128, 128), jnp.float32),
            pltpu.VMEM((2, FINE, chunks * 128), jnp.float32),
            pltpu.VMEM((2, FINE, chunks * 128), jnp.float32),
            pltpu.VMEM((lon // 2, lanes), jnp.float32),
            pltpu.VMEM((lon // 2, lanes), jnp.float32),
            pltpu.VMEM((lon, 128), jnp.float32),
            pltpu.VMEM((3, lon, 128), jnp.float32),
            pltpu.VMEM((2, 3, lon // 16, 128), jnp.float32),
            pltpu.VMEM((2, regions, lon // 2), jnp.bfloat16),
            pltpu.VMEM((2, regions, lon // 16), jnp.bfloat16),
            pltpu.VMEM((4, regions, 128), jnp.float32),
            pltpu.VMEM((regions, 128), jnp.float32),
            pltpu.VMEM((wide, REG_DEV, 128), jnp.float32),
            pltpu.SemaphoreType.DMA((1 + FETCHES, 2)),
            pltpu.SemaphoreType.DMA((3,)),
            pltpu.SemaphoreType.DMA((2, chunks, narrow)),
            pltpu.SemaphoreType.DMA((2, chunks, narrow)),
            pltpu.SemaphoreType.DMA((wide,)),
            pltpu.SemaphoreType.DMA((wide,)),
        ],
        compiler_params=pltpu.CompilerParams(
            collective_id=0, has_side_effects=True, vmem_limit_bytes=60 * 1024 * 1024
        ),
    )(
        pair_of_slot, lat_owner.reshape(1, lat), region_of_lon.reshape(-1, 128), spectra,
        jnp.transpose(legendre, (1, 0, 2)),
    )
    best = jnp.transpose(best, (0, 2, 1))
    return (best[:members], best[members:])


def solution(mesh):
    in_specs = (
        P(None, ("groups", "wide"), "narrow", None, None),
        P("narrow", None, None),
        P(),
        P(),
        P(),
    )
    out_specs = (P("groups", "narrow", "wide"), P("groups", "narrow", "wide"))

    def body(spectra, legendre, *rest):
        members, steps_here, slot_count = spectra.shape[:3]
        lat_here = legendre.shape[2] // mesh.shape["narrow"]
        packs = steps_here * lat_here == 128 and 2 * members * lat_here == 128
        packs = packs and slot_count % (2 * CHUNK) == 0 and slot_count >= 4 * CHUNK
        packs = packs and legendre.shape[2] == 128 and mesh.shape["narrow"] * CHUNK == 64
        packs = packs and rest[2].shape[0] == 2 * FINE * FINE
        chosen = per_device if packs else per_device_plain
        return chosen(spectra, legendre, *rest)

    return jax.shard_map(
        body, mesh=mesh, in_specs=in_specs, out_specs=out_specs, check_vma=False
    )
```

```python
import functools
import math

import jax
import jax.numpy as jnp
from jax import lax
from jax.experimental import pallas as pl
from jax.experimental.pallas import tpu as pltpu
from jax.sharding import PartitionSpec as P

M = 1280
LON = 2048
REG_DEV = 16
LON_FULL = 5120


def synthesize(operand, waves, start, width):
    columns = start + jnp.arange(width, dtype=jnp.int32)
    phase = waves[:, None] * columns[None, :] % LON_FULL
    angle = phase.astype(jnp.float32) * (2.0 * math.pi / LON_FULL)
    cosine = jnp.cos(angle)
    sine = jnp.sin(angle)
    rate = (waves.astype(jnp.float32) / M)[:, None]
    upper = jnp.concatenate([cosine, -rate * sine], axis=1)
    lower = jnp.concatenate([-sine, -rate * cosine], axis=1)
    table = jnp.concatenate([upper, lower], axis=0) * M ** (-0.5)
    return jnp.dot(operand, table, precision=lax.Precision.HIGHEST)


def synthesize_all(operand, waves):
    width = min(512, LON)
    starts = jnp.arange(LON // width, dtype=jnp.int32) * width

    def one_block(begin):
        return synthesize(operand, waves, begin, width)

    blocks = lax.map(one_block, starts)
    blocks = blocks.reshape(blocks.shape[0], blocks.shape[1], 2, width)
    value = jnp.transpose(blocks[:, :, 0], (1, 0, 2)).reshape(operand.shape[0], LON)
    slope = jnp.transpose(blocks[:, :, 1], (1, 0, 2)).reshape(operand.shape[0], LON)
    return (value, slope)


def region_peak(values, region_of_lon, wanted):
    hits = region_of_lon[:, None] == wanted[None, :]
    masked = jnp.where(hits[None, None], values[..., None], -1e30)
    return masked.max(axis=2)


def per_device_plain(spectra, legendre, pair_of_slot, lat_owner, region_of_lon):
    members = spectra.shape[0]
    steps_here = spectra.shape[1]
    slot_count = spectra.shape[2]
    length = spectra.shape[4]
    half_count = legendre.shape[0]
    lat_half = legendre.shape[2] // 2
    here = lax.axis_index("narrow")
    paired = lax.dynamic_slice_in_dim(pair_of_slot, here * slot_count, slot_count)
    position = jnp.arange(length, dtype=jnp.int32)[None, :]
    first_len = (M - paired)[:, None]
    leading = position < first_len
    offset = jnp.where(leading, position, position - first_len)
    even_term = offset % 2 == 0
    masks = jnp.stack(
        [leading & even_term, leading & ~even_term, ~leading & even_term, ~leading & ~even_term],
        axis=1,
    ).astype(jnp.bfloat16)
    ordered = jnp.transpose(spectra, (2, 0, 1, 3, 4))
    masked = masks[:, :, None, None, None, :] * ordered[:, None]
    masked = masked.reshape(half_count, 2, -1, length)
    table = legendre.reshape(half_count, length, 2, lat_half)
    sums = jnp.einsum("abrl,albj->abrj", masked, table, preferred_element_type=jnp.float32)
    sums = sums.reshape(slot_count, 4, members, steps_here, 2, lat_half)
    north_lead = sums[:, 0] + sums[:, 1]
    south_lead = sums[:, 0] - sums[:, 1]
    north_tail = sums[:, 2] + sums[:, 3]
    south_tail = sums[:, 2] - sums[:, 3]
    lead = jnp.concatenate([north_lead, jnp.flip(south_lead, axis=-1)], axis=-1)
    tail = jnp.concatenate([north_tail, jnp.flip(south_tail, axis=-1)], axis=-1)
    waved = jnp.stack([lead, tail], axis=1).reshape(2 * slot_count, members, steps_here, 2, -1)
    order = jnp.argsort(lat_owner, stable=True)
    waved = jnp.take(waved, order, axis=4)
    arrived = lax.all_to_all(waved, "narrow", split_axis=4, concat_axis=0, tiled=True)
    waves = jnp.stack([pair_of_slot, M - 1 - pair_of_slot], axis=1).reshape(-1)
    lat_here = arrived.shape[4]
    operand = jnp.transpose(arrived, (1, 2, 4, 3, 0)).reshape(members * steps_here * lat_here, -1)
    value, slope = synthesize_all(operand, waves)
    value = value.reshape(members, steps_here, lat_here, LON).max(axis=1)
    slope = jnp.abs(slope).reshape(members, steps_here, lat_here, LON).max(axis=1)
    wide_count = lax.axis_size("wide")
    mine_start = lax.axis_index("wide") * REG_DEV
    wanted = jnp.arange(REG_DEV * wide_count, dtype=jnp.int32)
    peaks = region_peak(value, region_of_lon, wanted)
    slopes = region_peak(slope, region_of_lon, wanted)
    peaks, slopes = lax.pmax((peaks, slopes), "wide")
    peak = lax.dynamic_slice_in_dim(peaks, mine_start, REG_DEV, 2)
    peak_slope = lax.dynamic_slice_in_dim(slopes, mine_start, REG_DEV, 2)
    return (peak, peak_slope)


CHUNK = 16
HALF = 8
FINE = 32
GROUP = 1024
FETCHES = 4
LAST = 1024
WIDEN = 32
MESH = pl.DeviceIdType.MESH


def split(values):
    high = values.astype(jnp.bfloat16)
    low = (values - high.astype(jnp.float32)).astype(jnp.bfloat16)
    return high, low


def dot(left, right):
    return jnp.dot(left, right, preferred_element_type=jnp.float32)


def turn(count):
    quarter = LON_FULL // 2
    whole = jnp.floor(count * (1.0 / quarter) + 0.5)
    angle = (count - whole * quarter) * (math.pi / LON_FULL)
    square = angle * angle
    sine = angle * (1.0 + square * (-1 / 6 + square * (1 / 120 + square * (-1 / 5040 + square * (1 / 362880)))))
    cosine = 1.0 + square * (
        -1 / 2 + square * (1 / 24 + square * (-1 / 720 + square * (1 / 40320 + square * (-1 / 3628800))))
    )
    turns = whole.astype(jnp.int32)
    swap = (turns & 1) == 1
    cos_sign = jnp.where(((turns + 1) & 2) == 2, -1.0, 1.0)
    sin_sign = jnp.where((turns & 2) == 2, -1.0, 1.0)
    return cos_sign * jnp.where(swap, sine, cosine), sin_sign * jnp.where(swap, cosine, sine)


def iota(shape, dim):
    return lax.broadcasted_iota(jnp.int32, shape, dim)


def pieces_of(chunks):
    pieces = [(0, 0), (0, 1), (1, 2)]
    pieces += [(c, 3) for c in range(2, chunks - 2, 2)]
    return pieces + [(chunks - 2, 2), (chunks - 1, 2)]


def fields_kernel(
    dims, pair_hbm, owner_hbm, region_hbm, x_hbm, table_hbm, out_ref,
    pair_ref, owner_ref, region_ref,
    table_buf, x_buf, lined, spread, last_row, sums, place, sent, held, ready, coef, coarse, fine, part_cos, part_sin, field,
    apart, apart_blocks, pick, pick_blocks, absent, peaks, peaks_in,
    fetch_sem, small_sem, send_sem, recv_sem, wide_send, wide_recv,
):
    narrow, wide, chunks, rows, members, steps_here, lat_here, lon = dims
    me = lax.axis_index("narrow")
    me_wide = lax.axis_index("wide")
    slot_count = chunks * CHUNK
    pairs = CHUNK // 2
    half_lon = lon // 2
    lat = narrow * lat_here

    part = M // FETCHES
    parts_of = [pl.ds(n * part, part + (n == FETCHES - 1)) for n in range(FETCHES)]

    def fetches(c, slot):
        return (
            *(
                pltpu.make_async_copy(
                    table_hbm.at[span, pl.ds(pl.multiple_of(c * pairs, pairs), pairs), :], table_buf.at[slot, span],
                    fetch_sem.at[1 + n, slot],
                )
                for n, span in enumerate(parts_of)
            ),
            pltpu.make_async_copy(
                x_hbm.at[:, :, pl.ds(c * CHUNK, CHUNK), :, :], x_buf.at[slot], fetch_sem.at[0, slot]
            ),
        )

    PIECES = pieces_of(chunks)

    def start_fetch(c, slot):
        for copy in fetches(c, slot):
            copy.start()

    def partner(ahead):
        return lax.rem(me + ahead, narrow)

    order = (2, 1, 3) if narrow == 4 else tuple(range(1, narrow))

    def rows_of(c, kind):
        if kind < 2:
            return pl.ds(pl.multiple_of(c * 2 * CHUNK + kind * CHUNK, CHUNK), CHUNK), kind
        return pl.ds(pl.multiple_of(c * 2 * CHUNK, 2 * CHUNK), (kind - 1) * 2 * CHUNK), 0

    def send(c, target, kind):
        span, at = rows_of(c, kind)
        return pltpu.make_async_remote_copy(
            src_ref=sent.at[target, span], dst_ref=held.at[me, span],
            send_sem=send_sem.at[at, c, target], recv_sem=recv_sem.at[at, c, me],
            device_id={"narrow": target}, device_id_type=MESH,
        )

    def arrive(c, kind):
        for ahead in range(1, narrow):
            origin = partner(ahead)
            span, at = rows_of(c, kind)
            pltpu.make_async_remote_copy(
                src_ref=sent.at[origin, span], dst_ref=held.at[origin, span],
                send_sem=send_sem.at[at, c, origin], recv_sem=recv_sem.at[at, c, origin],
                device_id={"narrow": origin}, device_id_type=MESH,
            ).wait_recv()

    start_fetch(0, 0)
    small = [
        pltpu.make_async_copy(source, goal, small_sem.at[n])
        for n, (source, goal) in enumerate(
            ((owner_hbm, owner_ref), (pair_hbm, pair_ref), (region_hbm, region_ref))
        )
    ]
    for copy in small:
        copy.start()
    barrier = pltpu.get_barrier_semaphore()
    for ahead in range(1, narrow):
        pl.semaphore_signal(barrier, inc=1, device_id={"narrow": partner(ahead)}, device_id_type=MESH)
    for ahead in range(1, wide):
        pl.semaphore_signal(
            barrier, inc=1, device_id={"wide": lax.rem(me_wide + ahead, wide)}, device_id_type=MESH
        )

    for copy in small:
        copy.wait()

    lane = iota((lat, lat), 1)
    below = iota((lat, lat), 0)
    below = jnp.where(below < lat // 2, below, 3 * lat // 2 - 1 - below)
    owners = jnp.broadcast_to(owner_ref[...], (lat, lat)).astype(jnp.float32)
    owner = jnp.sum(jnp.where(lane == below, owners, 0.0), axis=1, keepdims=True)
    ahead_of = (owners < owner) | ((owners == owner) & (lane < below))
    rank = jnp.sum(jnp.where(ahead_of, 1.0, 0.0), axis=1, keepdims=True).astype(jnp.int32)
    column = iota((lat, narrow * 128), 1)
    goal = (column // 128) * lat_here + column % lat_here
    for n in range(2 * members):
        wanted = (goal == rank) & ((column // lat_here) % (2 * members) == n)
        place[n * lat:(n + 1) * lat, :] = jnp.where(wanted, 1.0, 0.0).astype(jnp.bfloat16)

    position = iota((1, M), 1)
    sign = (1 - 2 * (position & 1)).astype(jnp.float32).astype(jnp.bfloat16)
    half_lane = iota((rows, 128), 1)
    block = M // 8

    def one_pair(c, slot, h, u):
        at = h * (HALF // 2) + u
        parts = []
        extras = []
        for half in range(2):
            inside = 2 * at + half
            lines = 2 * u + half
            first_len = M - pair_ref[me * slot_count + c * CHUNK + inside]
            leading = (position < first_len).astype(jnp.float32).astype(jnp.bfloat16)
            flip = (1 - 2 * (first_len & 1)).astype(jnp.float32)
            for e in range(members):
                for t in range(steps_here):
                    row = 2 * (e * steps_here + t)
                    lined[lines, row:row + 2, :] = x_buf[slot, e, t, inside]
            body = lined[lines, :, :M]
            first_part = body * leading
            parts.extend((first_part, first_part * sign, body, body * sign))
            last = lined[lines, :, M:].astype(jnp.float32)
            extras.append((last, flip))
        table = spread[h, pl.ds(u, M, stride=4), :].astype(jnp.bfloat16)
        out = dot(jnp.concatenate(parts, axis=0), table)
        edge = last_row[pl.ds(at, 1), :]
        for half in range(2):
            base = half * 4 * rows
            piece = [out[base + v * rows:base + (v + 1) * rows] for v in range(4)]
            last, flip = extras[half]
            term = last * edge
            piece[2] = piece[2] - piece[0] + term
            piece[3] = (piece[3] - piece[1] + term) * flip
            for tail_at in range(2):
                north, south = piece[2 * tail_at], piece[2 * tail_at + 1]
                if half == 0:
                    both = jnp.where(half_lane < 64, north, pltpu.roll(south, 64, 1))
                else:
                    both = jnp.where(half_lane < 64, pltpu.roll(north, 64, 1), south)
                at_row = (tail_at * HALF + 2 * u + half) * rows
                sums[at_row:at_row + rows, :] = both

    def one_half(c, slot, h):
        for u in range(HALF // 2):
            one_pair(c, slot, h, u)
        highs, lows = [], []
        for t in range(steps_here):
            wide_rows = jnp.concatenate(
                [
                    sums[pl.ds((e * steps_here + t) * 2 + part, CHUNK, stride=rows), :]
                    for part in range(2) for e in range(members)
                ],
                axis=1,
            )
            high, low = split(wide_rows)
            highs.append(high)
            lows.append(low)
        both = dot(jnp.concatenate(highs + lows, axis=0), place[...])
        moved = both[:steps_here * CHUNK] + both[steps_here * CHUNK:]
        where_to = pl.ds(pl.multiple_of((2 * c + h) * CHUNK, CHUNK), CHUNK)
        for t in range(steps_here):
            for d in range(narrow):
                sent[d, where_to, t * 128:(t + 1) * 128] = (
                    moved[t * CHUNK:(t + 1) * CHUNK, d * 128:(d + 1) * 128]
                )
        held[me, where_to, :] = sent[me, where_to, :]

        @pl.when((c == 0) & (h == 0))
        def _():
            pl.semaphore_wait(barrier, narrow - 1 + wide - 1)

        def sends(group, targets):
            for target in targets:
                @pl.when(me != target)
                def _():
                    for first, kind in group:
                        send(first, target, kind).start()

        for piece in PIECES:
            first, kind = piece
            after = first + (kind == 3)
            done = (c == first) & (h == 0) if kind == 0 else (c == after) & (h == 1)

            @pl.when(done)
            def _():
                if first >= chunks - 2:
                    sends([piece], range(0, narrow, 2))
                else:
                    for ahead in order:
                        send(first, partner(ahead), kind).start()

        @pl.when((c == chunks - 1) & (h == 1))
        def _():
            sends([piece for piece in PIECES if piece[0] >= chunks - 2], range(1, narrow, 2))

    def tables(c):
        lanes = iota((8, 128), 1)
        base = lanes & ~HALF
        lead = jnp.zeros((8, 128), jnp.int32)
        for h in range(2):
            for d in range(narrow):
                for s in range(HALF):
                    at = (h * narrow + d) * CHUNK + s
                    lead = jnp.where(base == at, pair_ref[d * slot_count + c * CHUNK + h * HALF + s], lead)
        wave = jnp.where((lanes & HALF) == HALF, M - 1 - lead, lead).astype(jnp.float32)
        here = pl.ds(pl.multiple_of(c * 128, 128), 128)
        rows_of = jnp.broadcast_to(wave[:1], (FINE, 128))
        index = iota((FINE, 128), 0).astype(jnp.float32)
        cosine, sine = turn(rows_of * (index * (2.0 * FINE)))
        coarse[0, :, here] = cosine
        coarse[1, :, here] = sine
        cosine, sine = turn(rows_of * (index * 2.0 + 1.0))
        fine[0, :, here] = cosine
        fine[1, :, here] = sine
        down = jnp.transpose(jnp.broadcast_to(wave[:1], (128, 128)))
        cosine, sine = turn(down * (lon - 1.0))
        low = iota((128, 128), 1) < 64
        cosine = cosine * (M ** -0.5)
        sine = sine * (M ** -0.5)
        rate = down * (1.0 / M)
        coef[0, here, :] = cosine * jnp.where(low, 1.0, -rate)
        coef[1, here, :] = sine * jnp.where(low, -1.0, -rate)
        coef[2, here, :] = sine * jnp.where(low, 1.0, -rate)
        coef[3, here, :] = cosine * jnp.where(low, 1.0, rate)

    def one_chunk(c, carry):
        slot = lax.rem(c, 2)
        x_copy, *table_copies = reversed(fetches(c, slot))
        x_copy.wait()
        table_copies = table_copies[::-1]

        @pl.when(c > 0)
        def _():
            for copy in table_copies:
                copy.wait()

            @pl.when(c + 1 < chunks)
            def _():
                start_fetch(c + 1, 1 - slot)

        def widen(groups, arriving=()):
            def some(n, carry):
                for v in range(block // WIDEN):
                    at = n * block + v * WIDEN
                    part = table_buf[slot, pl.ds(at, WIDEN)].astype(jnp.float32).reshape(WIDEN // 2, 2, pairs, 128)
                    first, second = part[:, 0], part[:, 1]
                    upper = iota(first.shape, 1) < 4
                    where_to = pl.ds(pl.multiple_of(at * 4, 8), WIDEN * 4)
                    if 0 in groups:
                        merged = jnp.where(upper, first, pltpu.roll(second, 4, 1))
                        spread[0, where_to, :] = merged.reshape(WIDEN * 4, 128)
                    if 1 in groups:
                        merged = jnp.where(upper, pltpu.roll(first, 4, 1), second)
                        spread[1, where_to, :] = merged.reshape(WIDEN * 4, 128)
                return carry

            if not arriving:
                lax.fori_loop(0, 8, some, 0)
            each = 8 // max(len(arriving), 1)
            for n, copy in enumerate(arriving):
                copy.wait()
                lax.fori_loop(n * each, (n + 1) * each, some, 0)

        @pl.when(c > 0)
        def _():
            widen((0, 1))

        def halves(h, carry):
            @pl.when((c == 0) & (h == 0))
            def _():
                widen((0,), table_copies)
                start_fetch(1, 1)

            @pl.when(h == 0)
            def _():
                last_row[...] = table_buf[slot, M].astype(jnp.float32)

            @pl.when((c == 0) & (h == 1))
            def _():
                widen((1,))

            one_half(c, slot, h)
            return carry

        lax.fori_loop(0, 2, halves, 0)
        tables(c)
        return carry

    lax.fori_loop(0, chunks, one_chunk, 0)

    def turned(pieces, here):
        evens, odds = [], []
        c1, s1, c2, s2 = (coef[n, here, :] for n in range(4))
        for t in range(steps_here):
            data = jnp.concatenate([held[d, span, t * 128:(t + 1) * 128] for d, span in pieces], axis=0)
            other = pltpu.roll(data, 64, 1)
            evens.append(data * c1 + other * s1)
            odds.append(data * c2 + other * s2)
        return split(jnp.concatenate(evens, axis=1)), split(jnp.concatenate(odds, axis=1))

    def waves_at(g, coarse_of, fine_of):
        cosines, sines = [], []
        many = GROUP // FINE
        span = pl.ds(pl.multiple_of(g * many, many), many)
        cu, su = coarse_of(0, span), coarse_of(1, span)
        c2, s2 = fine_of
        for u in range(many):
            c1, s1 = cu[u:u + 1], su[u:u + 1]
            cosines.append(c1 * c2 - s1 * s2)
            sines.append(s1 * c2 + c1 * s2)
        return split(jnp.concatenate(cosines, axis=0)), split(jnp.concatenate(sines, axis=0))

    def span_of(c, h):
        return pl.ds(pl.multiple_of((2 * c + h) * CHUNK, CHUNK), CHUNK)

    regions = wide * REG_DEV
    blocks = half_lon // 8

    def region_tables():
        number = iota((regions, 128), 0)
        begin = jnp.zeros((regions, 128), jnp.int32)
        end = begin
        for n in range(lon // 128):
            ids = region_ref[n:n + 1, :]
            begin = begin + jnp.where(ids < number, 1, 0)
            end = end + jnp.where(ids <= number, 1, 0)
        reach = 64
        while reach:
            begin = begin + pltpu.roll(begin, reach, 1)
            end = end + pltpu.roll(end, reach, 1)
            reach //= 2
        lanes = iota((regions, 128), 1)
        for side in range(2):
            if side == 0:
                first, last = half_lon - jnp.minimum(end, half_lon), half_lon - jnp.minimum(begin, half_lon)
            else:
                first, last = jnp.maximum(begin, half_lon) - half_lon, jnp.maximum(end, half_lon) - half_lon
            here = first < last
            for n in range(half_lon // 128):
                hit = (lanes + n * 128 == first) & here
                pick[side, :, n * 128:(n + 1) * 128] = jnp.where(hit, 1.0, 0.0).astype(jnp.bfloat16)
            start = (first + 7) >> 3
            whole = start * 8 < last
            pick_blocks[side] = jnp.where((lanes == start) & whole, 1.0, 0.0).astype(jnp.bfloat16)
            absent[2 * side] = jnp.where(here, 0.0, -1e30)
            absent[2 * side + 1] = jnp.where(whole, 0.0, -1e30)
        across, down = iota((128, 128), 1), iota((128, 128), 0)
        mirror = jnp.where(across + down == 127, 1.0, 0.0).astype(jnp.bfloat16)
        ids = region_ref[...].astype(jnp.float32)
        flipped = dot(ids.astype(jnp.bfloat16), mirror)
        tiles = half_lon // 128
        sub = iota((16, 8, 128), 1)
        for side in range(2):
            for n in range(tiles):
                source = flipped[tiles - 1 - n:tiles - n] if side == 0 else ids[tiles + n:tiles + n + 1]
                column = jnp.transpose(jnp.broadcast_to(source, (128, 128)))
                span = pl.ds(side * half_lon + n * 128, 128)
                field[span, :] = column
                column = column.reshape(16, 8, 128)
                for i, step in enumerate((1, 2, 4)):
                    same = (pltpu.roll(column, 8 - step, 1) == column) & (sub + step < 8)
                    apart[i, span, :] = jnp.where(same, 0.0, -1e30).reshape(128, 128)
            starts = field[pl.ds(side * half_lon, blocks, stride=8), :]
            for i, step in enumerate((1, 2, 4)):
                same = (pltpu.roll(starts, blocks - step, 0) == starts) & (iota((blocks, 128), 0) + step < blocks)
                apart_blocks[side, i] = jnp.where(same, 0.0, -1e30)

    region_tables()

    def two_chunks(k, carry):
        first = 2 * k

        def arrive_when(when, piece):
            @pl.when(when)
            def _():
                arrive(*piece)

        for piece in PIECES:
            if piece[0] < chunks - 2:
                arrive_when(k == piece[0] // 2, piece)

        here = pl.ds(pl.multiple_of(first * 128, 256), 256)
        pieces = [(d, span_of(first + n, h)) for n in range(2) for h in range(2) for d in range(narrow)]
        (even_hi, even_lo), (odd_hi, odd_lo) = turned(pieces, here)
        fine_of = fine[0, :, here], fine[1, :, here]

        def one_group(g, carry):
            (cos_hi, cos_lo), (sin_hi, sin_lo) = waves_at(g, lambda n, span: coarse[n, span, here], fine_of)
            where_to = pl.ds(pl.multiple_of(g * GROUP, GROUP), GROUP)
            new_cos = dot(cos_hi, even_hi) + dot(cos_lo, even_hi) + dot(cos_hi, even_lo)
            new_sin = dot(sin_hi, odd_hi) + dot(sin_lo, odd_hi) + dot(sin_hi, odd_lo)

            @pl.when(k == 0)
            def _():
                part_cos[where_to, :] = new_cos
                part_sin[where_to, :] = new_sin

            @pl.when(k > 0)
            def _():
                part_cos[where_to, :] += new_cos
                part_sin[where_to, :] += new_sin

            return carry

        lax.fori_loop(0, half_lon // GROUP, one_group, 0)
        return carry

    lax.fori_loop(0, chunks // 2 - 1, two_chunks, 0)

    def angles_ahead(c, h):
        chunk_here = pl.ds(c * 128, 128)

        def doubled(values):
            kept = iota(values.shape, 1) < 64
            moved = pltpu.roll(values, 64, 1)
            return jnp.where(kept, values, moved) if h == 0 else jnp.where(kept, moved, values)

        fine_of = tuple(doubled(fine[n, :, chunk_here]) for n in range(2))
        low = iota((GROUP, 128), 1) < 64

        def one_group(g, carry):
            both = waves_at(g, lambda n, span: doubled(coarse[n, span, chunk_here]), fine_of)
            where_to = pl.ds(pl.multiple_of(g * GROUP, GROUP), GROUP)
            for n, (high, part) in enumerate(both):
                ready[c % 2, h, n, where_to, :128] = jnp.where(low, high, part)
                ready[c % 2, h, n, where_to, 128:] = high
            return carry

        lax.fori_loop(0, half_lon // GROUP, one_group, 0)

    def half_chunks(c, some, last):
        evens, odds = [], []
        for h in some:
            here = pl.ds((c * 2 + h) * 64, 64)
            (even_hi, even_lo), (odd_hi, odd_lo) = turned([(d, span_of(c, h)) for d in range(narrow)], here)
            evens.append(jnp.concatenate([even_hi, even_hi, even_lo, jnp.zeros_like(even_lo)], axis=0))
            odds.append(jnp.concatenate([odd_hi, odd_hi, odd_lo, jnp.zeros_like(odd_lo)], axis=0))
        sign = jnp.where(iota((LAST, 128), 1) < 64, 1.0, -1.0)

        def one_group(g, carry):
            where_to = pl.ds(pl.multiple_of(g * LAST, LAST), LAST)
            new_cos = sum(dot(ready[c % 2, h, 0, where_to, :], even) for h, even in zip(some, evens))
            new_sin = sum(dot(ready[c % 2, h, 1, where_to, :], odd) for h, odd in zip(some, odds))
            if not last:
                part_cos[where_to, :] += new_cos
                part_sin[where_to, :] += new_sin
                return carry
            most = [None, None]
            least = [None, None]
            for t in range(steps_here):
                lanes = slice(t * 128, (t + 1) * 128)
                even_part = part_cos[where_to, lanes] + new_cos[:, lanes]
                odd_part = part_sin[where_to, lanes] + new_sin[:, lanes]
                for side, full in enumerate((even_part + odd_part, even_part - odd_part)):
                    most[side] = full if t == 0 else jnp.maximum(most[side], full)
                    least[side] = full if t == 0 else jnp.minimum(least[side], full)
            for side in range(2):
                span = pl.ds(pl.multiple_of(side * half_lon + g * LAST, LAST), LAST)
                best = jnp.maximum(most[side], least[side] * sign)
                best = best.reshape(LAST // 8, 8, 128)
                for i, step in enumerate((1, 2, 4)):
                    best = jnp.maximum(
                        best, pltpu.roll(best, 8 - step, 1) + apart[i, span, :].reshape(LAST // 8, 8, 128)
                    )
                field[span, :] = best.reshape(LAST, 128)
            return carry

        lax.fori_loop(0, half_lon // LAST, one_group, 0)

    angles_ahead(chunks - 2, 0)
    angles_ahead(chunks - 2, 1)
    angles_ahead(chunks - 1, 0)
    angles_ahead(chunks - 1, 1)
    for piece in PIECES:
        if piece[0] == chunks - 2:
            arrive(*piece)
    half_chunks(chunks - 2, (0, 1), False)
    arrive(chunks - 1, 2)
    half_chunks(chunks - 1, (0, 1), True)

    def chosen(picks, values, missing):
        high, low = split(values)
        both = dot(picks, jnp.concatenate([high, low], axis=1))
        return both[:, :128] + both[:, 128:] + missing

    parts = []
    for side in range(2):
        starts = field[pl.ds(side * half_lon, blocks, stride=8), :]
        for i, step in enumerate((1, 2, 4)):
            starts = jnp.maximum(starts, pltpu.roll(starts, blocks - step, 0) + apart_blocks[side, i])
        parts.append(chosen(pick_blocks[side], starts, absent[2 * side + 1]))
        parts.append(chosen(pick[side], field[pl.ds(side * half_lon, half_lon), :], absent[2 * side]))
    peaks[...] = jnp.maximum(jnp.maximum(parts[0], parts[1]), jnp.maximum(parts[2], parts[3]))

    def exchange(ahead, arriving):
        other = lax.rem(me_wide + ahead, wide)
        return pltpu.make_async_remote_copy(
            src_ref=peaks.at[pl.ds(pl.multiple_of(other * REG_DEV, REG_DEV), REG_DEV)],
            dst_ref=peaks_in.at[other if arriving else me_wide],
            send_sem=wide_send.at[other], recv_sem=wide_recv.at[other if arriving else me_wide],
            device_id={"wide": other}, device_id_type=MESH,
        )

    for ahead in range(wide - 1, 0, -1):
        exchange(ahead, False).start()
    for ahead in range(1, narrow):
        for first, kind in PIECES:
            send(first, partner(ahead), kind).wait_send()
    best = peaks[pl.ds(pl.multiple_of(me_wide * REG_DEV, REG_DEV), REG_DEV), :]
    for ahead in range(1, wide):
        exchange(ahead, True).wait_recv()
        best = jnp.maximum(best, peaks_in[lax.rem(me_wide + ahead, wide)])
    for n in range(2 * members):
        out_ref[n] = best[:, n * lat_here:(n + 1) * lat_here]

    for ahead in range(1, wide):
        exchange(ahead, False).wait_send()


def per_device(spectra, legendre, pair_of_slot, lat_owner, region_of_lon):
    members, steps_here, slot_count, _, length = spectra.shape
    lat = legendre.shape[2]
    narrow, wide = lax.axis_size("narrow"), lax.axis_size("wide")
    lat_here = lat // narrow
    lon = region_of_lon.shape[0]
    rows = members * steps_here * 2
    chunks = slot_count // CHUNK
    regions = REG_DEV * wide
    lanes = steps_here * 128
    dims = (narrow, wide, chunks, rows, members, steps_here, lat_here, lon)
    vmem = pl.BlockSpec(memory_space=pltpu.VMEM)
    hbm = pl.BlockSpec(memory_space=pl.ANY)
    best = pl.pallas_call(
        functools.partial(fields_kernel, dims),
        in_specs=[hbm] * 5,
        out_specs=vmem,
        out_shape=jax.ShapeDtypeStruct((2 * members, REG_DEV, lat_here), jnp.float32),
        scratch_shapes=[
            pltpu.SMEM((slot_count * narrow,), jnp.int32),
            pltpu.VMEM((1, lat), jnp.int32),
            pltpu.VMEM((lon // 128, 128), jnp.int32),
            pltpu.VMEM((2, length, CHUNK // 2, lat), jnp.bfloat16),
            pltpu.VMEM((2, members, steps_here, CHUNK, 2, length), jnp.bfloat16),
            pltpu.VMEM((HALF, rows, length), jnp.bfloat16),
            pltpu.VMEM((2, M * 4, 128), jnp.float32),
            pltpu.VMEM((CHUNK // 2, 128), jnp.float32),
            pltpu.VMEM((CHUNK * rows, 128), jnp.float32),
            pltpu.VMEM((2 * members * lat, narrow * 128), jnp.bfloat16),
            pltpu.VMEM((narrow, chunks * 2 * CHUNK, lanes), jnp.float32),
            pltpu.VMEM((narrow, chunks * 2 * CHUNK, lanes), jnp.float32),
            pltpu.VMEM((2, 2, 2, lon // 2, 256), jnp.bfloat16),
            pltpu.VMEM((4, chunks * 128, 128), jnp.float32),
            pltpu.VMEM((2, FINE, chunks * 128), jnp.float32),
            pltpu.VMEM((2, FINE, chunks * 128), jnp.float32),
            pltpu.VMEM((lon // 2, lanes), jnp.float32),
            pltpu.VMEM((lon // 2, lanes), jnp.float32),
            pltpu.VMEM((lon, 128), jnp.float32),
            pltpu.VMEM((3, lon, 128), jnp.float32),
            pltpu.VMEM((2, 3, lon // 16, 128), jnp.float32),
            pltpu.VMEM((2, regions, lon // 2), jnp.bfloat16),
            pltpu.VMEM((2, regions, lon // 16), jnp.bfloat16),
            pltpu.VMEM((4, regions, 128), jnp.float32),
            pltpu.VMEM((regions, 128), jnp.float32),
            pltpu.VMEM((wide, REG_DEV, 128), jnp.float32),
            pltpu.SemaphoreType.DMA((1 + FETCHES, 2)),
            pltpu.SemaphoreType.DMA((3,)),
            pltpu.SemaphoreType.DMA((2, chunks, narrow)),
            pltpu.SemaphoreType.DMA((2, chunks, narrow)),
            pltpu.SemaphoreType.DMA((wide,)),
            pltpu.SemaphoreType.DMA((wide,)),
        ],
        compiler_params=pltpu.CompilerParams(
            collective_id=0, has_side_effects=True, vmem_limit_bytes=60 * 1024 * 1024
        ),
    )(
        pair_of_slot, lat_owner.reshape(1, lat), region_of_lon.reshape(-1, 128), spectra,
        jnp.transpose(legendre, (1, 0, 2)),
    )
    best = jnp.transpose(best, (0, 2, 1))
    return (best[:members], best[members:])


def solution(mesh):
    in_specs = (
        P(None, ("groups", "wide"), "narrow", None, None),
        P("narrow", None, None),
        P(),
        P(),
        P(),
    )
    out_specs = (P("groups", "narrow", "wide"), P("groups", "narrow", "wide"))

    def body(spectra, legendre, *rest):
        members, steps_here, slot_count = spectra.shape[:3]
        lat_here = legendre.shape[2] // mesh.shape["narrow"]
        packs = steps_here * lat_here == 128 and 2 * members * lat_here == 128
        packs = packs and slot_count % (2 * CHUNK) == 0 and slot_count >= 4 * CHUNK
        packs = packs and legendre.shape[2] == 128 and mesh.shape["narrow"] * CHUNK == 64
        packs = packs and rest[2].shape[0] == 2 * FINE * FINE
        chosen = per_device if packs else per_device_plain
        return chosen(spectra, legendre, *rest)

    return jax.shard_map(
        body, mesh=mesh, in_specs=in_specs, out_specs=out_specs, check_vma=False
    )
```
